32 devices in a mesh: req: 4 (over z), exp: 8 (over y, x, core).
Axes of the slice: x: 2, y: 2, z: 4, core: 2. Of those that a mesh axis runs over, the one named last changes fastest.
Arguments:
- queries: bfloat16 [64, 32, 2304], P(('req', 'exp')), may hold values from -8 to 8
- draft_keys: bfloat16 [64, 32, 2304], P(('req', 'exp')), may hold values from -9 to 9
- draft_values: bfloat16 [64, 32, 2304], P(('req', 'exp')), may hold values from -6 to 6
- tree_parents: int32 [64, 32], P(('req', 'exp')), may hold values from -1 to 30, as said below
- cache_keys: bfloat16 [64, 768, 2304], P(('req', 'exp')), may hold values from -9 to 9
- cache_values: bfloat16 [64, 768, 2304], P(('req', 'exp')), may hold values from -6 to 6
- cache_lengths: int32 [64], P(('req', 'exp')), may hold values from 1 to 768, as said below
- prompt_keys: bfloat16 [8, 512, 2304], P('req', 'exp'), may hold values from -9 to 9
- prompt_values: bfloat16 [8, 512, 2304], P('req', 'exp'), may hold values from -6 to 6
- group_ids: int32 [64], P(('req', 'exp')), may hold values from 0 to 1
- residual: bfloat16 [64, 32, 2304], P(('req', 'exp')), may hold values from -6 to 6
- norm_gain: float32 [2304], replicated, may hold values from 0.5 to 1.5
- router: bfloat16 [2304, 8], replicated, may hold values from -0.125 to 0.125
- w_gate: bfloat16 [8, 2304, 5760], P('exp', None, 'req'), may hold values from -0.125 to 0.125
- w_up: bfloat16 [8, 2304, 5760], P('exp', None, 'req'), may hold values from -0.125 to 0.125
- w_down: bfloat16 [8, 5760, 2304], P('exp', 'req'), may hold values from -0.078125 to 0.078125
- expert_ids: int32 [64, 32, 2], P(('req', 'exp')), may hold values from 0 to 7, all different within a row; in each aligned block of 64 rows (0 to 63, 64 to 127, ..., all dimensions but the last counted through in order) at most 18 rows name the same one
- accepted_rows: int32 [64, 8], P(('req', 'exp')), may hold values from 0 to 31
Outputs:
- attended: bfloat16 [64, 32, 2304], P(('req', 'exp'))
- layer_out: bfloat16 [64, 32, 2304], P(('req', 'exp'))
- accepted_cache: bfloat16 [64, 2, 8, 2304], P(('req', 'exp'))
The draws below stay inside these ranges and needn't reach their ends.
Inputs may be any that keep to these rules, and one draw needn't show every extreme that they name: `tree_parents`: position 0 of every tree holds -1; every other position holds an earlier position of the same tree. `cache_lengths`: some request has all 768 slots used. `expert_ids`: the two experts of a position differ; among the rows of one device no expert is named more than 18 times, a bound that some block reaches.
All inputs are finite; a program needn't handle non-finite values.
Results may differ from the reference program's by a relative error of at most 0.013.
Values may be sent and summed in bfloat16 or wider, within the bound.
A program may use at most 192 MiB of HBM per device.

```python
import math
import jax
import jax.numpy as jnp
import numpy as np
from jax import lax

D = 2304
HEADS = 36
HDIM = 64
EXPERTS = 8
FF = 5760
TOPK = 2
TREE = 32
CACHE = 768
GRP = 2
PATH = 8
ROWS = 64
CAP = 18
ROW_REQS = 16
REQS = 64
PROMPT = 512
GROUPS = 8
HOLD = 1
FFH = 5760
FFD = 1440
N_REQ = 4
N_EXP = 8


def draw_queries(key, part):
    extent = (REQS, TREE, D)
    values = jnp.clip(1.5 * jax.random.normal(jax.random.fold_in(key, 1), extent, jnp.float32), -8.0, 8.0)
    return values.astype(jnp.bfloat16)


def draw_prompt_keys(key, part):
    extent = (GROUPS, PROMPT, D)
    values = jnp.clip(1.5 * jax.random.normal(jax.random.fold_in(key, 2), extent, jnp.float32), -9.0, 9.0)
    return values.astype(jnp.bfloat16)


def draw_cache_lengths(key, part):
    lengths = jax.random.randint(jax.random.fold_in(key, 3), (REQS,), 1, CACHE + 1)
    filled = jax.random.randint(jax.random.fold_in(key, 4), (), 0, REQS)
    return lengths.at[filled].set(CACHE).astype(jnp.int32)


def draw_tree_parents(key, part):
    position = jnp.arange(TREE, dtype=jnp.int32)[None, :]
    offset = jax.random.randint(jax.random.fold_in(key, 5), (REQS, TREE), 1, 5)
    parents = jnp.maximum(position - offset, 0)
    return jnp.where(position == 0, -1, parents).astype(jnp.int32)


def place_ends(values, stream_key, least, high):
    longest = values.shape.index(max(values.shape))
    spots = []
    for shift in (0, 1):
        where = [jax.random.randint(jax.random.fold_in(stream_key, axis), (), 0, length) for axis, length in enumerate(values.shape)]
        where[longest] = (where[longest] + shift) % values.shape[longest]
        spots.append(tuple(where))
    return values.at[spots[0]].set(least).at[spots[1]].set(high)


def steps_of(key, dims, shards, smallest, top_value):
    factor_of, own = 1.0, jax.random.fold_in(key, 6)
    for axis_at, blocks in shards:
        steps = jnp.exp(jax.random.uniform(jax.random.fold_in(own, axis_at), (blocks,), jnp.float32, smallest / len(shards), top_value / len(shards)))
        factor_of = factor_of * jnp.repeat(steps, dims[axis_at] // blocks).reshape([-1 if axis == axis_at else 1 for axis in range(len(dims))])
    return factor_of


def deal_out(key, own, number, rows, count, top, most, slope):
    sequence = jax.random.permutation(key, count)
    heavy_load, ordinary = shares(count, rows * top, most, slope, True), shares(count, rows * top, most, slope, False)
    places = jnp.arange(count)

    def named(tallies, offset_by):
        used = int((tallies > 0).sum())
        fixed = max(1, used // 4)
        shifted = fixed + (places - fixed + offset_by * (used - fixed)) % max(1, count - fixed)
        return jnp.zeros((count,), jnp.int32).at[sequence[jnp.where(places < fixed, places, shifted)]].set(jnp.asarray(tallies, jnp.int32))

    tallies = jnp.where(number % 4 == 0, named(heavy_load, number // 4), named(ordinary, number - number // 4 - 1))
    mixed = jax.random.permutation(jax.random.fold_in(own, 3), count)
    source_of, taker = mixed[0:count // 2 * 2:2], mixed[1:count // 2 * 2:2]
    room = jnp.minimum(tallies[source_of] - 1, most - tallies[taker]) // 2
    room = jnp.where((source_of == sequence[0]) | (taker == sequence[0]) | (tallies[taker] == 0), 0, jnp.maximum(room, 0))
    shifted = jax.random.randint(jax.random.fold_in(own, 4), (count // 2,), 0, 1 << 20) % (room + 1)
    tallies = tallies.at[source_of].add(-shifted).at[taker].add(shifted)
    labels = jnp.searchsorted(jnp.cumsum(tallies), jnp.arange(rows * top), side="right").astype(jnp.int32)
    listing = labels.reshape(top, rows).T
    listing = listing[jax.random.permutation(jax.random.fold_in(own, 1), rows)]
    offset_by = jax.random.randint(jax.random.fold_in(own, 2), (rows, 1), 0, top)
    return jnp.take_along_axis(listing, (jnp.arange(top)[None, :] + offset_by) % top, axis=1)


def shares(number_of, total, most, skew, full):
    loads = [(1 << 20) // math.isqrt(standing ** skew) + 1 for standing in range(1, number_of + 1)]
    largest = most if full else min(most, max(-(-total // number_of), total * loads[0] // sum(loads)))
    least = 1 if total - largest >= number_of - 1 else 0
    holding, spare = [largest] + [least] * (number_of - 1), total - largest - least * (number_of - 1)
    while spare > 0:
        movable = [i for i in range(1, number_of) if holding[i] < largest] or [i for i in range(1, number_of) if holding[i] < most]
        mass, budget = sum([loads[i] for i in movable]), spare
        for i in movable:
            more = min(most - holding[i], max(1, budget * loads[i] // mass), spare)
            holding[i] = holding[i] + more
            spare = spare - more
    return np.array(holding)


def centred(stream_key, shape, width, most, cuts=(), kind=jnp.bfloat16):
    factor_of = steps_of(stream_key, shape, cuts, -0.22, 0.18) if cuts else 1.0
    result = jax.random.normal(stream_key, shape, jnp.float32) * width * factor_of
    return jnp.minimum(jnp.maximum(result, -most), most).astype(kind)


def setup_inputs(seed: int = 0) -> dict:
    key_of = jax.random.split(jax.random.key(seed), 19)
    queries = draw_queries(jax.random.fold_in(key_of[18], 71), 0)
    draft_keys = centred(key_of[1], (REQS, TREE, D), 1.5, 9.0, ((0, 32),))
    draft_values = centred(key_of[2], (REQS, TREE, D), 1.0, 6.0, ((0, 32),))
    tree_parents = draw_tree_parents(jax.random.fold_in(key_of[18], 71), 0)
    cache_keys = centred(key_of[4], (REQS, CACHE, D), 1.5, 9.0, ((0, 32),))
    cache_values = centred(key_of[5], (REQS, CACHE, D), 1.0, 6.0, ((0, 32),))
    cache_lengths = draw_cache_lengths(jax.random.fold_in(key_of[18], 71), 0)
    prompt_keys = draw_prompt_keys(jax.random.fold_in(key_of[18], 71), 0)
    prompt_values = centred(key_of[8], (GROUPS, PROMPT, D), 1.0, 6.0, ((0, 4), (1, 8)))
    group_ids = place_ends(jax.random.randint(key_of[9], (REQS,), 0, GRP), jax.random.fold_in(key_of[9], 1), 0, GRP - 1).astype(jnp.int32)
    residual = centred(key_of[10], (REQS, TREE, D), 1.0, 6.0, ((0, 32),))
    norm_gain = jnp.clip(1.0 + 0.1 * jax.random.normal(key_of[11], (D,), jnp.float32), 0.5, 1.5)
    router = centred(key_of[12], (D, EXPERTS), D ** -0.5, 0.125)
    w_gate = centred(key_of[13], (N_EXP, D, FFH), D ** -0.5, 0.125, ((0, 8), (2, 4)))
    w_up = centred(key_of[14], (N_EXP, D, FFH), D ** -0.5, 0.125, ((0, 8), (2, 4)))
    w_down = centred(key_of[15], (N_EXP, FFH, D), FF ** -0.5, 0.078125, ((0, 8), (1, 4)))
    expert_ids_keys = jax.random.split(jax.random.fold_in(key_of[16], 1), REQS * TREE // ROWS)
    expert_ids_turns = jax.random.permutation(jax.random.fold_in(key_of[16], 3), REQS * TREE // ROWS)
    expert_ids = jax.vmap(lambda own, number: deal_out(jax.random.fold_in(key_of[16], 2), own, number, ROWS, EXPERTS, TOPK, CAP, 1))(expert_ids_keys, expert_ids_turns).reshape((REQS, TREE, TOPK))
    accepted_rows = place_ends(jax.random.randint(key_of[17], (REQS, PATH), 0, TREE), jax.random.fold_in(key_of[17], 1), 0, TREE - 1).astype(jnp.int32)
    return {"queries": queries, "draft_keys": draft_keys, "draft_values": draft_values, "tree_parents": tree_parents, "cache_keys": cache_keys, "cache_values": cache_values, "cache_lengths": cache_lengths, "prompt_keys": prompt_keys, "prompt_values": prompt_values, "group_ids": group_ids, "residual": residual, "norm_gain": norm_gain, "router": router, "w_gate": w_gate, "w_up": w_up, "w_down": w_down, "expert_ids": expert_ids, "accepted_rows": accepted_rows}


HIGH = lax.Precision.HIGHEST
EPSILON = 1e-05

def ancestry(parents):
    length = parents.shape[-1]
    column = jnp.arange(length, dtype=jnp.int32)
    reached = (parents[..., :, None] == column).astype(jnp.float32) + jnp.eye(length, dtype=jnp.float32)
    for repeat in range(max(1, (length - 1).bit_length())):
        reached = (jnp.einsum('...ij,...jk->...ik', reached, reached, precision=HIGH) > 0.5).astype(jnp.float32)
    return reached > 0.5

def slot_numbers(picked_ids):
    flattened = picked_ids.reshape(-1)
    onehot = (flattened[:, None] == jnp.arange(EXPERTS, dtype=jnp.int32)[None, :]).astype(jnp.int32)
    before = jnp.cumsum(onehot, axis=0) - onehot
    return lax.optimization_barrier(jnp.sum(before * onehot, axis=1)).reshape(picked_ids.shape)

def reference(queries, draft_keys, draft_values, tree_parents, cache_keys, cache_values, cache_lengths, prompt_keys, prompt_values, group_ids, residual, norm_gain, router, w_gate, w_up, w_down, expert_ids, accepted_rows):
    home = jnp.arange(REQS, dtype=jnp.int32) // ROW_REQS * GRP + group_ids
    score_scale = HDIM ** (-0.5)

    def attend_request(inputs):
        query, group, length, cache_k, cache_v, draft_k, draft_v, parents = inputs
        heads_q = query.astype(jnp.float32).reshape(TREE, HEADS, HDIM)
        keys_all = jnp.concatenate([prompt_keys[group], cache_k, draft_k], 0).astype(jnp.float32).reshape(-1, HEADS, HDIM)
        values_all = jnp.concatenate([prompt_values[group], cache_v, draft_v], 0).astype(jnp.float32).reshape(-1, HEADS, HDIM)
        scores = jnp.einsum('thd,khd->thk', heads_q, keys_all) * score_scale
        live_cache = jnp.arange(CACHE, dtype=jnp.int32) < length
        visible = jnp.concatenate([jnp.ones((TREE, PROMPT), jnp.bool_), jnp.broadcast_to(live_cache[None, :], (TREE, CACHE)), ancestry(parents)], 1)
        scores = jnp.where(visible[:, None, :], scores, -jnp.inf)
        highest = lax.optimization_barrier(jnp.max(scores, axis=-1, keepdims=True))
        weights = jnp.exp(scores - highest)
        total = lax.optimization_barrier(jnp.sum(weights, axis=-1))
        rounded = lax.optimization_barrier(weights.astype(jnp.bfloat16)).astype(jnp.float32)
        mixed = jnp.einsum('thk,khd->thd', rounded, values_all) / total[..., None]
        return mixed.reshape(TREE, D).astype(jnp.bfloat16)
    attended = lax.map(attend_request, (queries, home, cache_lengths, cache_keys, cache_values, draft_keys, draft_values, tree_parents))
    stream = (residual.astype(jnp.float32) + attended.astype(jnp.float32)).astype(jnp.bfloat16)
    rows_in = stream.reshape(-1, D).astype(jnp.float32)
    normed = (rows_in * lax.rsqrt(lax.optimization_barrier(jnp.mean(rows_in * rows_in, axis=-1, keepdims=True)) + EPSILON) * norm_gain).astype(jnp.bfloat16)
    logits = jnp.dot(normed, router, preferred_element_type=jnp.float32)
    chosen = jnp.take_along_axis(logits, expert_ids.reshape(-1, TOPK), axis=1)
    gate_first = 1.0 / (1.0 + jnp.exp(chosen[:, 1] - chosen[:, 0]))
    gates = jnp.stack([gate_first, 1.0 - gate_first], axis=1)
    blocks = N_REQ * N_EXP
    picked_ids = expert_ids.reshape(blocks, ROWS, TOPK)
    slots = jax.vmap(slot_numbers)(picked_ids)
    block_rows = normed.reshape(blocks, ROWS, D)

    def fill_block(rows_here, ids_here, slots_here):
        target = (ids_here * CAP + slots_here).reshape(-1)
        return jnp.zeros((EXPERTS * CAP, D), jnp.bfloat16).at[target].set(jnp.repeat(rows_here, TOPK, axis=0))
    buffers = jax.vmap(fill_block)(block_rows, picked_ids, slots)
    buffers = buffers.reshape(blocks, EXPERTS, CAP, D).transpose(1, 0, 2, 3).reshape(EXPERTS, blocks * CAP, D)
    gate_full = w_gate.reshape(EXPERTS, HOLD, D, FFH).transpose(0, 2, 1, 3).reshape(EXPERTS, D, FF)
    up_full = w_up.reshape(EXPERTS, HOLD, D, FFH).transpose(0, 2, 1, 3).reshape(EXPERTS, D, FF)
    down_full = w_down.reshape(EXPERTS, HOLD, FFH // FFD, FFD, D)

    def expert_out(inputs):
        rows_here, gate_w, up_w, down_w = inputs
        gate_proj = jnp.dot(rows_here, gate_w, preferred_element_type=jnp.float32)
        up_proj = jnp.dot(rows_here, up_w, preferred_element_type=jnp.float32)
        act = (jax.nn.silu(gate_proj) * up_proj).astype(jnp.bfloat16)
        act = act.reshape(rows_here.shape[0], HOLD, FFH // FFD, FFD).astype(jnp.float32)
        parts = jnp.einsum('nhrf,hrfd->hrnd', act, down_w.astype(jnp.float32))
        parts = lax.optimization_barrier(parts.astype(jnp.bfloat16)).astype(jnp.float32)
        holder = lax.optimization_barrier(lax.optimization_barrier(jnp.sum(parts, axis=1)).astype(jnp.bfloat16)).astype(jnp.float32)
        return lax.optimization_barrier(jnp.sum(holder, axis=0))
    outputs = lax.map(expert_out, (buffers, gate_full, up_full, down_full))
    block_index = jnp.arange(blocks, dtype=jnp.int32)[:, None, None]
    index = ((picked_ids * blocks + block_index) * CAP + slots).reshape(-1, TOPK).astype(jnp.int32)
    picked = outputs.reshape(-1, D)[index]
    layer_out = (rows_in + lax.optimization_barrier(jnp.sum(gates[:, :, None] * picked, axis=1))).astype(jnp.bfloat16).reshape(REQS, TREE, D)
    kept_keys = jnp.take_along_axis(draft_keys, accepted_rows[:, :, None], axis=1)
    kept_values = jnp.take_along_axis(draft_values, accepted_rows[:, :, None], axis=1)
    accepted_cache = jnp.stack([kept_keys, kept_values], axis=1)
    return (attended, layer_out, accepted_cache)
```

```python
import functools

import jax
import jax.numpy as jnp
from jax import lax
from jax.experimental import pallas as pl
from jax.experimental.pallas import tpu as pltpu
from jax.sharding import PartitionSpec as P

HEADS = 36
HDIM = 64
EXPERTS = 8
TOPK = 2
LANES = 128
PAIR = LANES // HDIM
WIDE = 256
MAIN = 16
SPILL = 2
CODE = 32
EPSILON = 1e-05
SCALE = HDIM ** (-0.5)
NT = (((1,), (1,)), ((), ()))
F32 = jnp.float32
BF16 = jnp.bfloat16
MESH = pl.DeviceIdType.MESH


def remote(src, dst, send, recv, axis, target):
    return pltpu.make_async_remote_copy(
        src_ref=src, dst_ref=dst, send_sem=send, recv_sem=recv, device_id={axis: target},
        device_id_type=MESH,
    )


def iota(shape, dim):
    return lax.broadcasted_iota(jnp.int32, shape, dim)


def flag(condition):
    return jnp.where(condition, 1.0, 0.0).astype(BF16)


def matmul(a, b):
    return jnp.dot(a, b, preferred_element_type=F32)


def matmul_nt(a, b):
    return lax.dot_general(a, b, NT, preferred_element_type=F32)


def greet_plane(size):
    e = lax.axis_index("exp")
    barrier = pltpu.get_barrier_semaphore()
    for step in range(1, size):
        pl.semaphore_signal(
            barrier, inc=1, device_id={"exp": lax.rem(e + step, size)}, device_id_type=MESH
        )


def owners_of(size, blocks):
    each = -(-blocks // size)
    while blocks % each:
        each += 1
    count = blocks // each
    idle = size - count
    devices = list(range(size))
    if idle == 2 and size == 8:
        devices = [0, 1, 2, 4, 6, 7]
    else:
        devices = [i * size // count for i in range(count)]
    return each, devices


def attention_kernel(
    size, each, owners,
    len_ref, meta_ref, gain_ref, q_hbm, dk_hbm, dv_hbm, res_hbm, ck_hbm, cv_hbm, pk_hbm, pv_hbm,
    att_ref, stream_ref, normed_ref, kept_ref, code_ref,
    ck, cv, q, dk, dv, res, group, acc, top_all, sum_all, kp, vp, qp, gp, staged, landed,
    csem, lsem, psend, precv, own, osend, orecv, oown,
):
    me = lax.axis_index("exp")
    rows, width = q.shape
    requests, cache = ck.shape[0], ck.shape[2]
    tree = rows // requests
    chunks = width // WIDE
    span = each * LANES
    count = len(owners)
    groups, positions = pk_hbm.shape[0], pk_hbm.shape[1]
    wide_heads = WIDE // HDIM

    def cols(g):
        return pl.ds(pl.multiple_of(g * WIDE, WIDE), WIDE)

    def cache_copy(which, b, g):
        src, dst = ((ck_hbm, ck), (cv_hbm, cv))[which]
        return pltpu.make_async_copy(
            src.at[b, :, cols(g)], dst.at[b, g], csem.at[which, b, g]
        )

    small = [
        pltpu.make_async_copy(src, dst, lsem.at[i])
        for i, (src, dst) in enumerate(((q_hbm, q), (dk_hbm, dk), (dv_hbm, dv), (res_hbm, res)))
    ]
    for copy in small[:3]:
        copy.start()

    def load(g, carry):
        for b in range(requests):
            for which in range(2):
                cache_copy(which, b, g).start()
        return carry

    greet_plane(size)

    row8 = iota((8, LANES), 0)
    group[...] = jnp.where(row8 == 0, meta_ref[4:5, 0:1], meta_ref[4:5, 1:2])
    for b in range(2, requests):
        group[...] = jnp.where(row8 == b, meta_ref[4:5, b : b + 1], group[...])

    pl.semaphore_wait(pltpu.get_barrier_semaphore(), size - 1)

    def device_of(i):
        device = i + owners[0]
        for j in range(1, count):
            device += jnp.where(i >= j, owners[j] - owners[j - 1] - 1, 0)
        return device

    slot = jnp.int32(0)
    holds = jnp.bool_(False)
    for i, device in enumerate(owners):
        slot = jnp.where(me == device, i, slot)
        holds = jnp.logical_or(holds, me == device)

    def from_source(s):
        return (
            kp.at[:, pl.ds(pl.multiple_of(s * positions, positions), positions), :],
            vp.at[:, pl.ds(pl.multiple_of(s * positions, positions), positions), :],
            qp.at[pl.ds(pl.multiple_of(s * rows, rows), rows), :],
            gp.at[s],
        )

    def to_owner(i):
        at = pl.ds(pl.multiple_of(i * span, LANES), span)
        return (pk_hbm.at[:, :, at], pv_hbm.at[:, :, at], q_hbm.at[:, at], group)

    def send_heads(o, carry):
        i = lax.rem(o + me, count)
        device = device_of(i)

        @pl.when(device != me)
        def _():
            for kind, (src, dst) in enumerate(zip(to_owner(i), from_source(me))):
                remote(
                    src, dst, psend.at[kind, i], precv.at[kind, me], "exp", device
                ).start()

        @pl.when(device == me)
        def _():
            for kind, (src, dst) in enumerate(zip(to_owner(i), from_source(me))):
                pltpu.make_async_copy(src, dst, own.at[kind]).start()

        return carry

    lax.fori_loop(0, count, send_heads, 0)
    lax.fori_loop(0, chunks, load, 0)
    small[3].start()

    eye = flag(iota((LANES, LANES), 0) == iota((LANES, LANES), 1))
    columns = matmul_nt(eye, meta_ref[...].astype(BF16))
    parent = columns[:rows, 0:1].astype(jnp.int32)
    at_row, at_col = iota((rows, rows), 0), iota((rows, rows), 1)
    base = at_row // tree * tree
    reached = jnp.logical_or(
        at_row == at_col, jnp.logical_and(at_col - base == parent, parent >= 0)
    )
    for _ in range(max(1, (tree - 1).bit_length())):
        step = flag(reached)
        reached = matmul(step, step) > 0.5
    related = jnp.where(reached, 1.0, 0.0)

    first, second = columns[:rows, 1:2], columns[:rows, 2:3]
    lane = iota((rows, LANES), 1)
    expert = lane.astype(F32)
    named = flag(jnp.logical_or(expert == first, expert == second))
    before = matmul(flag(at_col < at_row), named)
    codes = [
        e * CODE + jnp.sum(jnp.where(expert == e, before, 0.0), axis=1, keepdims=True)
        for e in (first, second)
    ]
    code_columns = jnp.where(lane == 0, codes[0], jnp.where(lane == 1, codes[1], 0.0))
    code_ref[...] = jnp.zeros_like(code_ref)
    code_ref[:, :rows] = matmul_nt(eye[:8], code_columns.astype(BF16))

    for copy in small[:3]:
        copy.wait()
    picks = columns[:MAIN, 3:4].astype(jnp.int32)
    path = kept_ref.shape[0] // (2 * requests)
    wanted = flag(
        iota((MAIN, rows), 1)
        == picks + jnp.where(iota((MAIN, rows), 0) // path == 1, tree, 0)
    )
    for kind, ref in enumerate((dk, dv)):
        kept = matmul(wanted, ref[...]).astype(BF16)
        for b in range(requests):
            kept_ref[pl.ds((2 * b + kind) * path, path), :] = kept[b * path : (b + 1) * path]

    head_wide = iota((tree, WIDE), 1) // HDIM
    masks = [flag(head_wide == h) for h in range(wide_heads)]
    stat_lane = iota((tree, LANES), 1)
    seen = [
        jnp.concatenate([related[b * tree : (b + 1) * tree]] * wide_heads, axis=0)
        for b in range(requests)
    ]
    slot_at = iota((wide_heads * tree, cache), 1)
    top_all[...] = jnp.zeros_like(top_all)
    sum_all[...] = jnp.zeros_like(sum_all)

    def local(g, carry):
        for b in range(requests):
            here = slice(b * tree, (b + 1) * tree)
            for which in range(2):
                cache_copy(which, b, g).wait()
            query = q[here, cols(g)] * BF16(SCALE)
            stacked = jnp.concatenate([query * mask for mask in masks], axis=0)
            s_cache = matmul_nt(stacked, ck[b, g])
            s_cache = jnp.where(slot_at < len_ref[b], s_cache, -jnp.inf)
            s_tree = jnp.where(seen[b] > 0.5, matmul_nt(stacked, dk[:, cols(g)]), -jnp.inf)
            top = jnp.maximum(
                jnp.max(s_cache, axis=1, keepdims=True), jnp.max(s_tree, axis=1, keepdims=True)
            )
            w_cache = jnp.exp(s_cache - top)
            w_tree = jnp.exp(s_tree - top)
            total = jnp.sum(w_cache, axis=1, keepdims=True) + jnp.sum(
                w_tree, axis=1, keepdims=True
            )
            mixed = matmul(w_cache.astype(BF16), cv[b, g])
            mixed += matmul(w_tree.astype(BF16), dv[:, cols(g)])
            out = mixed[:tree]
            tops, sums = top_all[here], sum_all[here]
            for h in range(wide_heads):
                part = slice(h * tree, (h + 1) * tree)
                if h:
                    out = jnp.where(head_wide == h, mixed[part], out)
                at = g * wide_heads + h
                tops = jnp.where(stat_lane == at, top[part], tops)
                sums = jnp.where(stat_lane == at, total[part], sums)
            acc[here, cols(g)] = out
            top_all[here] = tops
            sum_all[here] = sums
        return carry

    lax.fori_loop(0, chunks, local, 0)

    @pl.when(holds)
    def _():
        for kind, (src, dst) in enumerate(zip(to_owner(slot), from_source(me))):
            pltpu.make_async_copy(src, dst, own.at[kind]).wait()

        def arrive(o, carry):
            source = lax.rem(me + o, size)
            for kind, ref in enumerate(from_source(source)):
                remote(
                    ref, ref, psend.at[kind, 0], precv.at[kind, source], "exp", source
                ).wait_recv()
            return carry

        lax.fori_loop(1, size, arrive, 0)
        duo = 2 * rows
        pairs = size // 2
        half = iota((duo, LANES), 1) // HDIM
        sides = [flag(half == h) for h in range(PAIR)]
        left = half == 0
        stat_at = iota((duo, LANES), 1)

        def attend(step, carry):
            c = lax.rem(me // 2 + 1 + step, pairs)
            here = pl.ds(pl.multiple_of(c * duo, duo), duo)
            marks = []
            for s in range(2):
                mark = gp[2 * c + s]
                for b in range(requests):
                    marks.append(jnp.broadcast_to(mark[b : b + 1, 0:1], (tree, 1)))
            mark = jnp.concatenate(marks * PAIR, axis=0)
            stats = jnp.zeros((duo, LANES), F32)
            for j in range(each):
                at = slice(j * LANES, (j + 1) * LANES)
                query = qp[here, at] * BF16(SCALE)
                stacked = jnp.concatenate([query * side for side in sides], axis=0)
                scores = matmul_nt(stacked, kp[0, :, at])
                for g in range(1, groups):
                    scores = jnp.where(mark == g, matmul_nt(stacked, kp[g, :, at]), scores)
                top = jnp.max(scores, axis=1, keepdims=True).astype(BF16).astype(F32)
                weights = jnp.exp(scores - top)
                total = jnp.sum(weights, axis=1, keepdims=True)
                weights = weights.astype(BF16)
                mixed = None
                for g in range(groups):
                    part = matmul(
                        jnp.where(mark == g, weights, jnp.zeros_like(weights)), vp[g, :, at]
                    )
                    mixed = part if mixed is None else mixed + part
                staged[here, at] = jnp.where(left, mixed[:duo], mixed[duo:]).astype(BF16)
                high = total.astype(BF16).astype(F32)
                for h in range(PAIR):
                    part = slice(h * duo, (h + 1) * duo)
                    head = slot * (each * PAIR) + j * PAIR + h
                    stats = jnp.where(stat_at == head, top[part], stats)
                    stats = jnp.where(stat_at == head + HEADS, high[part], stats)
                    stats = jnp.where(
                        stat_at == head + 2 * HEADS, (total - high)[part], stats
                    )
            staged[here, span:] = stats.astype(BF16)
            for s in range(2):
                target = 2 * c + s
                src = staged.at[pl.ds(pl.multiple_of(target * rows, rows), rows), :]

                @pl.when(target != me)
                def _():
                    remote(
                        src, landed.at[slot], osend.at[target], orecv.at[slot], "exp", target
                    ).start()

                @pl.when(target == me)
                def _():
                    pltpu.make_async_copy(src, landed.at[slot], oown.at[0]).start()

            return carry

        lax.fori_loop(0, pairs, attend, 0)
        mine = staged.at[pl.ds(pl.multiple_of(me * rows, rows), rows), :]
        pltpu.make_async_copy(mine, landed.at[slot], oown.at[0]).wait()

    small[3].wait()
    for i, device in enumerate(owners):
        @pl.when(me != device)
        def _():
            remote(
                landed.at[i], landed.at[i], osend.at[0], orecv.at[i], "exp", device
            ).wait_recv()

    stats = landed[0, :, span:].astype(F32)
    for i in range(1, count):
        stats += landed[i, :, span:].astype(F32)
    theirs = pltpu.roll(stats, LANES - HEADS, 1) + pltpu.roll(stats, LANES - 2 * HEADS, 1)
    used = lane < HEADS
    ours = jnp.where(used, sum_all[...], 1.0)
    theirs = jnp.where(used, theirs, 1.0)
    top = jnp.maximum(top_all[...], stats)
    own_scale = jnp.exp(top_all[...] - top)
    far_scale = jnp.exp(jnp.where(used, stats, top) - top)
    total = own_scale * ours + far_scale * theirs
    own_scale, far_scale = own_scale / total, far_scale / total
    squares = jnp.zeros((rows, 1), F32)
    left = lane < HDIM
    for block in range(width // LANES):
        at = slice(block * LANES, (block + 1) * LANES)
        i, j = divmod(block, each)
        a = PAIR * block
        out = acc[:, at] * jnp.where(left, own_scale[:, a : a + 1], own_scale[:, a + 1 : a + 2])
        out += landed[i, :, j * LANES : (j + 1) * LANES].astype(F32) * jnp.where(
            left, far_scale[:, a : a + 1], far_scale[:, a + 1 : a + 2]
        )
        attended = out.astype(BF16)
        att_ref[:, at] = attended
        stream = (res[:, at].astype(F32) + attended.astype(F32)).astype(BF16)
        stream_ref[:, at] = stream
        stream = stream.astype(F32)
        squares += jnp.sum(stream * stream, axis=1, keepdims=True)
    factor = lax.rsqrt(squares / width + EPSILON)
    normed_ref[...] = (stream_ref[...].astype(F32) * factor * gain_ref[...]).astype(BF16)

    def sent(i, carry):
        device = device_of(i)

        @pl.when(device != me)
        def _():
            for kind, (src, dst) in enumerate(zip(to_owner(i), from_source(me))):
                remote(
                    src, dst, psend.at[kind, i], precv.at[kind, me], "exp", device
                ).wait_send()

        return carry

    lax.fori_loop(0, count, sent, 0)

    @pl.when(holds)
    def _():
        def returned(o, carry):
            target = lax.rem(me + o, size)
            src = staged.at[pl.ds(pl.multiple_of(target * rows, rows), rows), :]
            remote(
                src, landed.at[slot], osend.at[target], orecv.at[slot], "exp", target
            ).wait_send()
            return carry

        lax.fori_loop(1, size, returned, 0)


def attention(
    meta, lengths, gain, queries, draft_keys, draft_values, residual, cache_keys, cache_values,
    prompt_keys, prompt_values, size,
):
    requests, tree, width = queries.shape
    rows, cache = requests * tree, cache_keys.shape[1]
    groups, positions = prompt_keys.shape[:2]
    each, owners = owners_of(size, width // LANES)
    count, span, chunks = len(owners), each * LANES, width // WIDE
    path = 8
    flat = lambda a: a.reshape(rows, width)
    vmem = pl.BlockSpec(memory_space=pltpu.VMEM)
    hbm = pl.BlockSpec(memory_space=pl.ANY)
    dma = pltpu.SemaphoreType.DMA
    row_block = jax.ShapeDtypeStruct((rows, width), BF16)
    return pl.pallas_call(
        functools.partial(attention_kernel, size, each, owners),
        out_shape=[
            row_block, row_block, row_block,
            jax.ShapeDtypeStruct((requests * 2 * path, width), BF16),
            jax.ShapeDtypeStruct((8, LANES), F32),
        ],
        in_specs=[pl.BlockSpec(memory_space=pltpu.SMEM), vmem, vmem] + [hbm] * 8,
        out_specs=[vmem] * 5,
        scratch_shapes=[
            pltpu.VMEM((requests, chunks, cache, WIDE), BF16),
            pltpu.VMEM((requests, chunks, cache, WIDE), BF16),
            pltpu.VMEM((rows, width), BF16),
            pltpu.VMEM((rows, width), BF16),
            pltpu.VMEM((rows, width), BF16),
            pltpu.VMEM((rows, width), BF16),
            pltpu.VMEM((8, LANES), F32),
            pltpu.VMEM((rows, width), F32),
            pltpu.VMEM((rows, LANES), F32),
            pltpu.VMEM((rows, LANES), F32),
            pltpu.VMEM((groups, size * positions, span), BF16),
            pltpu.VMEM((groups, size * positions, span), BF16),
            pltpu.VMEM((size * rows, span), BF16),
            pltpu.VMEM((size, 8, LANES), F32),
            pltpu.VMEM((size * rows, span + LANES), BF16),
            pltpu.VMEM((count, rows, span + LANES), BF16),
            dma((2, requests, chunks)), dma((4,)), dma((4, count)), dma((4, size)), dma((4,)),
            dma((size,)), dma((count,)), dma((1,)),
        ],
        compiler_params=pltpu.CompilerParams(
            collective_id=0, has_side_effects=True, vmem_limit_bytes=44 * 1024 * 1024
        ),
        name="attention",
    )(
        lengths, meta, gain, flat(queries), flat(draft_keys), flat(draft_values), flat(residual),
        cache_keys, cache_values, prompt_keys, prompt_values,
    )


def expert_kernel(
    depth, size,
    normed_ref, stream_ref, code_ref, router_ref, wg_hbm, wu_hbm, wd_hbm,
    out_ref,
    wg, wu, wd, held, codes, staged, spilled, x, x_spill, hidden, y, y_spill, land, land_spill,
    mix, mix_spill, sums, part, passed,
    wsem, zsend, zrecv, dsend, drecv, ysend, yrecv, rsend, rrecv,
):
    z, e = lax.axis_index("req"), lax.axis_index("exp")
    rows, width = normed_ref.shape
    units = wg.shape[1]
    holders = size // EXPERTS
    spread = SPILL * depth
    split = MAIN // spread
    piece = width // split
    main = size * MAIN
    low = z < depth // 2

    weights = [
        pltpu.make_async_copy(src, dst, wsem.at[i])
        for i, (src, dst) in enumerate(((wg_hbm, wg), (wu_hbm, wu), (wd_hbm, wd)))
    ]
    held[z] = normed_ref[...]
    codes[z] = code_ref[...]

    barrier = pltpu.get_barrier_semaphore()
    greet_plane(size)

    @pl.when(z < depth - 1)
    def _():
        pl.semaphore_signal(barrier, inc=1, device_id={"req": z + 1}, device_id_type=MESH)

    @pl.when(z > 0)
    def _():
        pl.semaphore_signal(barrier, inc=1, device_id={"req": z - 1}, device_id_type=MESH)

    pl.semaphore_wait(
        barrier, size - 1 + jnp.where(z > 0, 1, 0) + jnp.where(z < depth - 1, 1, 0)
    )

    def order(p):
        near = jnp.where(low, z, depth - 1 - z)
        step = (p + 1) // 2
        at = jnp.where(p > 2 * near, p, jnp.where(p % 2 == 1, near - step, near + step))
        return jnp.where(low, at, depth - 1 - at)

    def place(k):
        near = jnp.where(low, z, depth - 1 - z)
        at = jnp.where(low, k, depth - 1 - k)
        gap = at - near
        return jnp.where(
            gap == 0, 0, jnp.where(gap < 0, -2 * gap - 1, jnp.where(gap <= near, 2 * gap, at))
        )

    def along(k, way):
        target = z + 1 if way == 0 else z - 1
        return [
            remote(ref.at[k], ref.at[k], zsend.at[kind, way, k], zrecv.at[kind, k], "req", target)
            for kind, ref in enumerate((codes, held))
        ]

    def passes(k, way):
        if way == 0:
            return jnp.logical_and(k <= z, z < depth - 1)
        return jnp.logical_and(k >= z, z > 0)

    def pass_on(k):
        for way in range(2):
            @pl.when(passes(k, way))
            def _():
                for copy in along(k, way):
                    copy.start()

    def block(p, target):
        return pl.ds(pl.multiple_of((p * size + target) * MAIN, MAIN), MAIN)

    def spot(target):
        return pl.ds(pl.multiple_of(target * MAIN, MAIN), MAIN)

    wanted = iota((main, rows), 0)
    wanted_code = ((wanted // MAIN) // holders * CODE + wanted % MAIN).astype(F32)

    def stage(p, carry):
        k = order(p)

        @pl.when(p > 0)
        def _():
            for copy in along(k, 0):
                copy.wait_recv()

        pass_on(k)
        code = codes[k]
        pick = flag(
            jnp.logical_or(code[0:1, :rows] == wanted_code, code[1:2, :rows] == wanted_code)
        )
        here = pl.ds(pl.multiple_of(p * main, main), main)
        step = 3 * WIDE if width % (3 * WIDE) == 0 else WIDE
        for c in range(0, width, step):
            staged[here, c : c + step] = matmul(pick, held[k, :, c : c + step]).astype(BF16)

        def send(o, carry):
            target = lax.rem(e + o, size)
            remote(
                staged.at[block(p, target)], x.at[block(p, e)], dsend.at[p, o], drecv.at[p, e],
                "exp", target,
            ).start()
            return carry

        lax.fori_loop(1, size, send, 0)
        x[block(p, e), :] = staged[block(p, e), :]
        return carry

    def all_landed(p, ref, sem, at):
        def wait(o, carry):
            source = lax.rem(e + o, size)
            remote(
                ref.at[at(source)], ref.at[at(source)], dsend.at[0, 0], sem.at[p, source], "exp",
                source,
            ).wait_recv()
            return carry

        lax.fori_loop(1, size, wait, 0)

    def experts(start, count):
        for at in range(start, start + count, 2 * WIDE):
            some_rows(at, min(2 * WIDE, start + count - at))

    def some_rows(start, count):
        here = slice(start, start + count)

        def up(at, n):
            gate = matmul(x[here, :], wg[:, pl.ds(at, n)])
            value = matmul(x[here, :], wu[:, pl.ds(at, n)])
            hidden[0:count, pl.ds(at, n)] = (gate / (1.0 + jnp.exp(-gate)) * value).astype(BF16)

        def up_loop(t, carry):
            up(pl.multiple_of(t * WIDE, WIDE), WIDE)
            return carry

        lax.fori_loop(0, units // WIDE, up_loop, 0)
        if units % WIDE:
            up(units // WIDE * WIDE, units % WIDE)

        def down(t, carry):
            at = pl.ds(pl.multiple_of(t * WIDE, WIDE), WIDE)
            y[here, at] = matmul(hidden[0:count, :], wd[:, at]).astype(BF16)
            return carry

        lax.fori_loop(0, width // WIDE, down, 0)

    def give_back(p):
        def send(o, carry):
            target = lax.rem(e + o, size)
            remote(
                y.at[block(p, target)], land.at[block(p, e)], ysend.at[p, o], yrecv.at[p, e],
                "exp", target,
            ).start()
            return carry

        lax.fori_loop(1, size, send, 0)
        land[block(p, e), :] = y[block(p, e), :]

    for copy in weights:
        copy.start()
    lax.fori_loop(0, depth - 1, stage, 0)
    for copy in weights:
        copy.wait()
    near = depth // 2
    for p in range(near):
        all_landed(p, x, drecv, lambda s, p=p: block(p, s))
    experts(0, near * main)
    stage(depth - 1, 0)

    slot = iota((main, rows), 0)
    slot_row = slot % MAIN
    slot_side, slot_item = slot_row // spread, slot_row % spread
    spill_code = ((slot // MAIN) // holders * CODE + MAIN + slot_item % SPILL).astype(F32)
    spill_sum = None
    for k in range(depth):
        code = codes[k]
        match = jnp.logical_and(
            jnp.logical_or(code[0:1, :rows] == spill_code, code[1:2, :rows] == spill_code),
            slot_item // SPILL == k,
        )
        for side in range(split):
            picked = matmul(
                flag(jnp.logical_and(match, slot_side == side)),
                held[k, :, side * piece : (side + 1) * piece],
            )
            spill_sum = picked if spill_sum is None else spill_sum + picked
    spilled[...] = spill_sum.astype(BF16)

    def send_spill(o, carry):
        target = lax.rem(e + o, size)
        remote(
            spilled.at[spot(target)], x_spill.at[spot(e)], dsend.at[depth, o], drecv.at[depth, e],
            "exp", target,
        ).start()
        return carry

    lax.fori_loop(1, size, send_spill, 0)
    x_spill[spot(e), :] = spilled[spot(e), :]
    for p in range(1, near):
        give_back(p)

    eye = flag(iota((rows, rows), 0) == iota((rows, rows), 1))
    mixed_slot = iota((rows, main), 1)
    mixed_code = ((mixed_slot // MAIN) // holders * CODE + mixed_slot % MAIN).astype(F32)
    mixed_row = mixed_slot % MAIN
    mixed_side, mixed_item = mixed_row // spread, mixed_row % spread
    mixed_spill = ((mixed_slot // MAIN) // holders * CODE + MAIN + mixed_item % SPILL).astype(F32)

    def weigh(k, carry):
        columns = matmul_nt(eye, codes[k][:, :rows].astype(BF16))
        first, second = columns[:, 0:1], columns[:, 1:2]
        logits = matmul(held[k], router_ref[...])
        choice = (iota(logits.shape, 1) * CODE).astype(F32)

        def chosen(code):
            hit = jnp.logical_and(code >= choice, code < choice + CODE)
            return jnp.sum(jnp.where(hit, logits, 0.0), axis=1, keepdims=True)

        gate = 1.0 / (1.0 + jnp.exp(chosen(second) - chosen(first)))
        mix[k] = (
            jnp.where(first == mixed_code, gate, 0.0)
            + jnp.where(second == mixed_code, 1.0 - gate, 0.0)
        ).astype(BF16)
        spill = jnp.where(first == mixed_spill, gate, 0.0) + jnp.where(
            second == mixed_spill, 1.0 - gate, 0.0
        )
        spill = jnp.where(mixed_item // SPILL == k, spill, 0.0)
        for side in range(split):
            mix_spill[k, side] = jnp.where(mixed_side == side, spill, 0.0).astype(BF16)
        return carry

    lax.fori_loop(0, depth, weigh, 0)

    for p in range(near, depth):
        all_landed(p, x, drecv, lambda s, p=p: block(p, s))
    all_landed(depth, x_spill, drecv, spot)
    few = size * spread
    few_row, few_col = iota((few, main), 0), iota((few, main), 1)
    for side in range(split):
        unpack = flag(few_col == few_row // spread * MAIN + side * spread + few_row % spread)
        x[depth * main :, side * piece : (side + 1) * piece] = matmul(
            unpack, x_spill[...]
        ).astype(BF16)
    experts(near * main, (depth - near) * main + few)
    few_row, few_col = iota((main, few), 1), iota((main, few), 0)
    packed = None
    for side in range(split):
        pack = flag(few_col == few_row // spread * MAIN + side * spread + few_row % spread)
        moved = matmul(pack, y[depth * main :, side * piece : (side + 1) * piece])
        packed = moved if packed is None else packed + moved
    y_spill[...] = packed.astype(BF16)

    def return_spill(o, carry):
        target = lax.rem(e + o, size)
        remote(
            y_spill.at[spot(target)], land_spill.at[spot(e)], ysend.at[depth, o],
            yrecv.at[depth, e], "exp", target,
        ).start()
        return carry

    lax.fori_loop(1, size, return_spill, 0)
    land_spill[spot(e), :] = y_spill[spot(e), :]
    for p in range(depth - 1, near - 1, -1):
        give_back(p)
    give_back(0)

    def relay(h, side, way):
        target = z + 1 if way == 0 else z - 1
        at = jnp.where(jnp.logical_and(way == 1, target == h), depth, h)
        return remote(
            part.at[h, side], passed.at[at, side], rsend.at[h, side], rrecv.at[at, side], "req",
            target,
        )

    def arrived(at, side):
        remote(
            passed.at[at, side], passed.at[at, side], rsend.at[0, 0], rrecv.at[at, side], "req",
            jnp.where(z > 0, z - 1, z + 1),
        ).wait_recv()

    def combine(h, side):
        p = place(h)
        here = pl.ds(pl.multiple_of(p * main, main), main)
        at = slice(side * piece, (side + 1) * piece)
        return matmul(mix[h], land[here, at]) + matmul(mix_spill[h, side], land_spill[...])

    all_landed(depth, land_spill, yrecv, spot)
    rank = jnp.where(low, 2 * z, 2 * (depth - 1 - z) + 1)

    def reduce(j, carry):
        i = j + jnp.where(j >= rank, 1, 0)
        h = jnp.where(i % 2 == 0, i // 2, depth - 1 - i // 2)
        p = place(h)
        all_landed(p, land, yrecv, lambda s: block(p, s))
        rising = h > z
        joined = jnp.logical_or(
            jnp.logical_and(rising, z > 0),
            jnp.logical_and(jnp.logical_not(rising), z < depth - 1),
        )
        for side in range(split):
            sums[...] = combine(h, side)

            @pl.when(joined)
            def _():
                arrived(h, side)
                sums[...] += passed[h, side].astype(F32)

            part[h, side] = sums[...].astype(BF16)

            @pl.when(rising)
            def _():
                relay(h, side, 0).start()

            @pl.when(jnp.logical_not(rising))
            def _():
                relay(h, side, 1).start()

        return carry

    lax.fori_loop(0, depth - 1, reduce, 0)
    all_landed(0, land, yrecv, lambda s: block(0, s))
    for side in range(split):
        at = slice(side * piece, (side + 1) * piece)
        sums[...] = combine(z, side) + stream_ref[:, at].astype(F32)

        @pl.when(z > 0)
        def _():
            arrived(z, side)
            sums[...] += passed[z, side].astype(F32)

        @pl.when(z < depth - 1)
        def _():
            arrived(depth, side)
            sums[...] += passed[depth, side].astype(F32)

        out_ref[:, at] = sums[...].astype(BF16)

    def finish(k, carry):
        for way in range(2):
            @pl.when(passes(k, way))
            def _():
                for copy in along(k, way):
                    copy.wait_send()

        for side in range(split):
            @pl.when(k > z)
            def _():
                relay(k, side, 0).wait_send()

            @pl.when(k < z)
            def _():
                relay(k, side, 1).wait_send()

        def lane_done(o, carry):
            target = lax.rem(e + o, size)
            remote(
                staged.at[block(k, target)], x.at[block(k, e)], dsend.at[k, o], drecv.at[k, e],
                "exp", target,
            ).wait_send()
            remote(
                y.at[block(k, target)], land.at[block(k, e)], ysend.at[k, o], yrecv.at[k, e],
                "exp", target,
            ).wait_send()
            return carry

        lax.fori_loop(1, size, lane_done, 0)
        return carry

    lax.fori_loop(0, depth, finish, 0)

    def spill_done(o, carry):
        target = lax.rem(e + o, size)
        remote(
            spilled.at[spot(target)], x_spill.at[spot(e)], dsend.at[depth, o], drecv.at[depth, e],
            "exp", target,
        ).wait_send()
        remote(
            y_spill.at[spot(target)], land_spill.at[spot(e)], ysend.at[depth, o],
            yrecv.at[depth, e], "exp", target,
        ).wait_send()
        return carry

    lax.fori_loop(1, size, spill_done, 0)


def expert_layer(normed, stream, code, router, w_gate, w_up, w_down, depth, size):
    rows, width = normed.shape
    units = w_gate.shape[1]
    spread = SPILL * depth
    split = MAIN // spread
    piece = width // split
    main = size * MAIN
    total = depth * main + size * spread
    most = min(2 * WIDE, total - depth // 2 * main)
    dma = pltpu.SemaphoreType.DMA
    vmem = pl.BlockSpec(memory_space=pltpu.VMEM)
    hbm = pl.BlockSpec(memory_space=pl.ANY)
    return pl.pallas_call(
        functools.partial(expert_kernel, depth, size),
        out_shape=jax.ShapeDtypeStruct((rows, width), BF16),
        in_specs=[vmem] * 4 + [hbm] * 3,
        out_specs=vmem,
        scratch_shapes=[
            pltpu.VMEM((width, units), BF16),
            pltpu.VMEM((width, units), BF16),
            pltpu.VMEM((units, width), BF16),
            pltpu.VMEM((depth, rows, width), BF16),
            pltpu.VMEM((depth, 8, LANES), F32),
            pltpu.VMEM((depth * main, width), BF16),
            pltpu.VMEM((main, piece), BF16),
            pltpu.VMEM((total, width), BF16),
            pltpu.VMEM((main, piece), BF16),
            pltpu.VMEM((most, units), BF16),
            pltpu.VMEM((total, width), BF16),
            pltpu.VMEM((main, piece), BF16),
            pltpu.VMEM((depth * main, width), BF16),
            pltpu.VMEM((main, piece), BF16),
            pltpu.VMEM((depth, rows, main), BF16),
            pltpu.VMEM((depth, split, rows, main), BF16),
            pltpu.VMEM((rows, piece), F32),
            pltpu.VMEM((depth, split, rows, piece), BF16),
            pltpu.VMEM((depth + 1, split, rows, piece), BF16),
            dma((3,)), dma((2, 2, depth)), dma((2, depth)),
            dma((depth + 1, size)), dma((depth + 1, size)),
            dma((depth + 1, size)), dma((depth + 1, size)),
            dma((depth, split)), dma((depth + 1, split)),
        ],
        compiler_params=pltpu.CompilerParams(
            collective_id=1, has_side_effects=True, vmem_limit_bytes=(48 if depth <= 4 else 60) * 1024 * 1024
        ),
        name="experts",
    )(normed, stream, code, router, w_gate, w_up, w_down)


def on_device(
    queries,
    draft_keys,
    draft_values,
    tree_parents,
    cache_keys,
    cache_values,
    cache_lengths,
    prompt_keys,
    prompt_values,
    group_ids,
    residual,
    norm_gain,
    router,
    w_gate,
    w_up,
    w_down,
    expert_ids,
    accepted_rows,
):
    requests, tree, width = queries.shape
    rows = requests * tree
    depth, size = lax.axis_size("req"), lax.axis_size("exp")

    def line(values):
        values = values.reshape(-1).astype(F32)
        return jnp.pad(values, (0, LANES - values.shape[0]))

    nothing = jnp.zeros((LANES,), F32)
    meta = jnp.stack(
        [
            line(tree_parents), line(expert_ids[:, :, 0]), line(expert_ids[:, :, 1]),
            line(accepted_rows), line(group_ids), nothing, nothing, nothing,
        ]
    )
    attended, stream, normed, kept, code = attention(
        meta, cache_lengths, norm_gain.reshape(1, width), queries, draft_keys, draft_values,
        residual, cache_keys, cache_values, prompt_keys, prompt_values, size,
    )
    layer_out = expert_layer(
        normed, stream, code, router, w_gate[0], w_up[0], w_down[0], depth, size
    )
    return (
        attended.reshape(requests, tree, width),
        layer_out.reshape(requests, tree, width),
        kept.reshape(requests, 2, accepted_rows.shape[1], width),
    )


def solution(mesh):
    both = ("req", "exp")
    return jax.shard_map(
        on_device,
        mesh=mesh,
        in_specs=(
            P(both, None, None),
            P(both, None, None),
            P(both, None, None),
            P(both, None),
            P(both, None, None),
            P(both, None, None),
            P(both),
            P("req", "exp", None),
            P("req", "exp", None),
            P(both),
            P(both, None, None),
            P(),
            P(),
            P("exp", None, "req"),
            P("exp", None, "req"),
            P("exp", "req", None),
            P(both, None, None),
            P(both, None),
        ),
        out_specs=(
            P(both, None, None),
            P(both, None, None),
            P(both, None, None, None),
        ),
        check_vma=False,
    )
```

```python
import functools

import jax
import jax.numpy as jnp
from jax import lax
from jax.experimental import pallas as pl
from jax.experimental.pallas import tpu as pltpu
from jax.sharding import PartitionSpec as P

HEADS = 36
HDIM = 64
EXPERTS = 8
TOPK = 2
LANES = 128
PAIR = LANES // HDIM
WIDE = 256
MAIN = 16
SPILL = 2
CODE = 32
EPSILON = 1e-05
SCALE = HDIM ** (-0.5)
NT = (((1,), (1,)), ((), ()))
F32 = jnp.float32
BF16 = jnp.bfloat16
MESH = pl.DeviceIdType.MESH


def remote(src, dst, send, recv, axis, target):
    return pltpu.make_async_remote_copy(
        src_ref=src, dst_ref=dst, send_sem=send, recv_sem=recv, device_id={axis: target},
        device_id_type=MESH,
    )


def iota(shape, dim):
    return lax.broadcasted_iota(jnp.int32, shape, dim)


def flag(condition):
    return jnp.where(condition, 1.0, 0.0).astype(BF16)


def matmul(a, b):
    return jnp.dot(a, b, preferred_element_type=F32)


def matmul_nt(a, b):
    return lax.dot_general(a, b, NT, preferred_element_type=F32)


def greet_plane(size):
    e = lax.axis_index("exp")
    barrier = pltpu.get_barrier_semaphore()
    for step in range(1, size):
        pl.semaphore_signal(
            barrier, inc=1, device_id={"exp": lax.rem(e + step, size)}, device_id_type=MESH
        )


def share_of(size, blocks):
    each = blocks // size
    more = blocks - each * size
    return each, [i * (size - 1) // max(more - 1, 1) for i in range(more)]


def attention_kernel(
    size, each, extras,
    len_ref, group_ref, parent_ref, chosen_ref, pick_ref, gain_ref, q_hbm, dk_hbm, dv_hbm, res_hbm, ck_hbm, cv_hbm, pk_hbm, pv_hbm,
    att_ref, stream_ref, normed_ref, kept_ref, code_ref,
    ck, cv, q, dk, dv, res, group, acc, top_all, sum_all, kp, vp, qp, gp, staged, landed, landed_more,
    stats, csem, lsem, psend, precv, own, msend, mrecv, osend, orecv, oown, nsend, nrecv, nown,
):
    me = lax.axis_index("exp")
    rows, width = q.shape
    requests, cache = ck.shape[0], ck.shape[2]
    tree = rows // requests
    chunks = width // WIDE
    span = each * LANES
    groups, positions = pk_hbm.shape[0], pk_hbm.shape[1]
    wide_heads = WIDE // HDIM

    def cols(g):
        return pl.ds(pl.multiple_of(g * WIDE, WIDE), WIDE)

    def cache_copy(which, b, g):
        src, dst = ((ck_hbm, ck), (cv_hbm, cv))[which]
        return pltpu.make_async_copy(
            src.at[b, :, cols(g)], dst.at[b, g], csem.at[which, b, g]
        )

    small = [
        pltpu.make_async_copy(src, dst, lsem.at[i])
        for i, (src, dst) in enumerate(((q_hbm, q), (dk_hbm, dk), (dv_hbm, dv), (res_hbm, res)))
    ]
    for copy in small[:3]:
        copy.start()

    def load(g, carry):
        for b in range(requests):
            for which in range(2):
                cache_copy(which, b, g).start()
        return carry

    greet_plane(size)

    row8 = iota((8, LANES), 0)
    marks = jnp.zeros((8, LANES), jnp.int32)
    for b in range(requests):
        marks = jnp.where(row8 == b, group_ref[b], marks)
    group[...] = marks.astype(F32)

    pl.semaphore_wait(pltpu.get_barrier_semaphore(), size - 1)

    more = jnp.int32(0)
    holds_more = jnp.bool_(False)
    for i, device in enumerate(extras):
        more = jnp.where(me == device, i, more)
        holds_more = jnp.logical_or(holds_more, me == device)

    def from_source(s, lanes):
        keys = pl.ds(pl.multiple_of(s * positions, positions), positions)
        return (
            kp.at[:, keys, lanes],
            vp.at[:, keys, lanes],
            qp.at[pl.ds(pl.multiple_of(s * rows, rows), rows), lanes],
        )

    base_lanes, more_lanes = pl.ds(0, span), pl.ds(span, LANES)

    def base_copies(i):
        at = pl.ds(pl.multiple_of(i * span, LANES), span)
        return list(
            zip(
                (pk_hbm.at[:, :, at], pv_hbm.at[:, :, at], q_hbm.at[:, at], group),
                from_source(me, base_lanes) + (gp.at[me],),
            )
        )

    def more_copies(i):
        at = pl.ds((size * each + i) * LANES, LANES)
        return list(
            zip(
                (pk_hbm.at[:, :, at], pv_hbm.at[:, :, at], q_hbm.at[:, at]),
                from_source(me, more_lanes),
            )
        )

    def base_remote(kind, src, dst, i):
        return remote(src, dst, psend.at[kind, i], precv.at[kind, me], "exp", i)

    def more_remote(kind, src, dst, i):
        return remote(src, dst, msend.at[kind, i], mrecv.at[kind, me], "exp", extras[i])

    def send_heads(o, carry):
        i = lax.rem(o + me, size)
        for kind, (src, dst) in enumerate(base_copies(i)):
            base_remote(kind, src, dst, i).start()
        return carry

    lax.fori_loop(1, size, send_heads, 0)
    for i, device in enumerate(extras):
        @pl.when(me != device)
        def _():
            for kind, (src, dst) in enumerate(more_copies(i)):
                more_remote(kind, src, dst, i).start()

        @pl.when(me == device)
        def _():
            for kind, (src, dst) in enumerate(more_copies(i)):
                pltpu.make_async_copy(src, dst, own.at[4 + kind]).start()

    for kind, (src, dst) in enumerate(base_copies(me)):
        pltpu.make_async_copy(src, dst, own.at[kind]).start()
    lax.fori_loop(0, chunks, load, 0)
    small[3].start()

    def column(lines):
        length = lines[0].shape[1]
        same = iota((length, length), 0) == iota((length, length), 1)
        return jnp.concatenate(
            [jnp.sum(jnp.where(same, line, 0), axis=1, keepdims=True) for line in lines], axis=0
        )

    parent = column([parent_ref[b : b + 1] for b in range(requests)])
    at_row, at_col = iota((rows, rows), 0), iota((rows, rows), 1)
    base = at_row // tree * tree
    reached = jnp.logical_or(
        at_row == at_col, jnp.logical_and(at_col - base == parent, parent >= 0)
    )
    for _ in range(max(1, (tree - 1).bit_length())):
        step = flag(reached)
        reached = matmul(step, step) > 0.5
    related = jnp.where(reached, 1.0, 0.0)

    first, second = [
        column([chosen_ref[b, k : k + 1] for b in range(requests)]).astype(F32) for k in range(TOPK)
    ]
    lane = iota((rows, LANES), 1)
    expert = lane.astype(F32)
    named = flag(jnp.logical_or(expert == first, expert == second))
    before = matmul(flag(at_col < at_row), named)
    codes = [
        e * CODE + jnp.sum(jnp.where(expert == e, before, 0.0), axis=1, keepdims=True)
        for e in (first, second)
    ]
    code_columns = jnp.where(lane == 0, codes[0], jnp.where(lane == 1, codes[1], 0.0))
    code_ref[...] = jnp.zeros_like(code_ref)
    code_ref[:, :rows] = matmul_nt(
        flag(iota((8, LANES), 0) == iota((8, LANES), 1)), code_columns.astype(BF16)
    )

    for copy in small[:3]:
        copy.wait()
    path = pick_ref.shape[1]
    picked = column([pick_ref[b : b + 1] for b in range(requests)])
    owner = iota((requests * path, rows), 0) // path
    wanted = flag(iota((requests * path, rows), 1) == picked + owner * tree)
    for kind, ref in enumerate((dk, dv)):
        kept = matmul(wanted, ref[...]).astype(BF16)
        for b in range(requests):
            kept_ref[pl.ds((2 * b + kind) * path, path), :] = kept[b * path : (b + 1) * path]

    head_wide = iota((tree, WIDE), 1) // HDIM
    masks = [flag(head_wide == h) for h in range(wide_heads)]
    stat_lane = iota((tree, LANES), 1)
    seen = [
        jnp.concatenate([related[b * tree : (b + 1) * tree]] * wide_heads, axis=0)
        for b in range(requests)
    ]
    slot_at = iota((wide_heads * tree, cache), 1)
    top_all[...] = jnp.zeros_like(top_all)
    sum_all[...] = jnp.zeros_like(sum_all)

    def local(g, carry):
        for b in range(requests):
            here = slice(b * tree, (b + 1) * tree)
            for which in range(2):
                cache_copy(which, b, g).wait()
            query = q[here, cols(g)] * BF16(SCALE)
            stacked = jnp.concatenate([query * mask for mask in masks], axis=0)
            s_cache = matmul_nt(stacked, ck[b, g])
            s_cache = jnp.where(slot_at < len_ref[b], s_cache, -jnp.inf)
            s_tree = jnp.where(seen[b] > 0.5, matmul_nt(stacked, dk[:, cols(g)]), -jnp.inf)
            top = jnp.maximum(
                jnp.max(s_cache, axis=1, keepdims=True), jnp.max(s_tree, axis=1, keepdims=True)
            )
            w_cache = jnp.exp(s_cache - top)
            w_tree = jnp.exp(s_tree - top)
            total = jnp.sum(w_cache, axis=1, keepdims=True) + jnp.sum(
                w_tree, axis=1, keepdims=True
            )
            mixed = matmul(w_cache.astype(BF16), cv[b, g])
            mixed += matmul(w_tree.astype(BF16), dv[:, cols(g)])
            out = mixed[:tree]
            tops, sums = top_all[here], sum_all[here]
            for h in range(wide_heads):
                part = slice(h * tree, (h + 1) * tree)
                if h:
                    out = jnp.where(head_wide == h, mixed[part], out)
                at = g * wide_heads + h
                tops = jnp.where(stat_lane == at, top[part], tops)
                sums = jnp.where(stat_lane == at, total[part], sums)
            acc[here, cols(g)] = out
            top_all[here] = tops
            sum_all[here] = sums
        return carry

    lax.fori_loop(0, chunks, local, 0)

    for kind, (src, dst) in enumerate(base_copies(me)):
        pltpu.make_async_copy(src, dst, own.at[kind]).wait()

    def arrive(o, carry):
        source = lax.rem(me + o, size)
        for kind, ref in enumerate(from_source(source, base_lanes) + (gp.at[source],)):
            remote(
                ref, ref, psend.at[kind, 0], precv.at[kind, source], "exp", source
            ).wait_recv()
        return carry

    lax.fori_loop(1, size, arrive, 0)

    @pl.when(holds_more)
    def _():
        for i, device in enumerate(extras):
            @pl.when(me == device)
            def _():
                for kind, (src, dst) in enumerate(more_copies(i)):
                    pltpu.make_async_copy(src, dst, own.at[4 + kind]).wait()

        def arrive_more(o, carry):
            source = lax.rem(me + o, size)
            for kind, ref in enumerate(from_source(source, more_lanes)):
                remote(
                    ref, ref, msend.at[kind, 0], mrecv.at[kind, source], "exp", source
                ).wait_recv()
            return carry

        lax.fori_loop(1, size, arrive_more, 0)

    duo = 2 * rows
    pairs = size // 2
    half = iota((duo, LANES), 1) // HDIM
    sides = [flag(half == h) for h in range(PAIR)]
    stat_at = iota((duo, LANES), 1)

    def answer(target):
        at = pl.ds(pl.multiple_of(target * rows, rows), rows)
        return staged.at[at, pl.ds(0, span + LANES)]

    def answer_more(target):
        at = pl.ds(pl.multiple_of(target * rows, rows), rows)
        return staged.at[at, pl.ds(span + LANES, LANES)]

    def answer_remote(target):
        return remote(
            answer(target), landed.at[me], osend.at[target], orecv.at[me], "exp", target
        )

    def answer_more_remote(target):
        return remote(
            answer_more(target), landed_more.at[more], nsend.at[target], nrecv.at[more], "exp",
            target,
        )

    def attend(step, carry):
        c = lax.rem(me // 2 + 1 + step, pairs)
        here = pl.ds(pl.multiple_of(c * duo, duo), duo)
        marks = []
        for s in range(2):
            mark = gp[2 * c + s]
            for b in range(requests):
                marks.append(jnp.broadcast_to(mark[b : b + 1, 0:1], (tree, 1)))
        mark = jnp.concatenate(marks * PAIR, axis=0)
        stats[...] = jnp.zeros_like(stats)

        def one(j, number, to):
            at = slice(j * LANES, (j + 1) * LANES)
            query = qp[here, at] * BF16(SCALE)
            stacked = jnp.concatenate([query * side for side in sides], axis=0)
            scores = matmul_nt(stacked, kp[0, :, at])
            for g in range(1, groups):
                scores = jnp.where(mark == g, matmul_nt(stacked, kp[g, :, at]), scores)
            top = jnp.max(scores, axis=1, keepdims=True).astype(BF16).astype(F32)
            weights = jnp.exp(scores - top)
            total = jnp.sum(weights, axis=1, keepdims=True)
            weights = weights.astype(BF16)
            mixed = None
            for g in range(groups):
                part = matmul(
                    jnp.where(mark == g, weights, jnp.zeros_like(weights)), vp[g, :, at]
                )
                mixed = part if mixed is None else mixed + part
            staged[here, to : to + LANES] = jnp.where(
                half == 0, mixed[:duo], mixed[duo:]
            ).astype(BF16)
            high = total.astype(BF16).astype(F32)
            got = stats[...]
            for h in range(PAIR):
                part = slice(h * duo, (h + 1) * duo)
                head = number * PAIR + h
                got = jnp.where(stat_at == head, top[part], got)
                got = jnp.where(stat_at == head + HEADS, high[part], got)
                got = jnp.where(stat_at == head + 2 * HEADS, (total - high)[part], got)
            stats[...] = got

        for j in range(each):
            one(j, me * each + j, j * LANES)

        @pl.when(holds_more)
        def _():
            one(each, size * each + more, span + LANES)

        staged[here, span : span + LANES] = stats[...].astype(BF16)
        for s in range(2):
            target = 2 * c + s

            @pl.when(target != me)
            def _():
                answer_remote(target).start()

                @pl.when(holds_more)
                def _():
                    answer_more_remote(target).start()

            @pl.when(target == me)
            def _():
                pltpu.make_async_copy(answer(me), landed.at[me], oown.at[0]).start()

                @pl.when(holds_more)
                def _():
                    pltpu.make_async_copy(
                        answer_more(me), landed_more.at[more], nown.at[0]
                    ).start()

        return carry

    lax.fori_loop(0, pairs, attend, 0)
    pltpu.make_async_copy(answer(me), landed.at[me], oown.at[0]).wait()

    @pl.when(holds_more)
    def _():
        pltpu.make_async_copy(answer_more(me), landed_more.at[more], nown.at[0]).wait()

    small[3].wait()

    def answered(o, carry):
        source = lax.rem(me + o, size)
        remote(
            landed.at[source], landed.at[source], osend.at[0], orecv.at[source], "exp", source
        ).wait_recv()
        return carry

    lax.fori_loop(1, size, answered, 0)
    for i, device in enumerate(extras):
        @pl.when(me != device)
        def _():
            remote(
                landed_more.at[i], landed_more.at[i], nsend.at[0], nrecv.at[i], "exp", device
            ).wait_recv()

    tops = landed[0, :, span:].astype(F32)
    for i in range(1, size):
        tops += landed[i, :, span:].astype(F32)
    theirs = pltpu.roll(tops, LANES - HEADS, 1) + pltpu.roll(tops, LANES - 2 * HEADS, 1)
    used = lane < HEADS
    ours = jnp.where(used, sum_all[...], 1.0)
    theirs = jnp.where(used, theirs, 1.0)
    tops = jnp.where(used, tops, 0.0)
    top = jnp.maximum(top_all[...], tops)
    own_scale = jnp.exp(top_all[...] - top)
    far_scale = jnp.exp(tops - top)
    total = own_scale * ours + far_scale * theirs
    own_scale, far_scale = own_scale / total, far_scale / total
    squares = jnp.zeros((rows, 1), F32)
    left = lane < HDIM
    for block in range(width // LANES):
        at = slice(block * LANES, (block + 1) * LANES)
        i, j = divmod(block, each)
        a = PAIR * block
        if i < size:
            far = landed[i, :, j * LANES : (j + 1) * LANES]
        else:
            far = landed_more[block - size * each]
        out = acc[:, at] * jnp.where(left, own_scale[:, a : a + 1], own_scale[:, a + 1 : a + 2])
        out += far.astype(F32) * jnp.where(
            left, far_scale[:, a : a + 1], far_scale[:, a + 1 : a + 2]
        )
        attended = out.astype(BF16)
        att_ref[:, at] = attended
        stream = (res[:, at].astype(F32) + attended.astype(F32)).astype(BF16)
        stream_ref[:, at] = stream
        stream = stream.astype(F32)
        squares += jnp.sum(stream * stream, axis=1, keepdims=True)
    factor = lax.rsqrt(squares / width + EPSILON)
    normed_ref[...] = (stream_ref[...].astype(F32) * factor * gain_ref[...].reshape(1, width)).astype(BF16)

    def sent(o, carry):
        i = lax.rem(me + o, size)
        for kind, (src, dst) in enumerate(base_copies(i)):
            base_remote(kind, src, dst, i).wait_send()
        answer_remote(i).wait_send()

        @pl.when(holds_more)
        def _():
            answer_more_remote(i).wait_send()

        return carry

    lax.fori_loop(1, size, sent, 0)
    for i, device in enumerate(extras):
        @pl.when(me != device)
        def _():
            for kind, (src, dst) in enumerate(more_copies(i)):
                more_remote(kind, src, dst, i).wait_send()


def attention(
    parents, chosen, picks, lengths, group_ids, gain, queries, draft_keys, draft_values, residual, cache_keys, cache_values,
    prompt_keys, prompt_values, size,
):
    requests, tree, width = queries.shape
    rows, cache = requests * tree, cache_keys.shape[1]
    groups, positions = prompt_keys.shape[:2]
    each, extras = share_of(size, width // LANES)
    count, span, chunks = len(extras), each * LANES, width // WIDE
    path = picks.shape[1]
    flat = lambda a: a.reshape(rows, width)
    vmem = pl.BlockSpec(memory_space=pltpu.VMEM)
    hbm = pl.BlockSpec(memory_space=pltpu.HBM)
    dma = pltpu.SemaphoreType.DMA
    row_block = jax.ShapeDtypeStruct((rows, width), BF16)
    return pl.pallas_call(
        functools.partial(attention_kernel, size, each, extras),
        out_shape=[
            row_block, row_block, row_block,
            jax.ShapeDtypeStruct((requests * 2 * path, width), BF16),
            jax.ShapeDtypeStruct((8, LANES), F32),
        ],
        in_specs=[pl.BlockSpec(memory_space=pltpu.SMEM)] * 2 + [vmem] * 4 + [hbm] * 8,
        out_specs=[vmem] * 5,
        scratch_shapes=[
            pltpu.VMEM((requests, chunks, cache, WIDE), BF16),
            pltpu.VMEM((requests, chunks, cache, WIDE), BF16),
            pltpu.VMEM((rows, width), BF16),
            pltpu.VMEM((rows, width), BF16),
            pltpu.VMEM((rows, width), BF16),
            pltpu.VMEM((rows, width), BF16),
            pltpu.VMEM((8, LANES), F32),
            pltpu.VMEM((rows, width), F32),
            pltpu.VMEM((rows, LANES), F32),
            pltpu.VMEM((rows, LANES), F32),
            pltpu.VMEM((groups, size * positions, span + LANES), BF16),
            pltpu.VMEM((groups, size * positions, span + LANES), BF16),
            pltpu.VMEM((size * rows, span + LANES), BF16),
            pltpu.VMEM((size, 8, LANES), F32),
            pltpu.VMEM((size * rows, span + 2 * LANES), BF16),
            pltpu.VMEM((size, rows, span + LANES), BF16),
            pltpu.VMEM((count, rows, LANES), BF16),
            pltpu.VMEM((2 * rows, LANES), F32),
            dma((2, requests, chunks)), dma((4,)), dma((4, size)), dma((4, size)), dma((7,)),
            dma((3, count)), dma((3, size)), dma((size,)), dma((size,)), dma((1,)),
            dma((size,)), dma((count,)), dma((1,)),
        ],
        compiler_params=pltpu.CompilerParams(
            collective_id=0, has_side_effects=True, vmem_limit_bytes=60 * 1024 * 1024
        ),
        name="attention",
    )(
        lengths, group_ids, parents, chosen, picks, gain, flat(queries), flat(draft_keys), flat(draft_values), flat(residual),
        cache_keys, cache_values, prompt_keys, prompt_values,
    )


def expert_kernel(
    depth, size,
    normed_hbm, stream_hbm, code_hbm, router_ref, wg_hbm, wu_hbm, wd_hbm,
    out_ref,
    wg, wu, wd, stream, held, codes, staged, spilled, x, x_spill, hidden, y, y_spill, land, land_spill,
    mix, mix_spill, sums, part, passed,
    wsem, zsend, zrecv, dsend, drecv, ysend, yrecv, rsend, rrecv,
):
    z, e = lax.axis_index("req"), lax.axis_index("exp")
    rows, width = normed_hbm.shape
    units = wg.shape[0]
    holders = size // EXPERTS
    spread = SPILL * depth
    split = MAIN // spread
    piece = width // split
    main = size * MAIN
    low = z < depth // 2

    weights = [
        pltpu.make_async_copy(src, dst, wsem.at[i])
        for i, (src, dst) in enumerate(((wg_hbm, wg), (wu_hbm, wu), (wd_hbm, wd)))
    ]
    inputs = [
        pltpu.make_async_copy(src, dst, wsem.at[3 + i])
        for i, (src, dst) in enumerate(
            ((normed_hbm, held.at[z]), (code_hbm, codes.at[z]), (stream_hbm, stream))
        )
    ]
    for copy in inputs:
        copy.start()

    barrier = pltpu.get_barrier_semaphore()
    greet_plane(size)

    @pl.when(z < depth - 1)
    def _():
        pl.semaphore_signal(barrier, inc=1, device_id={"req": z + 1}, device_id_type=MESH)

    @pl.when(z > 0)
    def _():
        pl.semaphore_signal(barrier, inc=1, device_id={"req": z - 1}, device_id_type=MESH)

    pl.semaphore_wait(
        barrier, size - 1 + jnp.where(z > 0, 1, 0) + jnp.where(z < depth - 1, 1, 0)
    )

    def order(p):
        near = jnp.where(low, z, depth - 1 - z)
        step = (p + 1) // 2
        at = jnp.where(p > 2 * near, p, jnp.where(p % 2 == 1, near - step, near + step))
        return jnp.where(low, at, depth - 1 - at)

    def place(k):
        near = jnp.where(low, z, depth - 1 - z)
        at = jnp.where(low, k, depth - 1 - k)
        gap = at - near
        return jnp.where(
            gap == 0, 0, jnp.where(gap < 0, -2 * gap - 1, jnp.where(gap <= near, 2 * gap, at))
        )

    def along(k, way):
        target = z + 1 if way == 0 else z - 1
        return [
            remote(ref.at[k], ref.at[k], zsend.at[kind, way, k], zrecv.at[kind, k], "req", target)
            for kind, ref in enumerate((codes, held))
        ]

    def passes(k, way):
        if way == 0:
            return jnp.logical_and(k <= z, z < depth - 1)
        return jnp.logical_and(k >= z, z > 0)

    def pass_on(k):
        for way in range(2):
            @pl.when(passes(k, way))
            def _():
                for copy in along(k, way):
                    copy.start()

    def block(p, target):
        return pl.ds(pl.multiple_of((p * size + target) * MAIN, MAIN), MAIN)

    def spot(target):
        return pl.ds(pl.multiple_of(target * MAIN, MAIN), MAIN)

    wanted = iota((main, rows), 0)
    wanted_code = ((wanted // MAIN) // holders * CODE + wanted % MAIN).astype(F32)

    def stage(p, carry):
        k = order(p)

        @pl.when(p > 0)
        def _():
            for copy in along(k, 0):
                copy.wait_recv()

        pass_on(k)
        code = codes[k]
        pick = flag(
            jnp.logical_or(code[0:1, :rows] == wanted_code, code[1:2, :rows] == wanted_code)
        )
        here = pl.ds(pl.multiple_of(p * main, main), main)
        step = 3 * WIDE if width % (3 * WIDE) == 0 else WIDE
        for c in range(0, width, step):
            staged[here, c : c + step] = matmul(pick, held[k, :, c : c + step]).astype(BF16)

        def send(o, carry):
            target = lax.rem(e + o, size)
            remote(
                staged.at[block(p, target)], x.at[block(p, e)], dsend.at[p, o], drecv.at[p, e],
                "exp", target,
            ).start()
            return carry

        lax.fori_loop(1, size, send, 0)
        x[block(p, e), :] = staged[block(p, e), :]
        return carry

    def all_landed(p, ref, sem, at):
        def wait(o, carry):
            source = lax.rem(e + o, size)
            remote(
                ref.at[at(source)], ref.at[at(source)], dsend.at[0, 0], sem.at[p, source], "exp",
                source,
            ).wait_recv()
            return carry

        lax.fori_loop(1, size, wait, 0)

    def parts_of(start, count):
        return [
            (at, min(2 * WIDE, start + count - at))
            for at in range(start, start + count, 2 * WIDE)
        ]

    def up(start, count):
        here = slice(start, start + count)
        for at in range(0, units, 2 * WIDE):
            unit = slice(at, min(at + 2 * WIDE, units))
            gate = matmul_nt(x[here, :], wg[unit, :])
            value = matmul_nt(x[here, :], wu[unit, :])
            hidden[0:count, unit] = (gate / (1.0 + jnp.exp(-gate)) * value).astype(BF16)

    def down(start, count):
        for at in range(0, width, WIDE):
            unit = slice(at, at + WIDE)
            y[start : start + count, unit] = matmul(hidden[0:count, :], wd[:, unit]).astype(BF16)

    def give_back(p):
        def send(o, carry):
            target = lax.rem(e + o, size)
            remote(
                y.at[block(p, target)], land.at[block(p, e)], ysend.at[p, o], yrecv.at[p, e],
                "exp", target,
            ).start()
            return carry

        lax.fori_loop(1, size, send, 0)
        land[block(p, e), :] = y[block(p, e), :]

    for copy in inputs:
        copy.wait()
    for copy in weights:
        copy.start()
    lax.fori_loop(0, depth - 1, stage, 0)
    for copy in weights:
        copy.wait()
    near = depth // 2
    for p in range(near):
        all_landed(p, x, drecv, lambda s, p=p: block(p, s))
    first = parts_of(0, near * main)
    for at in first[:-1]:
        up(*at)
        down(*at)
    up(*first[-1])
    stage(depth - 1, 0)

    slot = iota((main, rows), 0)
    slot_row = slot % MAIN
    slot_side, slot_item = slot_row // spread, slot_row % spread
    spill_code = ((slot // MAIN) // holders * CODE + MAIN + slot_item % SPILL).astype(F32)
    spill_sum = None
    for k in range(depth):
        code = codes[k]
        match = jnp.logical_and(
            jnp.logical_or(code[0:1, :rows] == spill_code, code[1:2, :rows] == spill_code),
            slot_item // SPILL == k,
        )
        for side in range(split):
            picked = matmul(
                flag(jnp.logical_and(match, slot_side == side)),
                held[k, :, side * piece : (side + 1) * piece],
            )
            spill_sum = picked if spill_sum is None else spill_sum + picked
    spilled[...] = spill_sum.astype(BF16)

    def send_spill(o, carry):
        target = lax.rem(e + o, size)
        remote(
            spilled.at[spot(target)], x_spill.at[spot(e)], dsend.at[depth, o], drecv.at[depth, e],
            "exp", target,
        ).start()
        return carry

    lax.fori_loop(1, size, send_spill, 0)
    x_spill[spot(e), :] = spilled[spot(e), :]
    down(*first[-1])

    eye = flag(iota((rows, rows), 0) == iota((rows, rows), 1))
    mixed_slot = iota((rows, main), 1)
    mixed_code = ((mixed_slot // MAIN) // holders * CODE + mixed_slot % MAIN).astype(F32)
    mixed_row = mixed_slot % MAIN
    mixed_side, mixed_item = mixed_row // spread, mixed_row % spread
    mixed_spill = ((mixed_slot // MAIN) // holders * CODE + MAIN + mixed_item % SPILL).astype(F32)

    def weigh(k, carry):
        columns = matmul_nt(eye, codes[k][:, :rows].astype(BF16))
        first, second = columns[:, 0:1], columns[:, 1:2]
        logits = matmul_nt(held[k], router_ref[...])
        choice = (iota(logits.shape, 1) * CODE).astype(F32)

        def chosen(code):
            hit = jnp.logical_and(code >= choice, code < choice + CODE)
            return jnp.sum(jnp.where(hit, logits, 0.0), axis=1, keepdims=True)

        gate = 1.0 / (1.0 + jnp.exp(chosen(second) - chosen(first)))
        mix[k] = (
            jnp.where(first == mixed_code, gate, 0.0)
            + jnp.where(second == mixed_code, 1.0 - gate, 0.0)
        ).astype(BF16)
        spill = jnp.where(first == mixed_spill, gate, 0.0) + jnp.where(
            second == mixed_spill, 1.0 - gate, 0.0
        )
        spill = jnp.where(mixed_item // SPILL == k, spill, 0.0)
        for side in range(split):
            mix_spill[k, side] = jnp.where(mixed_side == side, spill, 0.0).astype(BF16)
        return carry

    lax.fori_loop(0, depth, weigh, 0)

    for p in range(near, depth - 1):
        all_landed(p, x, drecv, lambda s, p=p: block(p, s))
    for at in parts_of(near * main, (depth - 1 - near) * main):
        up(*at)
        down(*at)
    all_landed(depth - 1, x, drecv, lambda s: block(depth - 1, s))
    all_landed(depth, x_spill, drecv, spot)
    for p in range(1, near):
        give_back(p)
    few = size * spread
    few_row, few_col = iota((few, main), 0), iota((few, main), 1)
    for side in range(split):
        unpack = flag(few_col == few_row // spread * MAIN + side * spread + few_row % spread)
        x[depth * main :, side * piece : (side + 1) * piece] = matmul(
            unpack, x_spill[...]
        ).astype(BF16)
    for at in parts_of((depth - 1) * main, main + few):
        up(*at)
        down(*at)
    few_row, few_col = iota((main, few), 1), iota((main, few), 0)
    packed = None
    for side in range(split):
        pack = flag(few_col == few_row // spread * MAIN + side * spread + few_row % spread)
        moved = matmul(pack, y[depth * main :, side * piece : (side + 1) * piece])
        packed = moved if packed is None else packed + moved
    y_spill[...] = packed.astype(BF16)

    def return_spill(o, carry):
        target = lax.rem(e + o, size)
        remote(
            y_spill.at[spot(target)], land_spill.at[spot(e)], ysend.at[depth, o],
            yrecv.at[depth, e], "exp", target,
        ).start()
        return carry

    lax.fori_loop(1, size, return_spill, 0)
    land_spill[spot(e), :] = y_spill[spot(e), :]
    give_back(depth - 1)

    def relay(h, side, way):
        target = z + 1 if way == 0 else z - 1
        at = jnp.where(jnp.logical_and(way == 1, target == h), depth, h)
        return remote(
            part.at[h, side], passed.at[at, side], rsend.at[h, side], rrecv.at[at, side], "req",
            target,
        )

    def arrived(at, side):
        remote(
            passed.at[at, side], passed.at[at, side], rsend.at[0, 0], rrecv.at[at, side], "req",
            jnp.where(z > 0, z - 1, z + 1),
        ).wait_recv()

    def combine(h, side):
        p = place(h)
        here = pl.ds(pl.multiple_of(p * main, main), main)
        at = slice(side * piece, (side + 1) * piece)
        return matmul(mix[h], land[here, at]) + matmul(mix_spill[h, side], land_spill[...])

    all_landed(depth, land_spill, yrecv, spot)
    rank = 2 * jnp.minimum(z, depth - 1 - z) + 1

    def reduce(j, carry):
        i = j + jnp.where(j >= rank, 1, 0)
        past = jnp.where(j >= 2, 1, 0)
        i = jnp.where(z == 0, jnp.where(j == 0, 2, j + past), i)
        last = jnp.where(j == 0, 3, j - 1 + past + jnp.where(j >= 3, 1, 0))
        i = jnp.where(z == depth - 1, last, i)
        swap = jnp.logical_and(low, z > 0)

        @pl.when(j <= depth - 1 - near)
        def _():
            give_back(jnp.where(j == depth - 1 - near, 0, depth - 2 - j))

        h = jnp.where(i % 2 == 0, i // 2, depth - 1 - i // 2)
        h = jnp.where(swap, depth - 1 - h, h)
        p = place(h)
        all_landed(p, land, yrecv, lambda s: block(p, s))
        rising = h > z
        joined = jnp.logical_or(
            jnp.logical_and(rising, z > 0),
            jnp.logical_and(jnp.logical_not(rising), z < depth - 1),
        )
        for side in range(split):
            sums[...] = combine(h, side)

            @pl.when(joined)
            def _():
                arrived(h, side)
                sums[...] += passed[h, side].astype(F32)

            part[h, side] = sums[...].astype(BF16)

            @pl.when(rising)
            def _():
                relay(h, side, 0).start()

            @pl.when(jnp.logical_not(rising))
            def _():
                relay(h, side, 1).start()

        return carry

    lax.fori_loop(0, depth - 1, reduce, 0)
    all_landed(0, land, yrecv, lambda s: block(0, s))
    for side in range(split):
        at = slice(side * piece, (side + 1) * piece)
        sums[...] = combine(z, side) + stream[:, at].astype(F32)

        @pl.when(z > 0)
        def _():
            arrived(z, side)
            sums[...] += passed[z, side].astype(F32)

        @pl.when(z < depth - 1)
        def _():
            arrived(depth, side)
            sums[...] += passed[depth, side].astype(F32)

        out_ref[:, at] = sums[...].astype(BF16)

    def finish(k, carry):
        for way in range(2):
            @pl.when(passes(k, way))
            def _():
                for copy in along(k, way):
                    copy.wait_send()

        for side in range(split):
            @pl.when(k > z)
            def _():
                relay(k, side, 0).wait_send()

            @pl.when(k < z)
            def _():
                relay(k, side, 1).wait_send()

        def lane_done(o, carry):
            target = lax.rem(e + o, size)
            remote(
                staged.at[block(k, target)], x.at[block(k, e)], dsend.at[k, o], drecv.at[k, e],
                "exp", target,
            ).wait_send()
            remote(
                y.at[block(k, target)], land.at[block(k, e)], ysend.at[k, o], yrecv.at[k, e],
                "exp", target,
            ).wait_send()
            return carry

        lax.fori_loop(1, size, lane_done, 0)
        return carry

    lax.fori_loop(0, depth, finish, 0)

    def spill_done(o, carry):
        target = lax.rem(e + o, size)
        remote(
            spilled.at[spot(target)], x_spill.at[spot(e)], dsend.at[depth, o], drecv.at[depth, e],
            "exp", target,
        ).wait_send()
        remote(
            y_spill.at[spot(target)], land_spill.at[spot(e)], ysend.at[depth, o],
            yrecv.at[depth, e], "exp", target,
        ).wait_send()
        return carry

    lax.fori_loop(1, size, spill_done, 0)


def expert_layer(normed, stream, code, router, w_gate, w_up, w_down, depth, size):
    rows, width = normed.shape
    units = w_gate.shape[0]
    spread = SPILL * depth
    split = MAIN // spread
    piece = width // split
    main = size * MAIN
    total = depth * main + size * spread
    most = min(2 * WIDE, max(depth // 2 * main, main + size * spread))
    dma = pltpu.SemaphoreType.DMA
    vmem = pl.BlockSpec(memory_space=pltpu.VMEM)
    hbm = pl.BlockSpec(memory_space=pltpu.HBM)
    return pl.pallas_call(
        functools.partial(expert_kernel, depth, size),
        out_shape=jax.ShapeDtypeStruct((rows, width), BF16),
        in_specs=[hbm] * 3 + [vmem] + [hbm] * 3,
        out_specs=vmem,
        scratch_shapes=[
            pltpu.VMEM((units, width), BF16),
            pltpu.VMEM((units, width), BF16),
            pltpu.VMEM((units, width), BF16),
            pltpu.VMEM((rows, width), BF16),
            pltpu.VMEM((depth, rows, width), BF16),
            pltpu.VMEM((depth, 8, LANES), F32),
            pltpu.VMEM((depth * main, width), BF16),
            pltpu.VMEM((main, piece), BF16),
            pltpu.VMEM((total, width), BF16),
            pltpu.VMEM((main, piece), BF16),
            pltpu.VMEM((most, units), BF16),
            pltpu.VMEM((total, width), BF16),
            pltpu.VMEM((main, piece), BF16),
            pltpu.VMEM((depth * main, width), BF16),
            pltpu.VMEM((main, piece), BF16),
            pltpu.VMEM((depth, rows, main), BF16),
            pltpu.VMEM((depth, split, rows, main), BF16),
            pltpu.VMEM((rows, piece), F32),
            pltpu.VMEM((depth, split, rows, piece), BF16),
            pltpu.VMEM((depth + 1, split, rows, piece), BF16),
            dma((6,)), dma((2, 2, depth)), dma((2, depth)),
            dma((depth + 1, size)), dma((depth + 1, size)),
            dma((depth + 1, size)), dma((depth + 1, size)),
            dma((depth, split)), dma((depth + 1, split)),
        ],
        compiler_params=pltpu.CompilerParams(
            collective_id=1, has_side_effects=True, vmem_limit_bytes=60 * 1024 * 1024
        ),
        name="experts",
    )(normed, stream, code, router, w_gate, w_up, w_down)


def on_device(
    queries,
    draft_keys,
    draft_values,
    tree_parents,
    cache_keys,
    cache_values,
    cache_lengths,
    prompt_keys,
    prompt_values,
    group_ids,
    residual,
    norm_gain,
    router,
    w_gate,
    w_up,
    w_down,
    expert_ids,
    accepted_rows,
):
    requests, tree, width = queries.shape
    rows = requests * tree
    depth, size = lax.axis_size("req"), lax.axis_size("exp")

    attended, stream, normed, kept, code = attention(
        tree_parents, jnp.swapaxes(expert_ids, 1, 2), accepted_rows, cache_lengths, group_ids,
        norm_gain, queries, draft_keys, draft_values,
        residual, cache_keys, cache_values, prompt_keys, prompt_values, size,
    )
    layer_out = expert_layer(
        normed, stream, code, router.T, w_gate[0].T, w_up[0].T, w_down[0], depth, size
    )
    return (
        attended.reshape(requests, tree, width),
        layer_out.reshape(requests, tree, width),
        kept.reshape(requests, 2, accepted_rows.shape[1], width),
    )


def solution(mesh):
    both = ("req", "exp")
    return jax.shard_map(
        on_device,
        mesh=mesh,
        in_specs=(
            P(both, None, None),
            P(both, None, None),
            P(both, None, None),
            P(both, None),
            P(both, None, None),
            P(both, None, None),
            P(both),
            P("req", "exp", None),
            P("req", "exp", None),
            P(both),
            P(both, None, None),
            P(),
            P(),
            P("exp", None, "req"),
            P("exp", None, "req"),
            P("exp", "req", None),
            P(both, None, None),
            P(both, None),
        ),
        out_specs=(
            P(both, None, None),
            P(both, None, None),
            P(both, None, None, None),
        ),
        check_vma=False,
    )
```

```python
import functools

import jax
import jax.numpy as jnp
from jax import lax
from jax.experimental import pallas as pl
from jax.experimental.pallas import tpu as pltpu
from jax.sharding import PartitionSpec as P

HEADS = 36
HDIM = 64
EXPERTS = 8
TOPK = 2
LANES = 128
PAIR = LANES // HDIM
WIDE = 256
MAIN = 16
SPILL = 2
PIECE = 384
HALVES = 2
CODE = 32
EPSILON = 1e-05
SCALE = HDIM ** (-0.5)
NT = (((1,), (1,)), ((), ()))
F32 = jnp.float32
BF16 = jnp.bfloat16
MESH = pl.DeviceIdType.MESH


def remote(src, dst, send, recv, axis, target):
    return pltpu.make_async_remote_copy(
        src_ref=src, dst_ref=dst, send_sem=send, recv_sem=recv, device_id={axis: target},
        device_id_type=MESH,
    )


def iota(shape, dim):
    return lax.broadcasted_iota(jnp.int32, shape, dim)


def flag(condition):
    return jnp.where(condition, 1.0, 0.0).astype(BF16)


def matmul(a, b):
    return jnp.dot(a, b, preferred_element_type=F32)


def matmul_nt(a, b):
    return lax.dot_general(a, b, NT, preferred_element_type=F32)


def greet_plane(size):
    e = lax.axis_index("exp")
    barrier = pltpu.get_barrier_semaphore()
    for step in range(1, size):
        pl.semaphore_signal(
            barrier, inc=1, device_id={"exp": lax.rem(e + step, size)}, device_id_type=MESH
        )


def share_of(size, blocks):
    each = blocks // size
    more = blocks - each * size
    return each, [i * (size - 1) // max(more - 1, 1) for i in range(more)]


def attention_kernel(
    size, each, extras,
    len_ref, group_ref, parent_ref, chosen_ref, pick_ref, gain_ref, q_hbm, dk_hbm, dv_hbm, res_hbm, ck_hbm, cv_hbm, pk_hbm, pv_hbm,
    att_ref, stream_ref, normed_ref, kept_ref, code_ref,
    ck, cv, q, dk, dv, res, group, acc, top_all, sum_all, kp, vp, qp, gp, staged, landed, landed_more,
    stats, csem, lsem, psend, precv, own, msend, mrecv, osend, orecv, oown, nsend, nrecv, nown,
):
    me = lax.axis_index("exp")
    rows, width = q.shape
    requests, cache = ck.shape[0], ck.shape[2]
    tree = rows // requests
    chunks = width // WIDE
    span = each * LANES
    groups, positions = pk_hbm.shape[0], pk_hbm.shape[1]
    wide_heads = WIDE // HDIM

    def cols(g):
        return pl.ds(pl.multiple_of(g * WIDE, WIDE), WIDE)

    def cache_copy(which, b, g):
        src, dst = ((ck_hbm, ck), (cv_hbm, cv))[which]
        return pltpu.make_async_copy(
            src.at[b, :, cols(g)], dst.at[b, g], csem.at[which, b, g]
        )

    small = [
        pltpu.make_async_copy(src, dst, lsem.at[i])
        for i, (src, dst) in enumerate(((q_hbm, q), (dk_hbm, dk), (dv_hbm, dv), (res_hbm, res)))
    ]
    for copy in small[:3]:
        copy.start()

    def load(g, carry):
        for b in range(requests):
            for which in range(2):
                cache_copy(which, b, g).start()
        return carry

    greet_plane(size)

    row8 = iota((8, LANES), 0)
    marks = jnp.zeros((8, LANES), jnp.int32)
    for b in range(requests):
        marks = jnp.where(row8 == b, group_ref[b], marks)
    group[...] = marks.astype(F32)

    pl.semaphore_wait(pltpu.get_barrier_semaphore(), size - 1)

    more = jnp.int32(0)
    holds_more = jnp.bool_(False)
    for i, device in enumerate(extras):
        more = jnp.where(me == device, i, more)
        holds_more = jnp.logical_or(holds_more, me == device)

    def from_source(s, lanes):
        keys = pl.ds(pl.multiple_of(s * positions, positions), positions)
        return (
            kp.at[:, keys, lanes],
            vp.at[:, keys, lanes],
            qp.at[pl.ds(pl.multiple_of(s * rows, rows), rows), lanes],
        )

    base_lanes, more_lanes = pl.ds(0, span), pl.ds(span, LANES)

    def base_copies(i):
        at = pl.ds(pl.multiple_of(i * span, LANES), span)
        return list(
            zip(
                (pk_hbm.at[:, :, at], pv_hbm.at[:, :, at], q_hbm.at[:, at], group),
                from_source(me, base_lanes) + (gp.at[me],),
            )
        )

    def more_copies(i):
        at = pl.ds((size * each + i) * LANES, LANES)
        return list(
            zip(
                (pk_hbm.at[:, :, at], pv_hbm.at[:, :, at], q_hbm.at[:, at]),
                from_source(me, more_lanes),
            )
        )

    def base_remote(kind, src, dst, i):
        return remote(src, dst, psend.at[kind, i], precv.at[kind, me], "exp", i)

    def more_remote(kind, src, dst, i):
        return remote(src, dst, msend.at[kind, i], mrecv.at[kind, me], "exp", extras[i])

    def send_heads(o, carry):
        i = lax.rem(o + me, size)
        for kind, (src, dst) in enumerate(base_copies(i)):
            base_remote(kind, src, dst, i).start()
        return carry

    lax.fori_loop(1, size, send_heads, 0)
    for i, device in enumerate(extras):
        @pl.when(me != device)
        def _():
            for kind, (src, dst) in enumerate(more_copies(i)):
                more_remote(kind, src, dst, i).start()

        @pl.when(me == device)
        def _():
            for kind, (src, dst) in enumerate(more_copies(i)):
                pltpu.make_async_copy(src, dst, own.at[4 + kind]).start()

    for kind, (src, dst) in enumerate(base_copies(me)):
        pltpu.make_async_copy(src, dst, own.at[kind]).start()
    lax.fori_loop(0, chunks, load, 0)
    small[3].start()

    def column(lines):
        length = lines[0].shape[1]
        same = iota((length, length), 0) == iota((length, length), 1)
        return jnp.concatenate(
            [jnp.sum(jnp.where(same, line, 0), axis=1, keepdims=True) for line in lines], axis=0
        )

    parent = column([parent_ref[b : b + 1] for b in range(requests)])
    at_row, at_col = iota((rows, rows), 0), iota((rows, rows), 1)
    base = at_row // tree * tree
    reached = jnp.logical_or(
        at_row == at_col, jnp.logical_and(at_col - base == parent, parent >= 0)
    )
    for _ in range(max(1, (tree - 1).bit_length())):
        step = flag(reached)
        reached = matmul(step, step) > 0.5
    related = jnp.where(reached, 1.0, 0.0)

    first, second = [
        column([chosen_ref[b, k : k + 1] for b in range(requests)]).astype(F32) for k in range(TOPK)
    ]
    lane = iota((rows, LANES), 1)
    expert = lane.astype(F32)
    named = flag(jnp.logical_or(expert == first, expert == second))
    before = matmul(flag(at_col < at_row), named)
    codes = [
        e * CODE + jnp.sum(jnp.where(expert == e, before, 0.0), axis=1, keepdims=True)
        for e in (first, second)
    ]
    code_columns = jnp.where(lane == 0, codes[0], jnp.where(lane == 1, codes[1], 0.0))
    code_ref[...] = jnp.zeros_like(code_ref)
    code_ref[:, :rows] = matmul_nt(
        flag(iota((8, LANES), 0) == iota((8, LANES), 1)), code_columns.astype(BF16)
    )

    for copy in small[:3]:
        copy.wait()
    path = pick_ref.shape[1]
    picked = column([pick_ref[b : b + 1] for b in range(requests)])
    owner = iota((requests * path, rows), 0) // path
    wanted = flag(iota((requests * path, rows), 1) == picked + owner * tree)
    for kind, ref in enumerate((dk, dv)):
        kept = matmul(wanted, ref[...]).astype(BF16)
        for b in range(requests):
            kept_ref[pl.ds((2 * b + kind) * path, path), :] = kept[b * path : (b + 1) * path]

    head_wide = iota((tree, WIDE), 1) // HDIM
    masks = [flag(head_wide == h) for h in range(wide_heads)]
    stat_lane = iota((tree, LANES), 1)
    seen = [
        jnp.concatenate([related[b * tree : (b + 1) * tree]] * wide_heads, axis=0)
        for b in range(requests)
    ]
    slot_at = iota((wide_heads * tree, cache), 1)
    top_all[...] = jnp.zeros_like(top_all)
    sum_all[...] = jnp.zeros_like(sum_all)

    def local(g, carry):
        for b in range(requests):
            here = slice(b * tree, (b + 1) * tree)
            for which in range(2):
                cache_copy(which, b, g).wait()
            query = q[here, cols(g)] * BF16(SCALE)
            stacked = jnp.concatenate([query * mask for mask in masks], axis=0)
            s_cache = matmul_nt(stacked, ck[b, g])
            s_cache = jnp.where(slot_at < len_ref[b], s_cache, -jnp.inf)
            s_tree = jnp.where(seen[b] > 0.5, matmul_nt(stacked, dk[:, cols(g)]), -jnp.inf)
            top = jnp.maximum(
                jnp.max(s_cache, axis=1, keepdims=True), jnp.max(s_tree, axis=1, keepdims=True)
            )
            w_cache = jnp.exp(s_cache - top)
            w_tree = jnp.exp(s_tree - top)
            total = jnp.sum(w_cache, axis=1, keepdims=True) + jnp.sum(
                w_tree, axis=1, keepdims=True
            )
            mixed = matmul(w_cache.astype(BF16), cv[b, g])
            mixed += matmul(w_tree.astype(BF16), dv[:, cols(g)])
            out = mixed[:tree]
            tops, sums = top_all[here], sum_all[here]
            for h in range(wide_heads):
                part = slice(h * tree, (h + 1) * tree)
                if h:
                    out = jnp.where(head_wide == h, mixed[part], out)
                at = g * wide_heads + h
                tops = jnp.where(stat_lane == at, top[part], tops)
                sums = jnp.where(stat_lane == at, total[part], sums)
            acc[here, cols(g)] = out
            top_all[here] = tops
            sum_all[here] = sums
        return carry

    lax.fori_loop(0, chunks, local, 0)

    for kind, (src, dst) in enumerate(base_copies(me)):
        pltpu.make_async_copy(src, dst, own.at[kind]).wait()

    def arrive(o, carry):
        source = lax.rem(me + o, size)
        for kind, ref in enumerate(from_source(source, base_lanes) + (gp.at[source],)):
            remote(
                ref, ref, psend.at[kind, 0], precv.at[kind, source], "exp", source
            ).wait_recv()
        return carry

    lax.fori_loop(1, size, arrive, 0)

    duo = 2 * rows
    pairs = size // 2
    half = iota((duo, LANES), 1) // HDIM
    sides = [flag(half == h) for h in range(PAIR)]
    stat_at = iota((duo, LANES), 1)

    def answer(target):
        at = pl.ds(pl.multiple_of(target * rows, rows), rows)
        return staged.at[at, pl.ds(0, span + LANES)]

    def answer_more(target):
        at = pl.ds(pl.multiple_of(target * rows, rows), rows)
        return staged.at[at, pl.ds(span + LANES, 2 * LANES)]

    def answer_remote(target):
        return remote(
            answer(target), landed.at[me], osend.at[target], orecv.at[me], "exp", target
        )

    def answer_more_remote(target):
        return remote(
            answer_more(target), landed_more.at[more], nsend.at[target], nrecv.at[more], "exp",
            target,
        )

    def visit(step):
        c = lax.rem(me // 2 + 1 + step, pairs)
        here = pl.ds(pl.multiple_of(c * duo, duo), duo)
        marks = []
        for s in range(2):
            mark = gp[2 * c + s]
            for b in range(requests):
                marks.append(jnp.broadcast_to(mark[b : b + 1, 0:1], (tree, 1)))
        mark = jnp.concatenate(marks * PAIR, axis=0)
        stats[...] = jnp.zeros_like(stats)

        def one(j, number, to):
            at = slice(j * LANES, (j + 1) * LANES)
            query = qp[here, at] * BF16(SCALE)
            stacked = jnp.concatenate([query * side for side in sides], axis=0)
            scores = matmul_nt(stacked, kp[0, :, at])
            for g in range(1, groups):
                scores = jnp.where(mark == g, matmul_nt(stacked, kp[g, :, at]), scores)
            top = jnp.max(scores, axis=1, keepdims=True).astype(BF16).astype(F32)
            weights = jnp.exp(scores - top)
            total = jnp.sum(weights, axis=1, keepdims=True)
            weights = weights.astype(BF16)
            mixed = None
            for g in range(groups):
                part = matmul(
                    jnp.where(mark == g, weights, jnp.zeros_like(weights)), vp[g, :, at]
                )
                mixed = part if mixed is None else mixed + part
            staged[here, to : to + LANES] = jnp.where(
                half == 0, mixed[:duo], mixed[duo:]
            ).astype(BF16)
            high = total.astype(BF16).astype(F32)
            got = stats[...]
            for h in range(PAIR):
                part = slice(h * duo, (h + 1) * duo)
                head = number * PAIR + h
                got = jnp.where(stat_at == head, top[part], got)
                got = jnp.where(stat_at == head + HEADS, high[part], got)
                got = jnp.where(stat_at == head + 2 * HEADS, (total - high)[part], got)
            stats[...] = got

        return c, here, one

    def attend(step, carry):
        c, here, one = visit(step)
        for j in range(each):
            one(j, me * each + j, j * LANES)
        staged[here, span : span + LANES] = stats[...].astype(BF16)
        for s in range(2):
            target = 2 * c + s

            @pl.when(target != me)
            def _():
                answer_remote(target).start()

            @pl.when(target == me)
            def _():
                pltpu.make_async_copy(answer(me), landed.at[me], oown.at[0]).start()

        return carry

    lax.fori_loop(0, pairs, attend, 0)

    @pl.when(holds_more)
    def _():
        for i, device in enumerate(extras):
            @pl.when(me == device)
            def _():
                for kind, (src, dst) in enumerate(more_copies(i)):
                    pltpu.make_async_copy(src, dst, own.at[4 + kind]).wait()

        def arrive_more(o, carry):
            source = lax.rem(me + o, size)
            for kind, ref in enumerate(from_source(source, more_lanes)):
                remote(
                    ref, ref, msend.at[kind, 0], mrecv.at[kind, source], "exp", source
                ).wait_recv()
            return carry

        lax.fori_loop(1, size, arrive_more, 0)

        def attend_more(step, carry):
            c, here, one = visit(step)
            one(each, size * each + more, span + LANES)
            staged[here, span + 2 * LANES :] = stats[...].astype(BF16)
            for s in range(2):
                target = 2 * c + s

                @pl.when(target != me)
                def _():
                    answer_more_remote(target).start()

                @pl.when(target == me)
                def _():
                    pltpu.make_async_copy(
                        answer_more(me), landed_more.at[more], nown.at[0]
                    ).start()

            return carry

        lax.fori_loop(0, pairs, attend_more, 0)
        pltpu.make_async_copy(answer_more(me), landed_more.at[more], nown.at[0]).wait()

    pltpu.make_async_copy(answer(me), landed.at[me], oown.at[0]).wait()

    small[3].wait()

    def answered(o, carry):
        source = lax.rem(me + o, size)
        remote(
            landed.at[source], landed.at[source], osend.at[0], orecv.at[source], "exp", source
        ).wait_recv()
        return carry

    lax.fori_loop(1, size, answered, 0)
    for i, device in enumerate(extras):
        @pl.when(me != device)
        def _():
            remote(
                landed_more.at[i], landed_more.at[i], nsend.at[0], nrecv.at[i], "exp", device
            ).wait_recv()

    tops = landed[0, :, span:].astype(F32)
    for i in range(1, size):
        tops += landed[i, :, span:].astype(F32)
    for i in range(len(extras)):
        tops += landed_more[i, :, LANES:].astype(F32)
    theirs = pltpu.roll(tops, LANES - HEADS, 1) + pltpu.roll(tops, LANES - 2 * HEADS, 1)
    used = lane < HEADS
    ours = jnp.where(used, sum_all[...], 1.0)
    theirs = jnp.where(used, theirs, 1.0)
    tops = jnp.where(used, tops, 0.0)
    top = jnp.maximum(top_all[...], tops)
    own_scale = jnp.exp(top_all[...] - top)
    far_scale = jnp.exp(tops - top)
    total = own_scale * ours + far_scale * theirs
    own_scale, far_scale = own_scale / total, far_scale / total
    squares = jnp.zeros((rows, 1), F32)
    left = lane < HDIM
    for block in range(width // LANES):
        at = slice(block * LANES, (block + 1) * LANES)
        i, j = divmod(block, each)
        a = PAIR * block
        if i < size:
            far = landed[i, :, j * LANES : (j + 1) * LANES]
        else:
            far = landed_more[block - size * each, :, :LANES]
        out = acc[:, at] * jnp.where(left, own_scale[:, a : a + 1], own_scale[:, a + 1 : a + 2])
        out += far.astype(F32) * jnp.where(
            left, far_scale[:, a : a + 1], far_scale[:, a + 1 : a + 2]
        )
        attended = out.astype(BF16)
        att_ref[:, at] = attended
        stream = (res[:, at].astype(F32) + attended.astype(F32)).astype(BF16)
        stream_ref[:, at] = stream
        stream = stream.astype(F32)
        squares += jnp.sum(stream * stream, axis=1, keepdims=True)
    factor = lax.rsqrt(squares / width + EPSILON)
    normed_ref[...] = (stream_ref[...].astype(F32) * factor * gain_ref[...].reshape(1, width)).astype(BF16)

    def sent(o, carry):
        i = lax.rem(me + o, size)
        for kind, (src, dst) in enumerate(base_copies(i)):
            base_remote(kind, src, dst, i).wait_send()
        answer_remote(i).wait_send()

        @pl.when(holds_more)
        def _():
            answer_more_remote(i).wait_send()

        return carry

    lax.fori_loop(1, size, sent, 0)
    for i, device in enumerate(extras):
        @pl.when(me != device)
        def _():
            for kind, (src, dst) in enumerate(more_copies(i)):
                more_remote(kind, src, dst, i).wait_send()


def attention(
    parents, chosen, picks, lengths, group_ids, gain, queries, draft_keys, draft_values, residual, cache_keys, cache_values,
    prompt_keys, prompt_values, size,
):
    requests, tree, width = queries.shape
    rows, cache = requests * tree, cache_keys.shape[1]
    groups, positions = prompt_keys.shape[:2]
    each, extras = share_of(size, width // LANES)
    count, span, chunks = len(extras), each * LANES, width // WIDE
    path = picks.shape[1]
    flat = lambda a: a.reshape(rows, width)
    vmem = pl.BlockSpec(memory_space=pltpu.VMEM)
    hbm = pl.BlockSpec(memory_space=pltpu.HBM)
    dma = pltpu.SemaphoreType.DMA
    row_block = jax.ShapeDtypeStruct((rows, width), BF16)
    return pl.pallas_call(
        functools.partial(attention_kernel, size, each, extras),
        out_shape=[
            row_block, row_block, row_block,
            jax.ShapeDtypeStruct((requests * 2 * path, width), BF16),
            jax.ShapeDtypeStruct((8, LANES), F32),
        ],
        in_specs=[pl.BlockSpec(memory_space=pltpu.SMEM)] * 2 + [vmem] * 4 + [hbm] * 8,
        out_specs=[vmem] * 5,
        scratch_shapes=[
            pltpu.VMEM((requests, chunks, cache, WIDE), BF16),
            pltpu.VMEM((requests, chunks, cache, WIDE), BF16),
            pltpu.VMEM((rows, width), BF16),
            pltpu.VMEM((rows, width), BF16),
            pltpu.VMEM((rows, width), BF16),
            pltpu.VMEM((rows, width), BF16),
            pltpu.VMEM((8, LANES), F32),
            pltpu.VMEM((rows, width), F32),
            pltpu.VMEM((rows, LANES), F32),
            pltpu.VMEM((rows, LANES), F32),
            pltpu.VMEM((groups, size * positions, span + LANES), BF16),
            pltpu.VMEM((groups, size * positions, span + LANES), BF16),
            pltpu.VMEM((size * rows, span + LANES), BF16),
            pltpu.VMEM((size, 8, LANES), F32),
            pltpu.VMEM((size * rows, span + 3 * LANES), BF16),
            pltpu.VMEM((size, rows, span + LANES), BF16),
            pltpu.VMEM((count, rows, 2 * LANES), BF16),
            pltpu.VMEM((2 * rows, LANES), F32),
            dma((2, requests, chunks)), dma((4,)), dma((4, size)), dma((4, size)), dma((7,)),
            dma((3, count)), dma((3, size)), dma((size,)), dma((size,)), dma((1,)),
            dma((size,)), dma((count,)), dma((1,)),
        ],
        compiler_params=pltpu.CompilerParams(
            collective_id=0, has_side_effects=True, vmem_limit_bytes=60 * 1024 * 1024
        ),
        name="attention",
    )(
        lengths, group_ids, parents, chosen, picks, gain, flat(queries), flat(draft_keys), flat(draft_values), flat(residual),
        cache_keys, cache_values, prompt_keys, prompt_values,
    )


def few_of(size):
    return -(-size * SPILL // MAIN) * MAIN


def expert_kernel(
    depth, size,
    normed_hbm, stream_hbm, code_hbm, router_ref, wg_hbm, wu_hbm, wd_hbm,
    out_ref,
    wg, wu, wd, stream, held, codes, staged, spilled, x, x_spill, hidden, y, y_spill, land, land_spill,
    mix, mix_spill, sums, part, passed,
    wsem, zsend, zrecv, dsend, drecv, ysend, yrecv, rsend, rrecv,
):
    z, e = lax.axis_index("req"), lax.axis_index("exp")
    rows, width = normed_hbm.shape
    units = wg.shape[0]
    holders = size // EXPERTS
    split = width // PIECE
    piece = width // HALVES
    main = size * MAIN
    few = few_of(size)
    unit = main + few
    low = z < depth // 2

    weights = [
        pltpu.make_async_copy(src, dst, wsem.at[i])
        for i, (src, dst) in enumerate(((wg_hbm, wg), (wu_hbm, wu), (wd_hbm, wd)))
    ]
    inputs = [
        pltpu.make_async_copy(src, dst, wsem.at[3 + i])
        for i, (src, dst) in enumerate(
            ((normed_hbm, held.at[z]), (code_hbm, codes.at[z]), (stream_hbm, stream))
        )
    ]
    for copy in inputs:
        copy.start()

    barrier = pltpu.get_barrier_semaphore()
    greet_plane(size)

    @pl.when(z < depth - 1)
    def _():
        pl.semaphore_signal(barrier, inc=1, device_id={"req": z + 1}, device_id_type=MESH)

    @pl.when(z > 0)
    def _():
        pl.semaphore_signal(barrier, inc=1, device_id={"req": z - 1}, device_id_type=MESH)

    pl.semaphore_wait(
        barrier, size - 1 + jnp.where(z > 0, 1, 0) + jnp.where(z < depth - 1, 1, 0)
    )

    def order(p):
        near = jnp.where(low, z, depth - 1 - z)
        step = (p + 1) // 2
        at = jnp.where(p > 2 * near, p, jnp.where(p % 2 == 1, near - step, near + step))
        return jnp.where(low, at, depth - 1 - at)

    def place(k):
        near = jnp.where(low, z, depth - 1 - z)
        at = jnp.where(low, k, depth - 1 - k)
        gap = at - near
        return jnp.where(
            gap == 0, 0, jnp.where(gap < 0, -2 * gap - 1, jnp.where(gap <= near, 2 * gap, at))
        )

    def along(k, way):
        target = z + 1 if way == 0 else z - 1
        return [
            remote(ref.at[k], ref.at[k], zsend.at[kind, way, k], zrecv.at[kind, k], "req", target)
            for kind, ref in enumerate((codes, held))
        ]

    def passes(k, way):
        if way == 0:
            return jnp.logical_and(k <= z, z < depth - 1)
        return jnp.logical_and(k >= z, z > 0)

    def pass_on(k):
        for way in range(2):
            @pl.when(passes(k, way))
            def _():
                for copy in along(k, way):
                    copy.start()

    def block(p, target, height=main):
        return pl.ds(pl.multiple_of(p * height + target * MAIN, MAIN), MAIN)

    def spot(target):
        return pl.ds(pl.multiple_of(target * MAIN, MAIN), MAIN)

    def outward(p, target, kinds=(0, 1)):
        return [
            remote(
                src, dst, dsend.at[kind, p, target], drecv.at[kind, p, e], "exp", target
            )
            for kind, (src, dst) in enumerate(
                (
                    (staged.at[block(p, target)], x.at[block(p, e, unit)]),
                    (spilled.at[p, spot(target)], x_spill.at[p, spot(e)]),
                )
            )
            if kind in kinds
        ]

    def homeward(p, target):
        return [
            remote(
                src, dst, ysend.at[kind, p, target], yrecv.at[kind, p, e], "exp", target
            )
            for kind, (src, dst) in enumerate(
                (
                    (y.at[block(p, target, unit)], land.at[block(p, e)]),
                    (y_spill.at[p, spot(target)], land_spill.at[p, spot(e)]),
                )
            )
        ]

    def start_all(copies, p, **kinds):
        def send(o, carry):
            for copy in copies(p, lax.rem(e + o, size), **kinds):
                copy.start()
            return carry

        lax.fori_loop(1, size, send, 0)

    slot = iota((main, rows), 0)
    slot_side, slot_item = slot % MAIN // SPILL, slot % SPILL
    spill_code = ((slot // MAIN) // holders * CODE + MAIN + slot_item).astype(F32)
    wanted = iota((main, rows), 0)
    wanted_code = ((wanted // MAIN) // holders * CODE + wanted % MAIN).astype(F32)

    def stage(p, carry):
        k = order(p)

        @pl.when(p > 0)
        def _():
            for copy in along(k, 0):
                copy.wait_recv()

        pass_on(k)
        code = codes[k]
        pick = flag(
            jnp.logical_or(code[0:1, :rows] == wanted_code, code[1:2, :rows] == wanted_code)
        )
        here = pl.ds(pl.multiple_of(p * main, main), main)
        step = 3 * WIDE if width % (3 * WIDE) == 0 else WIDE
        for c in range(0, width, step):
            staged[here, c : c + step] = matmul(pick, held[k, :, c : c + step]).astype(BF16)

        start_all(outward, p, kinds=(0,))
        match = jnp.logical_or(code[0:1, :rows] == spill_code, code[1:2, :rows] == spill_code)
        total = None
        for side in range(split):
            picked = matmul(
                flag(jnp.logical_and(match, slot_side == side)),
                held[k, :, side * PIECE : (side + 1) * PIECE],
            )
            total = picked if total is None else total + picked
        spilled[p] = total.astype(BF16)
        start_all(outward, p, kinds=(1,))
        x[block(p, e, unit), :] = staged[block(p, e), :]
        x_spill[p, spot(e)] = spilled[p, spot(e)]
        return carry

    def all_landed(p, refs, sem):
        def wait(o, carry):
            source = lax.rem(e + o, size)
            for kind, ref in enumerate(refs(source)):
                remote(
                    ref, ref, dsend.at[kind, 0, 0], sem.at[kind, p, source], "exp", source
                ).wait_recv()
            return carry

        lax.fori_loop(1, size, wait, 0)

    few_row, few_col = iota((few, main), 0), iota((few, main), 1)
    row_few, col_few = iota((main, few), 1), iota((main, few), 0)

    def arrive(p):
        all_landed(p, lambda s: (x.at[block(p, s, unit)], x_spill.at[p, spot(s)]), drecv)
        for side in range(split):
            unpack = flag(
                few_col == few_row // SPILL * MAIN + side * SPILL + few_row % SPILL
            )
            x[p * unit + main : (p + 1) * unit, side * PIECE : (side + 1) * PIECE] = matmul(
                unpack, x_spill[p]
            ).astype(BF16)

    def pack(p):
        total = None
        for side in range(split):
            move = flag(col_few == row_few // SPILL * MAIN + side * SPILL + row_few % SPILL)
            moved = matmul(
                move, y[p * unit + main : (p + 1) * unit, side * PIECE : (side + 1) * PIECE]
            )
            total = moved if total is None else total + moved
        y_spill[p] = total.astype(BF16)

    def returned(p):
        all_landed(p, lambda s: (land.at[block(p, s)], land_spill.at[p, spot(s)]), yrecv)

    def parts_of(start, count):
        return [
            (at, min(2 * WIDE, start + count - at))
            for at in range(start, start + count, 2 * WIDE)
        ]

    def up(start, count):
        here = slice(start, start + count)
        for at in range(0, units, 2 * WIDE):
            tile = slice(at, min(at + 2 * WIDE, units))
            gate = matmul_nt(x[here, :], wg[tile, :])
            value = matmul_nt(x[here, :], wu[tile, :])
            hidden[0:count, tile] = (gate / (1.0 + jnp.exp(-gate)) * value).astype(BF16)

    def down(start, count):
        for at in range(0, width, WIDE):
            tile = slice(at, at + WIDE)
            y[start : start + count, tile] = matmul(hidden[0:count, :], wd[:, tile]).astype(BF16)

    def both(start, count):
        for at in parts_of(start * unit, count * unit):
            up(*at)
            down(*at)

    def give_back(p):
        start_all(homeward, p)
        land[block(p, e), :] = y[block(p, e, unit), :]
        land_spill[p, spot(e)] = y_spill[p, spot(e)]

    for copy in inputs:
        copy.wait()
    for copy in weights:
        copy.start()
    lax.fori_loop(0, depth - 1, stage, 0)
    for copy in weights:
        copy.wait()
    near = depth // 2
    inside = jnp.logical_and(z > 0, z < depth - 1)

    @pl.when(inside)
    def _():
        stage(depth - 1, 0)

    for p in range(near):
        arrive(p)
    first = parts_of(0, near * unit)
    for at in first[:-1]:
        up(*at)
        down(*at)
    up(*first[-1])

    @pl.when(jnp.logical_not(inside))
    def _():
        stage(depth - 1, 0)

    down(*first[-1])
    for p in range(near):
        pack(p)
    for p in range(1, near):
        give_back(p)

    eye = flag(iota((rows, rows), 0) == iota((rows, rows), 1))
    mixed_slot = iota((rows, main), 1)
    mixed_code = ((mixed_slot // MAIN) // holders * CODE + mixed_slot % MAIN).astype(F32)
    mixed_side = mixed_slot % MAIN // SPILL
    mixed_spill = (
        (mixed_slot // MAIN) // holders * CODE + MAIN + mixed_slot % SPILL
    ).astype(F32)

    def weigh(k, carry):
        columns = matmul_nt(eye, codes[k][:, :rows].astype(BF16))
        first, second = columns[:, 0:1], columns[:, 1:2]
        logits = matmul_nt(held[k], router_ref[...])
        choice = (iota(logits.shape, 1) * CODE).astype(F32)

        def chosen(code):
            hit = jnp.logical_and(code >= choice, code < choice + CODE)
            return jnp.sum(jnp.where(hit, logits, 0.0), axis=1, keepdims=True)

        gate = 1.0 / (1.0 + jnp.exp(chosen(second) - chosen(first)))
        mix[k] = (
            jnp.where(first == mixed_code, gate, 0.0)
            + jnp.where(second == mixed_code, 1.0 - gate, 0.0)
        ).astype(BF16)
        mix_spill[k] = (
            jnp.where(first == mixed_spill, gate, 0.0)
            + jnp.where(second == mixed_spill, 1.0 - gate, 0.0)
        ).astype(BF16)
        return carry

    lax.fori_loop(0, depth, weigh, 0)

    for p in range(near, depth - 1):
        arrive(p)
    both(near, depth - 1 - near)
    for p in range(near, depth - 1):
        pack(p)
    arrive(depth - 1)
    both(depth - 1, 1)
    pack(depth - 1)
    for p in range(depth - 1, near - 1, -1):
        give_back(p)
    give_back(0)

    def relay(h, side, way):
        target = z + 1 if way == 0 else z - 1
        at = jnp.where(jnp.logical_and(way == 1, target == h), depth, h)
        return remote(
            part.at[h, side], passed.at[at, side], rsend.at[h, side], rrecv.at[at, side], "req",
            target,
        )

    def arrived(at, side):
        remote(
            passed.at[at, side], passed.at[at, side], rsend.at[0, 0], rrecv.at[at, side], "req",
            jnp.where(z > 0, z - 1, z + 1),
        ).wait_recv()

    def combine(h, side):
        p = place(h)
        here = pl.ds(pl.multiple_of(p * main, main), main)
        for c in range(piece // PIECE):
            number = side * (piece // PIECE) + c
            at = slice(number * PIECE, (number + 1) * PIECE)
            spill = mix_spill[h]
            sums[:, c * PIECE : (c + 1) * PIECE] = matmul(mix[h], land[here, at]) + matmul(
                jnp.where(mixed_side == number, spill, jnp.zeros_like(spill)), land_spill[p]
            )

    rank = 2 * jnp.minimum(z, depth - 1 - z) + 1

    def reduce(j, carry):
        i = j + jnp.where(j >= rank, 1, 0)
        past = jnp.where(j >= 2, 1, 0)
        i = jnp.where(z == 0, jnp.where(j == 0, 2, j + past), i)
        last = jnp.where(j == 0, 3, j - 1 + past + jnp.where(j >= 3, 1, 0))
        i = jnp.where(z == depth - 1, last, i)
        swap = jnp.logical_and(low, z > 0)

        h = jnp.where(i % 2 == 0, i // 2, depth - 1 - i // 2)
        h = jnp.where(swap, depth - 1 - h, h)
        p = place(h)
        returned(p)
        rising = h > z
        joined = jnp.logical_or(
            jnp.logical_and(rising, z > 0),
            jnp.logical_and(jnp.logical_not(rising), z < depth - 1),
        )
        for side in range(HALVES):
            combine(h, side)

            @pl.when(joined)
            def _():
                arrived(h, side)
                sums[...] += passed[h, side].astype(F32)

            part[h, side] = sums[...].astype(BF16)

            @pl.when(rising)
            def _():
                relay(h, side, 0).start()

            @pl.when(jnp.logical_not(rising))
            def _():
                relay(h, side, 1).start()

        return carry

    lax.fori_loop(0, depth - 1, reduce, 0)
    returned(0)
    for side in range(HALVES):
        at = slice(side * piece, (side + 1) * piece)
        combine(z, side)
        sums[...] += stream[:, at].astype(F32)

        @pl.when(z > 0)
        def _():
            arrived(z, side)
            sums[...] += passed[z, side].astype(F32)

        @pl.when(z < depth - 1)
        def _():
            arrived(depth, side)
            sums[...] += passed[depth, side].astype(F32)

        out_ref[:, at] = sums[...].astype(BF16)

    def finish(k, carry):
        for way in range(2):
            @pl.when(passes(k, way))
            def _():
                for copy in along(k, way):
                    copy.wait_send()

        for side in range(HALVES):
            @pl.when(k > z)
            def _():
                relay(k, side, 0).wait_send()

            @pl.when(k < z)
            def _():
                relay(k, side, 1).wait_send()

        def plane_done(o, carry):
            target = lax.rem(e + o, size)
            for copy in outward(k, target) + homeward(k, target):
                copy.wait_send()
            return carry

        lax.fori_loop(1, size, plane_done, 0)
        return carry

    lax.fori_loop(0, depth, finish, 0)


def expert_layer(normed, stream, code, router, w_gate, w_up, w_down, depth, size):
    rows, width = normed.shape
    units = w_gate.shape[0]
    piece = width // HALVES
    main = size * MAIN
    unit = main + few_of(size)
    most = min(2 * WIDE, max(depth // 2, 1) * unit)
    dma = pltpu.SemaphoreType.DMA
    vmem = pl.BlockSpec(memory_space=pltpu.VMEM)
    hbm = pl.BlockSpec(memory_space=pltpu.HBM)
    return pl.pallas_call(
        functools.partial(expert_kernel, depth, size),
        out_shape=jax.ShapeDtypeStruct((rows, width), BF16),
        in_specs=[hbm] * 3 + [vmem] + [hbm] * 3,
        out_specs=vmem,
        scratch_shapes=[
            pltpu.VMEM((units, width), BF16),
            pltpu.VMEM((units, width), BF16),
            pltpu.VMEM((units, width), BF16),
            pltpu.VMEM((rows, width), BF16),
            pltpu.VMEM((depth, rows, width), BF16),
            pltpu.VMEM((depth, 8, LANES), F32),
            pltpu.VMEM((depth * main, width), BF16),
            pltpu.VMEM((depth, main, PIECE), BF16),
            pltpu.VMEM((depth * unit, width), BF16),
            pltpu.VMEM((depth, main, PIECE), BF16),
            pltpu.VMEM((most, units), BF16),
            pltpu.VMEM((depth * unit, width), BF16),
            pltpu.VMEM((depth, main, PIECE), BF16),
            pltpu.VMEM((depth * main, width), BF16),
            pltpu.VMEM((depth, main, PIECE), BF16),
            pltpu.VMEM((depth, rows, main), BF16),
            pltpu.VMEM((depth, rows, main), BF16),
            pltpu.VMEM((rows, piece), F32),
            pltpu.VMEM((depth, HALVES, rows, piece), BF16),
            pltpu.VMEM((depth + 1, HALVES, rows, piece), BF16),
            dma((6,)), dma((2, 2, depth)), dma((2, depth)),
            dma((2, depth, size)), dma((2, depth, size)),
            dma((2, depth, size)), dma((2, depth, size)),
            dma((depth, HALVES)), dma((depth + 1, HALVES)),
        ],
        compiler_params=pltpu.CompilerParams(
            collective_id=1, has_side_effects=True, vmem_limit_bytes=60 * 1024 * 1024
        ),
        name="experts",
    )(normed, stream, code, router, w_gate, w_up, w_down)


def on_device(
    queries,
    draft_keys,
    draft_values,
    tree_parents,
    cache_keys,
    cache_values,
    cache_lengths,
    prompt_keys,
    prompt_values,
    group_ids,
    residual,
    norm_gain,
    router,
    w_gate,
    w_up,
    w_down,
    expert_ids,
    accepted_rows,
):
    requests, tree, width = queries.shape
    rows = requests * tree
    depth, size = lax.axis_size("req"), lax.axis_size("exp")

    attended, stream, normed, kept, code = attention(
        tree_parents, jnp.swapaxes(expert_ids, 1, 2), accepted_rows, cache_lengths, group_ids,
        norm_gain, queries, draft_keys, draft_values,
        residual, cache_keys, cache_values, prompt_keys, prompt_values, size,
    )
    layer_out = expert_layer(
        normed, stream, code, router.T, w_gate[0].T, w_up[0].T, w_down[0], depth, size
    )
    return (
        attended.reshape(requests, tree, width),
        layer_out.reshape(requests, tree, width),
        kept.reshape(requests, 2, accepted_rows.shape[1], width),
    )


def solution(mesh):
    both = ("req", "exp")
    return jax.shard_map(
        on_device,
        mesh=mesh,
        in_specs=(
            P(both, None, None),
            P(both, None, None),
            P(both, None, None),
            P(both, None),
            P(both, None, None),
            P(both, None, None),
            P(both),
            P("req", "exp", None),
            P("req", "exp", None),
            P(both),
            P(both, None, None),
            P(),
            P(),
            P("exp", None, "req"),
            P("exp", None, "req"),
            P("exp", "req", None),
            P(both, None, None),
            P(both, None),
        ),
        out_specs=(
            P(both, None, None),
            P(both, None, None),
            P(both, None, None, None),
        ),
        check_vma=False,
    )
```

```python
import functools

import jax
import jax.numpy as jnp
from jax import lax
from jax.experimental import pallas as pl
from jax.experimental.pallas import tpu as pltpu
from jax.sharding import PartitionSpec as P

HEADS = 36
HDIM = 64
EXPERTS = 8
TOPK = 2
LANES = 128
PAIR = LANES // HDIM
WIDE = 256
MAIN = 16
SPILL = 2
PIECE = 384
CODE = 32
EPSILON = 1e-05
SCALE = HDIM ** (-0.5)
NT = (((1,), (1,)), ((), ()))
F32 = jnp.float32
BF16 = jnp.bfloat16
MESH = pl.DeviceIdType.MESH


def remote(src, dst, send, recv, axis, target):
    return pltpu.make_async_remote_copy(
        src_ref=src, dst_ref=dst, send_sem=send, recv_sem=recv, device_id={axis: target},
        device_id_type=MESH,
    )


def iota(shape, dim):
    return lax.broadcasted_iota(jnp.int32, shape, dim)


def flag(condition):
    return jnp.where(condition, 1.0, 0.0).astype(BF16)


def matmul(a, b):
    return jnp.dot(a, b, preferred_element_type=F32)


def matmul_nt(a, b):
    return lax.dot_general(a, b, NT, preferred_element_type=F32)


def greet_plane(size):
    e = lax.axis_index("exp")
    barrier = pltpu.get_barrier_semaphore()
    for step in range(1, size):
        pl.semaphore_signal(
            barrier, inc=1, device_id={"exp": lax.rem(e + step, size)}, device_id_type=MESH
        )


def share_of(size, blocks):
    each = blocks // size
    more = blocks - each * size
    return each, [i * (size - 1) // max(more - 1, 1) for i in range(more)]


def attention_kernel(
    size, each, extras,
    len_ref, group_ref, parent_ref, chosen_ref, pick_ref, gain_ref, q_hbm, dk_hbm, dv_hbm, res_hbm, ck_hbm, cv_hbm, pk_hbm, pv_hbm,
    att_ref, stream_ref, normed_ref, kept_ref, code_ref,
    ck, cv, q, dk, dv, res, group, acc, top_all, sum_all, kp, vp, qp, gp, staged, landed, landed_more,
    stats, csem, lsem, psend, precv, own, msend, mrecv, osend, orecv, oown, nsend, nrecv, nown,
):
    me = lax.axis_index("exp")
    rows, width = q.shape
    requests, cache = ck.shape[0], ck.shape[2]
    tree = rows // requests
    chunks = width // WIDE
    span = each * LANES
    groups, positions = pk_hbm.shape[0], pk_hbm.shape[1]
    wide_heads = WIDE // HDIM

    def cols(g):
        return pl.ds(pl.multiple_of(g * WIDE, WIDE), WIDE)

    def cache_copy(which, b, g):
        src, dst = ((ck_hbm, ck), (cv_hbm, cv))[which]
        return pltpu.make_async_copy(
            src.at[b, :, cols(g)], dst.at[b, g], csem.at[which, b, g]
        )

    small = [
        pltpu.make_async_copy(src, dst, lsem.at[i])
        for i, (src, dst) in enumerate(((q_hbm, q), (dk_hbm, dk), (dv_hbm, dv), (res_hbm, res)))
    ]
    for copy in small[:3]:
        copy.start()

    def load(g, carry):
        for b in range(requests):
            for which in range(2):
                cache_copy(which, b, g).start()
        return carry

    greet_plane(size)

    row8 = iota((8, LANES), 0)
    marks = jnp.zeros((8, LANES), jnp.int32)
    for b in range(requests):
        marks = jnp.where(row8 == b, group_ref[b], marks)
    group[...] = marks.astype(F32)

    pl.semaphore_wait(pltpu.get_barrier_semaphore(), size - 1)

    more = jnp.int32(0)
    holds_more = jnp.bool_(False)
    for i, device in enumerate(extras):
        more = jnp.where(me == device, i, more)
        holds_more = jnp.logical_or(holds_more, me == device)

    def from_source(s, lanes):
        keys = pl.ds(pl.multiple_of(s * positions, positions), positions)
        return (
            kp.at[:, keys, lanes],
            vp.at[:, keys, lanes],
            qp.at[pl.ds(pl.multiple_of(s * rows, rows), rows), lanes],
        )

    base_lanes, more_lanes = pl.ds(0, span), pl.ds(span, LANES)

    def base_copies(i):
        at = pl.ds(pl.multiple_of(i * span, LANES), span)
        return list(
            zip(
                (pk_hbm.at[:, :, at], pv_hbm.at[:, :, at], q_hbm.at[:, at], group),
                from_source(me, base_lanes) + (gp.at[me],),
            )
        )

    def more_copies(i):
        at = pl.ds((size * each + i) * LANES, LANES)
        return list(
            zip(
                (pk_hbm.at[:, :, at], pv_hbm.at[:, :, at], q_hbm.at[:, at]),
                from_source(me, more_lanes),
            )
        )

    def base_remote(kind, src, dst, i):
        return remote(src, dst, psend.at[kind, i], precv.at[kind, me], "exp", i)

    def more_remote(kind, src, dst, i):
        return remote(src, dst, msend.at[kind, i], mrecv.at[kind, me], "exp", extras[i])

    def send_heads(o, carry):
        i = lax.rem(o + me, size)
        for kind, (src, dst) in enumerate(base_copies(i)):
            base_remote(kind, src, dst, i).start()
        return carry

    lax.fori_loop(1, size, send_heads, 0)
    for i, device in enumerate(extras):
        @pl.when(me != device)
        def _():
            for kind, (src, dst) in enumerate(more_copies(i)):
                more_remote(kind, src, dst, i).start()

        @pl.when(me == device)
        def _():
            for kind, (src, dst) in enumerate(more_copies(i)):
                pltpu.make_async_copy(src, dst, own.at[4 + kind]).start()

    for kind, (src, dst) in enumerate(base_copies(me)):
        pltpu.make_async_copy(src, dst, own.at[kind]).start()
    lax.fori_loop(0, chunks, load, 0)
    small[3].start()

    def column(lines):
        length = lines[0].shape[1]
        same = iota((length, length), 0) == iota((length, length), 1)
        return jnp.concatenate(
            [jnp.sum(jnp.where(same, line, 0), axis=1, keepdims=True) for line in lines], axis=0
        )

    parent = column([parent_ref[b : b + 1] for b in range(requests)])
    at_row, at_col = iota((rows, rows), 0), iota((rows, rows), 1)
    base = at_row // tree * tree
    reached = jnp.logical_or(
        at_row == at_col, jnp.logical_and(at_col - base == parent, parent >= 0)
    )
    for _ in range(max(1, (tree - 1).bit_length())):
        step = flag(reached)
        reached = matmul(step, step) > 0.5
    related = jnp.where(reached, 1.0, 0.0)

    first, second = [
        column([chosen_ref[b, k : k + 1] for b in range(requests)]).astype(F32) for k in range(TOPK)
    ]
    lane = iota((rows, LANES), 1)
    expert = lane.astype(F32)
    named = flag(jnp.logical_or(expert == first, expert == second))
    before = matmul(flag(at_col < at_row), named)
    codes = [
        e * CODE + jnp.sum(jnp.where(expert == e, before, 0.0), axis=1, keepdims=True)
        for e in (first, second)
    ]
    code_columns = jnp.where(lane == 0, codes[0], jnp.where(lane == 1, codes[1], 0.0))
    code_ref[...] = jnp.zeros_like(code_ref)
    code_ref[:, :rows] = matmul_nt(
        flag(iota((8, LANES), 0) == iota((8, LANES), 1)), code_columns.astype(BF16)
    )

    for copy in small[:3]:
        copy.wait()
    path = pick_ref.shape[1]
    picked = column([pick_ref[b : b + 1] for b in range(requests)])
    owner = iota((requests * path, rows), 0) // path
    wanted = flag(iota((requests * path, rows), 1) == picked + owner * tree)
    for kind, ref in enumerate((dk, dv)):
        kept = matmul(wanted, ref[...]).astype(BF16)
        for b in range(requests):
            kept_ref[pl.ds((2 * b + kind) * path, path), :] = kept[b * path : (b + 1) * path]

    head_wide = iota((tree, WIDE), 1) // HDIM
    masks = [flag(head_wide == h) for h in range(wide_heads)]
    stat_lane = iota((tree, LANES), 1)
    seen = [
        jnp.concatenate([related[b * tree : (b + 1) * tree]] * wide_heads, axis=0)
        for b in range(requests)
    ]
    slot_at = iota((wide_heads * tree, cache), 1)
    top_all[...] = jnp.zeros_like(top_all)
    sum_all[...] = jnp.zeros_like(sum_all)

    def local(g, carry):
        for b in range(requests):
            here = slice(b * tree, (b + 1) * tree)
            for which in range(2):
                cache_copy(which, b, g).wait()
            query = q[here, cols(g)] * BF16(SCALE)
            stacked = jnp.concatenate([query * mask for mask in masks], axis=0)
            s_cache = matmul_nt(stacked, ck[b, g])
            s_cache = jnp.where(slot_at < len_ref[b], s_cache, -jnp.inf)
            s_tree = jnp.where(seen[b] > 0.5, matmul_nt(stacked, dk[:, cols(g)]), -jnp.inf)
            top = jnp.maximum(
                jnp.max(s_cache, axis=1, keepdims=True), jnp.max(s_tree, axis=1, keepdims=True)
            )
            w_cache = jnp.exp(s_cache - top)
            w_tree = jnp.exp(s_tree - top)
            total = jnp.sum(w_cache, axis=1, keepdims=True) + jnp.sum(
                w_tree, axis=1, keepdims=True
            )
            mixed = matmul(w_cache.astype(BF16), cv[b, g])
            mixed += matmul(w_tree.astype(BF16), dv[:, cols(g)])
            out = mixed[:tree]
            tops, sums = top_all[here], sum_all[here]
            for h in range(wide_heads):
                part = slice(h * tree, (h + 1) * tree)
                if h:
                    out = jnp.where(head_wide == h, mixed[part], out)
                at = g * wide_heads + h
                tops = jnp.where(stat_lane == at, top[part], tops)
                sums = jnp.where(stat_lane == at, total[part], sums)
            acc[here, cols(g)] = out
            top_all[here] = tops
            sum_all[here] = sums
        return carry

    lax.fori_loop(0, chunks, local, 0)

    for kind, (src, dst) in enumerate(base_copies(me)):
        pltpu.make_async_copy(src, dst, own.at[kind]).wait()

    def arrive(o, carry):
        source = lax.rem(me + o, size)
        for kind, ref in enumerate(from_source(source, base_lanes) + (gp.at[source],)):
            remote(
                ref, ref, psend.at[kind, 0], precv.at[kind, source], "exp", source
            ).wait_recv()
        return carry

    lax.fori_loop(1, size, arrive, 0)

    duo = 2 * rows
    pairs = size // 2
    half = iota((duo, LANES), 1) // HDIM
    sides = [flag(half == h) for h in range(PAIR)]
    stat_at = iota((duo, LANES), 1)

    def answer(target):
        at = pl.ds(pl.multiple_of(target * rows, rows), rows)
        return staged.at[at, pl.ds(0, span + LANES)]

    def answer_more(target):
        at = pl.ds(pl.multiple_of(target * rows, rows), rows)
        return staged.at[at, pl.ds(span + LANES, 2 * LANES)]

    def answer_remote(target):
        return remote(
            answer(target), landed.at[me], osend.at[target], orecv.at[me], "exp", target
        )

    def answer_more_remote(target):
        return remote(
            answer_more(target), landed_more.at[more], nsend.at[target], nrecv.at[more], "exp",
            target,
        )

    def visit(step):
        c = lax.rem(me // 2 + 1 + step, pairs)
        here = pl.ds(pl.multiple_of(c * duo, duo), duo)
        marks = []
        for s in range(2):
            mark = gp[2 * c + s]
            for b in range(requests):
                marks.append(jnp.broadcast_to(mark[b : b + 1, 0:1], (tree, 1)))
        mark = jnp.concatenate(marks * PAIR, axis=0)
        stats[...] = jnp.zeros_like(stats)

        def one(j, number, to):
            at = slice(j * LANES, (j + 1) * LANES)
            query = qp[here, at] * BF16(SCALE)
            stacked = jnp.concatenate([query * side for side in sides], axis=0)
            scores = matmul_nt(stacked, kp[0, :, at])
            for g in range(1, groups):
                scores = jnp.where(mark == g, matmul_nt(stacked, kp[g, :, at]), scores)
            top = jnp.max(scores, axis=1, keepdims=True).astype(BF16).astype(F32)
            weights = jnp.exp(scores - top)
            total = jnp.sum(weights, axis=1, keepdims=True)
            weights = weights.astype(BF16)
            mixed = None
            for g in range(groups):
                part = matmul(
                    jnp.where(mark == g, weights, jnp.zeros_like(weights)), vp[g, :, at]
                )
                mixed = part if mixed is None else mixed + part
            staged[here, to : to + LANES] = jnp.where(
                half == 0, mixed[:duo], mixed[duo:]
            ).astype(BF16)
            high = total.astype(BF16).astype(F32)
            got = stats[...]
            for h in range(PAIR):
                part = slice(h * duo, (h + 1) * duo)
                head = number * PAIR + h
                got = jnp.where(stat_at == head, top[part], got)
                got = jnp.where(stat_at == head + HEADS, high[part], got)
                got = jnp.where(stat_at == head + 2 * HEADS, (total - high)[part], got)
            stats[...] = got

        return c, here, one

    def attend(step, carry):
        c, here, one = visit(step)
        for j in range(each):
            one(j, me * each + j, j * LANES)
        staged[here, span : span + LANES] = stats[...].astype(BF16)
        for s in range(2):
            target = 2 * c + s

            @pl.when(target != me)
            def _():
                answer_remote(target).start()

            @pl.when(target == me)
            def _():
                pltpu.make_async_copy(answer(me), landed.at[me], oown.at[0]).start()

        return carry

    lax.fori_loop(0, pairs, attend, 0)

    @pl.when(holds_more)
    def _():
        for i, device in enumerate(extras):
            @pl.when(me == device)
            def _():
                for kind, (src, dst) in enumerate(more_copies(i)):
                    pltpu.make_async_copy(src, dst, own.at[4 + kind]).wait()

        def arrive_more(o, carry):
            source = lax.rem(me + o, size)
            for kind, ref in enumerate(from_source(source, more_lanes)):
                remote(
                    ref, ref, msend.at[kind, 0], mrecv.at[kind, source], "exp", source
                ).wait_recv()
            return carry

        lax.fori_loop(1, size, arrive_more, 0)

        def attend_more(step, carry):
            c, here, one = visit(step)
            one(each, size * each + more, span + LANES)
            staged[here, span + 2 * LANES :] = stats[...].astype(BF16)
            for s in range(2):
                target = 2 * c + s

                @pl.when(target != me)
                def _():
                    answer_more_remote(target).start()

                @pl.when(target == me)
                def _():
                    pltpu.make_async_copy(
                        answer_more(me), landed_more.at[more], nown.at[0]
                    ).start()

            return carry

        lax.fori_loop(0, pairs, attend_more, 0)
        pltpu.make_async_copy(answer_more(me), landed_more.at[more], nown.at[0]).wait()

    pltpu.make_async_copy(answer(me), landed.at[me], oown.at[0]).wait()

    small[3].wait()

    def answered(o, carry):
        source = lax.rem(me + o, size)
        remote(
            landed.at[source], landed.at[source], osend.at[0], orecv.at[source], "exp", source
        ).wait_recv()
        return carry

    lax.fori_loop(1, size, answered, 0)
    for i, device in enumerate(extras):
        @pl.when(me != device)
        def _():
            remote(
                landed_more.at[i], landed_more.at[i], nsend.at[0], nrecv.at[i], "exp", device
            ).wait_recv()

    tops = landed[0, :, span:].astype(F32)
    for i in range(1, size):
        tops += landed[i, :, span:].astype(F32)
    for i in range(len(extras)):
        tops += landed_more[i, :, LANES:].astype(F32)
    theirs = pltpu.roll(tops, LANES - HEADS, 1) + pltpu.roll(tops, LANES - 2 * HEADS, 1)
    used = lane < HEADS
    ours = jnp.where(used, sum_all[...], 1.0)
    theirs = jnp.where(used, theirs, 1.0)
    tops = jnp.where(used, tops, 0.0)
    top = jnp.maximum(top_all[...], tops)
    own_scale = jnp.exp(top_all[...] - top)
    far_scale = jnp.exp(tops - top)
    total = own_scale * ours + far_scale * theirs
    own_scale, far_scale = own_scale / total, far_scale / total
    squares = jnp.zeros((rows, 1), F32)
    left = lane < HDIM
    for block in range(width // LANES):
        at = slice(block * LANES, (block + 1) * LANES)
        i, j = divmod(block, each)
        a = PAIR * block
        if i < size:
            far = landed[i, :, j * LANES : (j + 1) * LANES]
        else:
            far = landed_more[block - size * each, :, :LANES]
        out = acc[:, at] * jnp.where(left, own_scale[:, a : a + 1], own_scale[:, a + 1 : a + 2])
        out += far.astype(F32) * jnp.where(
            left, far_scale[:, a : a + 1], far_scale[:, a + 1 : a + 2]
        )
        attended = out.astype(BF16)
        att_ref[:, at] = attended
        stream = (res[:, at].astype(F32) + attended.astype(F32)).astype(BF16)
        stream_ref[:, at] = stream
        stream = stream.astype(F32)
        squares += jnp.sum(stream * stream, axis=1, keepdims=True)
    factor = lax.rsqrt(squares / width + EPSILON)
    normed_ref[...] = (stream_ref[...].astype(F32) * factor * gain_ref[...].reshape(1, width)).astype(BF16)

    def sent(o, carry):
        i = lax.rem(me + o, size)
        for kind, (src, dst) in enumerate(base_copies(i)):
            base_remote(kind, src, dst, i).wait_send()
        answer_remote(i).wait_send()

        @pl.when(holds_more)
        def _():
            answer_more_remote(i).wait_send()

        return carry

    lax.fori_loop(1, size, sent, 0)
    for i, device in enumerate(extras):
        @pl.when(me != device)
        def _():
            for kind, (src, dst) in enumerate(more_copies(i)):
                more_remote(kind, src, dst, i).wait_send()


def attention(
    parents, chosen, picks, lengths, group_ids, gain, queries, draft_keys, draft_values, residual, cache_keys, cache_values,
    prompt_keys, prompt_values, size,
):
    requests, tree, width = queries.shape
    rows, cache = requests * tree, cache_keys.shape[1]
    groups, positions = prompt_keys.shape[:2]
    each, extras = share_of(size, width // LANES)
    count, span, chunks = len(extras), each * LANES, width // WIDE
    path = picks.shape[1]
    flat = lambda a: a.reshape(rows, width)
    vmem = pl.BlockSpec(memory_space=pltpu.VMEM)
    hbm = pl.BlockSpec(memory_space=pltpu.HBM)
    dma = pltpu.SemaphoreType.DMA
    row_block = jax.ShapeDtypeStruct((rows, width), BF16)
    return pl.pallas_call(
        functools.partial(attention_kernel, size, each, extras),
        out_shape=[
            row_block, row_block, row_block,
            jax.ShapeDtypeStruct((requests * 2 * path, width), BF16),
            jax.ShapeDtypeStruct((8, LANES), F32),
        ],
        in_specs=[pl.BlockSpec(memory_space=pltpu.SMEM)] * 2 + [vmem] * 4 + [hbm] * 8,
        out_specs=[vmem] * 5,
        scratch_shapes=[
            pltpu.VMEM((requests, chunks, cache, WIDE), BF16),
            pltpu.VMEM((requests, chunks, cache, WIDE), BF16),
            pltpu.VMEM((rows, width), BF16),
            pltpu.VMEM((rows, width), BF16),
            pltpu.VMEM((rows, width), BF16),
            pltpu.VMEM((rows, width), BF16),
            pltpu.VMEM((8, LANES), F32),
            pltpu.VMEM((rows, width), F32),
            pltpu.VMEM((rows, LANES), F32),
            pltpu.VMEM((rows, LANES), F32),
            pltpu.VMEM((groups, size * positions, span + LANES), BF16),
            pltpu.VMEM((groups, size * positions, span + LANES), BF16),
            pltpu.VMEM((size * rows, span + LANES), BF16),
            pltpu.VMEM((size, 8, LANES), F32),
            pltpu.VMEM((size * rows, span + 3 * LANES), BF16),
            pltpu.VMEM((size, rows, span + LANES), BF16),
            pltpu.VMEM((count, rows, 2 * LANES), BF16),
            pltpu.VMEM((2 * rows, LANES), F32),
            dma((2, requests, chunks)), dma((4,)), dma((4, size)), dma((4, size)), dma((7,)),
            dma((3, count)), dma((3, size)), dma((size,)), dma((size,)), dma((1,)),
            dma((size,)), dma((count,)), dma((1,)),
        ],
        compiler_params=pltpu.CompilerParams(
            collective_id=0, has_side_effects=True, vmem_limit_bytes=60 * 1024 * 1024
        ),
        name="attention",
    )(
        lengths, group_ids, parents, chosen, picks, gain, flat(queries), flat(draft_keys), flat(draft_values), flat(residual),
        cache_keys, cache_values, prompt_keys, prompt_values,
    )


def cuts_of(width):
    pieces = width // PIECE
    back = 3 if pieces % 3 == 0 else pieces
    return pieces, back


def few_of(size):
    return -(-size * SPILL // MAIN) * MAIN


def turns_of(depth):
    if depth == 4:
        return [[1, 3, 2], [3, 0, 2], [0, 3, 1], [2, 0, 1]]
    turns = []
    for z in range(depth):
        ends = [(i, depth - 1 - i) for i in range(depth // 2)]
        pairs = [pair[::-1] if z < depth // 2 else pair for pair in ends]
        turns.append([h for pair in pairs for h in pair if h != z])
    return turns


def expert_kernel(
    depth, size,
    normed_hbm, stream_hbm, code_hbm, router_ref, wg_hbm, wu_hbm, wd_hbm,
    out_ref,
    wg, wu, wd, stream, held, codes, staged, spilled, x, x_spill, hidden, y, y_spill, land, land_spill,
    mix, mix_spill, sums, part, passed,
    wsem, zsend, zrecv, dsend, drecv, ysend, yrecv, rsend, rrecv,
):
    z, e = lax.axis_index("req"), lax.axis_index("exp")
    rows, width = normed_hbm.shape
    units = wg.shape[0]
    holders = size // EXPERTS
    split = width // PIECE
    cuts, back = cuts_of(width)
    piece = width // cuts
    main = size * MAIN
    few = few_of(size)
    unit = main + few
    low = z < depth // 2

    weights = [
        pltpu.make_async_copy(src, dst, wsem.at[i])
        for i, (src, dst) in enumerate(((wg_hbm, wg), (wu_hbm, wu), (wd_hbm, wd)))
    ]
    inputs = [
        pltpu.make_async_copy(src, dst, wsem.at[3 + i])
        for i, (src, dst) in enumerate(
            ((normed_hbm, held.at[z]), (code_hbm, codes.at[z]), (stream_hbm, stream))
        )
    ]
    for copy in inputs:
        copy.start()

    barrier = pltpu.get_barrier_semaphore()
    greet_plane(size)

    @pl.when(z < depth - 1)
    def _():
        pl.semaphore_signal(barrier, inc=1, device_id={"req": z + 1}, device_id_type=MESH)

    @pl.when(z > 0)
    def _():
        pl.semaphore_signal(barrier, inc=1, device_id={"req": z - 1}, device_id_type=MESH)

    def order(p):
        near = jnp.where(low, z, depth - 1 - z)
        step = (p + 1) // 2
        at = jnp.where(p > 2 * near, p, jnp.where(p % 2 == 1, near - step, near + step))
        return jnp.where(low, at, depth - 1 - at)

    def place(k):
        near = jnp.where(low, z, depth - 1 - z)
        at = jnp.where(low, k, depth - 1 - k)
        gap = at - near
        return jnp.where(
            gap == 0, 0, jnp.where(gap < 0, -2 * gap - 1, jnp.where(gap <= near, 2 * gap, at))
        )

    def along(k, way):
        target = z + 1 if way == 0 else z - 1
        return [
            remote(ref.at[k], ref.at[k], zsend.at[kind, way, k], zrecv.at[kind, k], "req", target)
            for kind, ref in enumerate((codes, held))
        ]

    def passes(k, way):
        if way == 0:
            return jnp.logical_and(k <= z, z < depth - 1)
        return jnp.logical_and(k >= z, z > 0)

    def pass_on(k):
        for way in range(2):
            @pl.when(passes(k, way))
            def _():
                for copy in along(k, way):
                    copy.start()

    def block(p, target, height=main):
        return pl.ds(pl.multiple_of(p * height + target * MAIN, MAIN), MAIN)

    def spot(target):
        return pl.ds(pl.multiple_of(target * MAIN, MAIN), MAIN)

    def outward(p, target, kinds=(0, 1)):
        return [
            remote(
                src, dst, dsend.at[kind, p, target], drecv.at[kind, p, e], "exp", target
            )
            for kind, (src, dst) in enumerate(
                (
                    (staged.at[block(p, target)], x.at[block(p, e, unit)]),
                    (spilled.at[p, spot(target)], x_spill.at[p, spot(e)]),
                )
            )
            if kind in kinds
        ]

    def homeward(p, target, only=None):
        groups = [
            (
                y.at[block(p, target, unit), pl.ds(g * (width // back), width // back)],
                land.at[block(p, e), pl.ds(g * (width // back), width // back)],
            )
            for g in range(back)
        ]
        return [
            remote(
                src, dst, ysend.at[kind, p, target], yrecv.at[kind, p, e], "exp", target
            )
            for kind, (src, dst) in enumerate(
                [(y_spill.at[p, spot(target)], land_spill.at[p, spot(e)])] + groups
            )
            if only is None or kind == only
        ]

    def start_all(copies, p, **kinds):
        def send(o, carry):
            for copy in copies(p, lax.rem(e + o, size), **kinds):
                copy.start()
            return carry

        lax.fori_loop(1, size, send, 0)

    slot = iota((main, rows), 0)
    slot_side, slot_item = slot % MAIN // SPILL, slot % SPILL
    spill_code = ((slot // MAIN) // holders * CODE + MAIN + slot_item).astype(F32)
    wanted = iota((main, rows), 0)
    wanted_code = ((wanted // MAIN) // holders * CODE + wanted % MAIN).astype(F32)

    def pick_main(p, k):
        code = codes[k]
        pick = flag(
            jnp.logical_or(code[0:1, :rows] == wanted_code, code[1:2, :rows] == wanted_code)
        )
        here = pl.ds(pl.multiple_of(p * main, main), main)
        step = 3 * WIDE if width % (3 * WIDE) == 0 else WIDE
        for c in range(0, width, step):
            staged[here, c : c + step] = matmul(pick, held[k, :, c : c + step]).astype(BF16)

    def pick_spill(p, k):
        code = codes[k]
        match = jnp.logical_or(code[0:1, :rows] == spill_code, code[1:2, :rows] == spill_code)
        total = None
        for side in range(split):
            picked = matmul(
                flag(jnp.logical_and(match, slot_side == side)),
                held[k, :, side * PIECE : (side + 1) * PIECE],
            )
            total = picked if total is None else total + picked
        spilled[p] = total.astype(BF16)

    def keep(p):
        x[block(p, e, unit), :] = staged[block(p, e), :]
        x_spill[p, spot(e)] = spilled[p, spot(e)]

    def stage(p, carry):
        k = order(p)
        for copy in along(k, 0):
            copy.wait_recv()
        pass_on(k)
        pick_main(p, k)
        start_all(outward, p, kinds=(0,))
        pick_spill(p, k)
        start_all(outward, p, kinds=(1,))
        keep(p)
        return carry

    def all_landed(p, refs, sem, first=0):
        def wait(o, carry):
            source = lax.rem(e + o, size)
            for kind, ref in enumerate(refs(source), first):
                remote(
                    ref, ref, dsend.at[0, 0, 0], sem.at[kind, p, source], "exp", source
                ).wait_recv()
            return carry

        lax.fori_loop(1, size, wait, 0)

    few_row, few_col = iota((few, main), 0), iota((few, main), 1)
    row_few, col_few = iota((main, few), 1), iota((main, few), 0)

    def arrive(p):
        all_landed(p, lambda s: (x.at[block(p, s, unit)], x_spill.at[p, spot(s)]), drecv)
        for side in range(split):
            unpack = flag(
                few_col == few_row // SPILL * MAIN + side * SPILL + few_row % SPILL
            )
            x[p * unit + main : (p + 1) * unit, side * PIECE : (side + 1) * PIECE] = matmul(
                unpack, x_spill[p]
            ).astype(BF16)

    def pack(p):
        total = None
        for side in range(split):
            move = flag(col_few == row_few // SPILL * MAIN + side * SPILL + row_few % SPILL)
            moved = matmul(
                move, y[p * unit + main : (p + 1) * unit, side * PIECE : (side + 1) * PIECE]
            )
            total = moved if total is None else total + moved
        y_spill[p] = total.astype(BF16)

    def returned(p, g):
        at = pl.ds(g * (width // back), width // back)
        if g == 0:
            all_landed(p, lambda s: (land_spill.at[p, spot(s)],), yrecv)
        all_landed(p, lambda s: (land.at[block(p, s), at],), yrecv, 1 + g)

    def parts_of(start, count):
        return [
            (at, min(2 * WIDE, start + count - at))
            for at in range(start, start + count, 2 * WIDE)
        ]

    def up(start, count):
        here = slice(start, start + count)
        for at in range(0, units, 2 * WIDE):
            tile = slice(at, min(at + 2 * WIDE, units))
            gate = matmul_nt(x[here, :], wg[tile, :])
            value = matmul_nt(x[here, :], wu[tile, :])
            hidden[0:count, tile] = (gate / (1.0 + jnp.exp(-gate)) * value).astype(BF16)

    def down(start, count):
        for at in range(0, width, WIDE):
            tile = slice(at, at + WIDE)
            y[start : start + count, tile] = matmul(hidden[0:count, :], wd[:, tile]).astype(BF16)

    def both(start, count):
        for at in parts_of(start * unit, count * unit):
            up(*at)
            down(*at)

    def give_back(p):
        def send(kind):
            def one(o, carry):
                homeward(p, lax.rem(e + o, size), kind)[0].start()
                return carry

            lax.fori_loop(1, size, one, 0)

        for kind in range(1 + back):
            send(kind)
        land[block(p, e), :] = y[block(p, e, unit), :]
        land_spill[p, spot(e)] = y_spill[p, spot(e)]

    for copy in inputs[:2]:
        copy.wait()
    pick_main(0, z)
    pick_spill(0, z)
    pl.semaphore_wait(
        barrier, size - 1 + jnp.where(z > 0, 1, 0) + jnp.where(z < depth - 1, 1, 0)
    )
    pass_on(z)
    start_all(outward, 0)
    keep(0)
    for copy in weights:
        copy.start()
    lax.fori_loop(1, depth - 1, stage, 0)
    for copy in weights:
        copy.wait()
    inputs[2].wait()
    near = depth // 2
    inside = jnp.logical_and(z > 0, z < depth - 1)

    @pl.when(inside)
    def _():
        stage(depth - 1, 0)

    for p in range(near):
        arrive(p)
    first = parts_of(0, near * unit)
    for at in first[:-1]:
        up(*at)
        down(*at)
    up(*first[-1])

    @pl.when(jnp.logical_not(inside))
    def _():
        stage(depth - 1, 0)

    down(*first[-1])
    for p in range(near):
        pack(p)
    for p in range(1, near):
        give_back(p)

    eye = flag(iota((rows, rows), 0) == iota((rows, rows), 1))
    mixed_slot = iota((rows, main), 1)
    mixed_code = ((mixed_slot // MAIN) // holders * CODE + mixed_slot % MAIN).astype(F32)
    mixed_side = mixed_slot % MAIN // SPILL
    mixed_spill = (
        (mixed_slot // MAIN) // holders * CODE + MAIN + mixed_slot % SPILL
    ).astype(F32)

    def weigh(k, carry):
        columns = matmul_nt(eye, codes[k][:, :rows].astype(BF16))
        first, second = columns[:, 0:1], columns[:, 1:2]
        logits = matmul_nt(held[k], router_ref[...])
        choice = (iota(logits.shape, 1) * CODE).astype(F32)

        def chosen(code):
            hit = jnp.logical_and(code >= choice, code < choice + CODE)
            return jnp.sum(jnp.where(hit, logits, 0.0), axis=1, keepdims=True)

        gate = 1.0 / (1.0 + jnp.exp(chosen(second) - chosen(first)))
        mix[k] = (
            jnp.where(first == mixed_code, gate, 0.0)
            + jnp.where(second == mixed_code, 1.0 - gate, 0.0)
        ).astype(BF16)
        mix_spill[k] = (
            jnp.where(first == mixed_spill, gate, 0.0)
            + jnp.where(second == mixed_spill, 1.0 - gate, 0.0)
        ).astype(BF16)
        return carry

    lax.fori_loop(0, depth, weigh, 0)

    for p in range(near, depth - 1):
        arrive(p)
    both(near, depth - 1 - near)
    for p in range(near, depth - 1):
        pack(p)
    arrive(depth - 1)
    both(depth - 1, 1)
    pack(depth - 1)
    for p in range(depth - 1, near - 1, -1):
        give_back(p)
    give_back(0)

    def relay(h, side, way):
        target = z + 1 if way == 0 else z - 1
        at = jnp.where(jnp.logical_and(way == 1, target == h), depth, h)
        return remote(
            part.at[h, side], passed.at[at, side], rsend.at[h, side], rrecv.at[at, side], "req",
            target,
        )

    def arrived(at, side):
        remote(
            passed.at[at, side], passed.at[at, side], rsend.at[0, 0], rrecv.at[at, side], "req",
            jnp.where(z > 0, z - 1, z + 1),
        ).wait_recv()

    def combine(h, side):
        p = place(h)
        here = pl.ds(pl.multiple_of(p * main, main), main)
        for c in range(piece // PIECE):
            number = side * (piece // PIECE) + c
            at = slice(number * PIECE, (number + 1) * PIECE)
            spill = mix_spill[h]
            sums[:, c * PIECE : (c + 1) * PIECE] = matmul(mix[h], land[here, at]) + matmul(
                jnp.where(mixed_side == number, spill, jnp.zeros_like(spill)), land_spill[p]
            )

    turns = turns_of(depth)

    def reduce(j, carry):
        h = jnp.int32(0)
        for at, turn in enumerate(turns):
            for i, home in enumerate(turn):
                h = jnp.where(jnp.logical_and(z == at, j == i), home, h)
        p = place(h)
        rising = h > z
        joined = jnp.logical_or(
            jnp.logical_and(rising, z > 0),
            jnp.logical_and(jnp.logical_not(rising), z < depth - 1),
        )
        for side in range(cuts):
            if side % (cuts // back) == 0:
                returned(p, side // (cuts // back))
            combine(h, side)

            @pl.when(joined)
            def _():
                arrived(h, side)
                sums[...] += passed[h, side].astype(F32)

            part[h, side] = sums[...].astype(BF16)

            @pl.when(rising)
            def _():
                relay(h, side, 0).start()

            @pl.when(jnp.logical_not(rising))
            def _():
                relay(h, side, 1).start()

        return carry

    lax.fori_loop(0, depth - 1, reduce, 0)
    for side in range(cuts):
        at = slice(side * piece, (side + 1) * piece)
        if side % (cuts // back) == 0:
            returned(0, side // (cuts // back))
        combine(z, side)
        sums[...] += stream[:, at].astype(F32)

        @pl.when(z > 0)
        def _():
            arrived(z, side)
            sums[...] += passed[z, side].astype(F32)

        @pl.when(z < depth - 1)
        def _():
            arrived(depth, side)
            sums[...] += passed[depth, side].astype(F32)

        out_ref[:, at] = sums[...].astype(BF16)

    def finish(k, carry):
        for way in range(2):
            @pl.when(passes(k, way))
            def _():
                for copy in along(k, way):
                    copy.wait_send()

        for side in range(cuts):
            @pl.when(k > z)
            def _():
                relay(k, side, 0).wait_send()

            @pl.when(k < z)
            def _():
                relay(k, side, 1).wait_send()

        def plane_done(o, carry):
            target = lax.rem(e + o, size)
            for copy in outward(k, target) + homeward(k, target):
                copy.wait_send()
            return carry

        lax.fori_loop(1, size, plane_done, 0)
        return carry

    lax.fori_loop(0, depth, finish, 0)


def expert_layer(normed, stream, code, router, w_gate, w_up, w_down, depth, size):
    rows, width = normed.shape
    units = w_gate.shape[0]
    cuts, back = cuts_of(width)
    piece = width // cuts
    main = size * MAIN
    unit = main + few_of(size)
    most = min(2 * WIDE, max(depth // 2, 1) * unit)
    dma = pltpu.SemaphoreType.DMA
    vmem = pl.BlockSpec(memory_space=pltpu.VMEM)
    hbm = pl.BlockSpec(memory_space=pltpu.HBM)
    return pl.pallas_call(
        functools.partial(expert_kernel, depth, size),
        out_shape=jax.ShapeDtypeStruct((rows, width), BF16),
        in_specs=[hbm] * 3 + [vmem] + [hbm] * 3,
        out_specs=vmem,
        scratch_shapes=[
            pltpu.VMEM((units, width), BF16),
            pltpu.VMEM((units, width), BF16),
            pltpu.VMEM((units, width), BF16),
            pltpu.VMEM((rows, width), BF16),
            pltpu.VMEM((depth, rows, width), BF16),
            pltpu.VMEM((depth, 8, LANES), F32),
            pltpu.VMEM((depth * main, width), BF16),
            pltpu.VMEM((depth, main, PIECE), BF16),
            pltpu.VMEM((depth * unit, width), BF16),
            pltpu.VMEM((depth, main, PIECE), BF16),
            pltpu.VMEM((most, units), BF16),
            pltpu.VMEM((depth * unit, width), BF16),
            pltpu.VMEM((depth, main, PIECE), BF16),
            pltpu.VMEM((depth * main, width), BF16),
            pltpu.VMEM((depth, main, PIECE), BF16),
            pltpu.VMEM((depth, rows, main), BF16),
            pltpu.VMEM((depth, rows, main), BF16),
            pltpu.VMEM((rows, piece), F32),
            pltpu.VMEM((depth, cuts, rows, piece), BF16),
            pltpu.VMEM((depth + 1, cuts, rows, piece), BF16),
            dma((6,)), dma((2, 2, depth)), dma((2, depth)),
            dma((2, depth, size)), dma((2, depth, size)),
            dma((1 + back, depth, size)), dma((1 + back, depth, size)),
            dma((depth, cuts)), dma((depth + 1, cuts)),
        ],
        compiler_params=pltpu.CompilerParams(
            collective_id=1, has_side_effects=True, vmem_limit_bytes=60 * 1024 * 1024
        ),
        name="experts",
    )(normed, stream, code, router, w_gate, w_up, w_down)


def on_device(
    queries,
    draft_keys,
    draft_values,
    tree_parents,
    cache_keys,
    cache_values,
    cache_lengths,
    prompt_keys,
    prompt_values,
    group_ids,
    residual,
    norm_gain,
    router,
    w_gate,
    w_up,
    w_down,
    expert_ids,
    accepted_rows,
):
    requests, tree, width = queries.shape
    rows = requests * tree
    depth, size = lax.axis_size("req"), lax.axis_size("exp")

    attended, stream, normed, kept, code = attention(
        tree_parents, jnp.swapaxes(expert_ids, 1, 2), accepted_rows, cache_lengths, group_ids,
        norm_gain, queries, draft_keys, draft_values,
        residual, cache_keys, cache_values, prompt_keys, prompt_values, size,
    )
    layer_out = expert_layer(
        normed, stream, code, router.T, w_gate[0].T, w_up[0].T, w_down[0], depth, size
    )
    return (
        attended.reshape(requests, tree, width),
        layer_out.reshape(requests, tree, width),
        kept.reshape(requests, 2, accepted_rows.shape[1], width),
    )


def solution(mesh):
    both = ("req", "exp")
    return jax.shard_map(
        on_device,
        mesh=mesh,
        in_specs=(
            P(both, None, None),
            P(both, None, None),
            P(both, None, None),
            P(both, None),
            P(both, None, None),
            P(both, None, None),
            P(both),
            P("req", "exp", None),
            P("req", "exp", None),
            P(both),
            P(both, None, None),
            P(),
            P(),
            P("exp", None, "req"),
            P("exp", None, "req"),
            P("exp", "req", None),
            P(both, None, None),
            P(both, None),
        ),
        out_specs=(
            P(both, None, None),
            P(both, None, None),
            P(both, None, None, None),
        ),
        check_vma=False,
    )
```

```python
import functools

import jax
import jax.numpy as jnp
from jax import lax
from jax.experimental import pallas as pl
from jax.experimental.pallas import tpu as pltpu
from jax.sharding import PartitionSpec as P

HEADS = 36
HDIM = 64
EXPERTS = 8
TOPK = 2
LANES = 128
PAIR = LANES // HDIM
WIDE = 256
MAIN = 16
SPILL = 2
PIECE = 384
CODE = 32
EPSILON = 1e-05
SCALE = HDIM ** (-0.5)
NT = (((1,), (1,)), ((), ()))
F32 = jnp.float32
BF16 = jnp.bfloat16
MESH = pl.DeviceIdType.MESH


def remote(src, dst, send, recv, axis, target):
    return pltpu.make_async_remote_copy(
        src_ref=src, dst_ref=dst, send_sem=send, recv_sem=recv, device_id={axis: target},
        device_id_type=MESH,
    )


def iota(shape, dim):
    return lax.broadcasted_iota(jnp.int32, shape, dim)


def flag(condition):
    return jnp.where(condition, 1.0, 0.0).astype(BF16)


def matmul(a, b):
    return jnp.dot(a, b, preferred_element_type=F32)


def matmul_nt(a, b):
    return lax.dot_general(a, b, NT, preferred_element_type=F32)


def greet_plane(size):
    e = lax.axis_index("exp")
    barrier = pltpu.get_barrier_semaphore()
    for step in range(1, size):
        pl.semaphore_signal(
            barrier, inc=1, device_id={"exp": lax.rem(e + step, size)}, device_id_type=MESH
        )


def share_of(size, blocks):
    each = blocks // size
    more = blocks - each * size
    return each, [i * (size - 1) // max(more - 1, 1) for i in range(more)]


def attention_kernel(
    size, each, extras,
    len_ref, group_ref, parent_ref, chosen_ref, pick_ref, gain_ref, q_hbm, dk_hbm, dv_hbm, res_hbm, ck_hbm, cv_hbm, pk_hbm, pv_hbm,
    att_ref, stream_ref, normed_ref, kept_ref, code_ref,
    ck, cv, q, dk, dv, res, group, acc, top_all, sum_all, kp, vp, qp, gp, staged, landed, landed_more,
    stats, csem, lsem, psend, precv, own, msend, mrecv, osend, orecv, oown, nsend, nrecv, nown,
):
    me = lax.axis_index("exp")
    rows, width = q.shape
    requests, cache = ck.shape[0], ck.shape[2]
    tree = rows // requests
    chunks = width // WIDE
    span = each * LANES
    groups, positions = pk_hbm.shape[0], pk_hbm.shape[1]
    wide_heads = WIDE // HDIM

    def cols(g):
        return pl.ds(pl.multiple_of(g * WIDE, WIDE), WIDE)

    def cache_copy(which, b, g):
        src, dst = ((ck_hbm, ck), (cv_hbm, cv))[which]
        return pltpu.make_async_copy(
            src.at[b, :, cols(g)], dst.at[b, g], csem.at[which, b, g]
        )

    small = [
        pltpu.make_async_copy(src, dst, lsem.at[i])
        for i, (src, dst) in enumerate(((q_hbm, q), (dk_hbm, dk), (dv_hbm, dv), (res_hbm, res)))
    ]
    for copy in small[:3]:
        copy.start()

    def load(g, carry):
        for b in range(requests):
            for which in range(2):
                cache_copy(which, b, g).start()
        return carry

    greet_plane(size)

    row8 = iota((8, LANES), 0)
    marks = jnp.zeros((8, LANES), jnp.int32)
    for b in range(requests):
        marks = jnp.where(row8 == b, group_ref[b], marks)
    group[...] = marks.astype(F32)

    pl.semaphore_wait(pltpu.get_barrier_semaphore(), size - 1)

    more = jnp.int32(0)
    holds_more = jnp.bool_(False)
    for i, device in enumerate(extras):
        more = jnp.where(me == device, i, more)
        holds_more = jnp.logical_or(holds_more, me == device)

    def from_source(s, lanes):
        keys = pl.ds(pl.multiple_of(s * positions, positions), positions)
        return (
            kp.at[:, keys, lanes],
            vp.at[:, keys, lanes],
            qp.at[pl.ds(pl.multiple_of(s * rows, rows), rows), lanes],
        )

    base_lanes, more_lanes = pl.ds(0, span), pl.ds(span, LANES)

    def base_copies(i):
        at = pl.ds(pl.multiple_of(i * span, LANES), span)
        return list(
            zip(
                (pk_hbm.at[:, :, at], pv_hbm.at[:, :, at], q_hbm.at[:, at], group),
                from_source(me, base_lanes) + (gp.at[me],),
            )
        )

    def more_copies(i):
        at = pl.ds((size * each + i) * LANES, LANES)
        return list(
            zip(
                (pk_hbm.at[:, :, at], pv_hbm.at[:, :, at], q_hbm.at[:, at]),
                from_source(me, more_lanes),
            )
        )

    def base_remote(kind, src, dst, i):
        return remote(src, dst, psend.at[kind, i], precv.at[kind, me], "exp", i)

    def more_remote(kind, src, dst, i):
        return remote(src, dst, msend.at[kind, i], mrecv.at[kind, me], "exp", extras[i])

    def send_heads(o, carry):
        i = lax.rem(o + me, size)
        for kind, (src, dst) in enumerate(base_copies(i)):
            base_remote(kind, src, dst, i).start()
        return carry

    lax.fori_loop(1, size, send_heads, 0)
    for i, device in enumerate(extras):
        @pl.when(me != device)
        def _():
            for kind, (src, dst) in enumerate(more_copies(i)):
                more_remote(kind, src, dst, i).start()

        @pl.when(me == device)
        def _():
            for kind, (src, dst) in enumerate(more_copies(i)):
                pltpu.make_async_copy(src, dst, own.at[4 + kind]).start()

    for kind, (src, dst) in enumerate(base_copies(me)):
        pltpu.make_async_copy(src, dst, own.at[kind]).start()
    lax.fori_loop(0, chunks, load, 0)
    small[3].start()

    def column(lines):
        length = lines[0].shape[1]
        same = iota((length, length), 0) == iota((length, length), 1)
        return jnp.concatenate(
            [jnp.sum(jnp.where(same, line, 0), axis=1, keepdims=True) for line in lines], axis=0
        )

    parent = column([parent_ref[b : b + 1] for b in range(requests)])
    at_row, at_col = iota((rows, rows), 0), iota((rows, rows), 1)
    base = at_row // tree * tree
    reached = jnp.logical_or(
        at_row == at_col, jnp.logical_and(at_col - base == parent, parent >= 0)
    )
    for _ in range(max(1, (tree - 1).bit_length())):
        step = flag(reached)
        reached = matmul(step, step) > 0.5
    related = jnp.where(reached, 1.0, 0.0)

    first, second = [
        column([chosen_ref[b, k : k + 1] for b in range(requests)]).astype(F32) for k in range(TOPK)
    ]
    lane = iota((rows, LANES), 1)
    expert = lane.astype(F32)
    named = flag(jnp.logical_or(expert == first, expert == second))
    before = matmul(flag(at_col < at_row), named)
    codes = [
        e * CODE + jnp.sum(jnp.where(expert == e, before, 0.0), axis=1, keepdims=True)
        for e in (first, second)
    ]
    code_columns = jnp.where(lane == 0, codes[0], jnp.where(lane == 1, codes[1], 0.0))
    code_ref[...] = jnp.zeros_like(code_ref)
    code_ref[:, :rows] = matmul_nt(
        flag(iota((8, LANES), 0) == iota((8, LANES), 1)), code_columns.astype(BF16)
    )

    for copy in small[:3]:
        copy.wait()
    path = pick_ref.shape[1]
    picked = column([pick_ref[b : b + 1] for b in range(requests)])
    owner = iota((requests * path, rows), 0) // path
    wanted = flag(iota((requests * path, rows), 1) == picked + owner * tree)
    for kind, ref in enumerate((dk, dv)):
        kept = matmul(wanted, ref[...]).astype(BF16)
        for b in range(requests):
            kept_ref[pl.ds((2 * b + kind) * path, path), :] = kept[b * path : (b + 1) * path]

    head_wide = iota((tree, WIDE), 1) // HDIM
    masks = [flag(head_wide == h) for h in range(wide_heads)]
    stat_lane = iota((tree, LANES), 1)
    seen = [
        jnp.concatenate([related[b * tree : (b + 1) * tree]] * wide_heads, axis=0)
        for b in range(requests)
    ]
    slot_at = iota((wide_heads * tree, cache), 1)
    top_all[...] = jnp.zeros_like(top_all)
    sum_all[...] = jnp.zeros_like(sum_all)

    def local(g, carry):
        for b in range(requests):
            here = slice(b * tree, (b + 1) * tree)
            for which in range(2):
                cache_copy(which, b, g).wait()
            query = q[here, cols(g)] * BF16(SCALE)
            stacked = jnp.concatenate([query * mask for mask in masks], axis=0)
            s_cache = matmul_nt(stacked, ck[b, g])
            s_cache = jnp.where(slot_at < len_ref[b], s_cache, -jnp.inf)
            s_tree = jnp.where(seen[b] > 0.5, matmul_nt(stacked, dk[:, cols(g)]), -jnp.inf)
            top = jnp.maximum(
                jnp.max(s_cache, axis=1, keepdims=True), jnp.max(s_tree, axis=1, keepdims=True)
            )
            w_cache = jnp.exp(s_cache - top)
            w_tree = jnp.exp(s_tree - top)
            total = jnp.sum(w_cache, axis=1, keepdims=True) + jnp.sum(
                w_tree, axis=1, keepdims=True
            )
            mixed = matmul(w_cache.astype(BF16), cv[b, g])
            mixed += matmul(w_tree.astype(BF16), dv[:, cols(g)])
            out = mixed[:tree]
            tops, sums = top_all[here], sum_all[here]
            for h in range(wide_heads):
                part = slice(h * tree, (h + 1) * tree)
                if h:
                    out = jnp.where(head_wide == h, mixed[part], out)
                at = g * wide_heads + h
                tops = jnp.where(stat_lane == at, top[part], tops)
                sums = jnp.where(stat_lane == at, total[part], sums)
            acc[here, cols(g)] = out
            top_all[here] = tops
            sum_all[here] = sums
        return carry

    lax.fori_loop(0, chunks, local, 0)

    for kind, (src, dst) in enumerate(base_copies(me)):
        pltpu.make_async_copy(src, dst, own.at[kind]).wait()

    def arrive(o, carry):
        source = lax.rem(me + o, size)
        for kind, ref in enumerate(from_source(source, base_lanes) + (gp.at[source],)):
            remote(
                ref, ref, psend.at[kind, 0], precv.at[kind, source], "exp", source
            ).wait_recv()
        return carry

    lax.fori_loop(1, size, arrive, 0)

    duo = 2 * rows
    pairs = size // 2
    half = iota((duo, LANES), 1) // HDIM
    sides = [flag(half == h) for h in range(PAIR)]
    stat_at = iota((duo, LANES), 1)

    def answer(target):
        at = pl.ds(pl.multiple_of(target * rows, rows), rows)
        return staged.at[at, pl.ds(0, span + LANES)]

    def answer_more(target):
        at = pl.ds(pl.multiple_of(target * rows, rows), rows)
        return staged.at[at, pl.ds(span + LANES, 2 * LANES)]

    def answer_remote(target):
        return remote(
            answer(target), landed.at[me], osend.at[target], orecv.at[me], "exp", target
        )

    def answer_more_remote(target):
        return remote(
            answer_more(target), landed_more.at[more], nsend.at[target], nrecv.at[more], "exp",
            target,
        )

    def visit(step):
        c = lax.rem(me // 2 + 1 + step, pairs)
        here = pl.ds(pl.multiple_of(c * duo, duo), duo)
        marks = []
        for s in range(2):
            mark = gp[2 * c + s]
            for b in range(requests):
                marks.append(jnp.broadcast_to(mark[b : b + 1, 0:1], (tree, 1)))
        mark = jnp.concatenate(marks * PAIR, axis=0)
        stats[...] = jnp.zeros_like(stats)

        def one(j, number, to):
            at = slice(j * LANES, (j + 1) * LANES)
            query = qp[here, at] * BF16(SCALE)
            stacked = jnp.concatenate([query * side for side in sides], axis=0)
            scores = matmul_nt(stacked, kp[0, :, at])
            for g in range(1, groups):
                scores = jnp.where(mark == g, matmul_nt(stacked, kp[g, :, at]), scores)
            top = jnp.max(scores, axis=1, keepdims=True).astype(BF16).astype(F32)
            weights = jnp.exp(scores - top)
            total = jnp.sum(weights, axis=1, keepdims=True)
            weights = weights.astype(BF16)
            mixed = None
            for g in range(groups):
                part = matmul(
                    jnp.where(mark == g, weights, jnp.zeros_like(weights)), vp[g, :, at]
                )
                mixed = part if mixed is None else mixed + part
            staged[here, to : to + LANES] = jnp.where(
                half == 0, mixed[:duo], mixed[duo:]
            ).astype(BF16)
            high = total.astype(BF16).astype(F32)
            got = stats[...]
            for h in range(PAIR):
                part = slice(h * duo, (h + 1) * duo)
                head = number * PAIR + h
                got = jnp.where(stat_at == head, top[part], got)
                got = jnp.where(stat_at == head + HEADS, high[part], got)
                got = jnp.where(stat_at == head + 2 * HEADS, (total - high)[part], got)
            stats[...] = got

        return c, here, one

    def attend(step, carry):
        c, here, one = visit(step)
        for j in range(each):
            one(j, me * each + j, j * LANES)
        staged[here, span : span + LANES] = stats[...].astype(BF16)
        for s in range(2):
            target = 2 * c + s

            @pl.when(target != me)
            def _():
                answer_remote(target).start()

            @pl.when(target == me)
            def _():
                pltpu.make_async_copy(answer(me), landed.at[me], oown.at[0]).start()

        return carry

    lax.fori_loop(0, pairs, attend, 0)

    @pl.when(holds_more)
    def _():
        for i, device in enumerate(extras):
            @pl.when(me == device)
            def _():
                for kind, (src, dst) in enumerate(more_copies(i)):
                    pltpu.make_async_copy(src, dst, own.at[4 + kind]).wait()

        def arrive_more(o, carry):
            source = lax.rem(me + o, size)
            for kind, ref in enumerate(from_source(source, more_lanes)):
                remote(
                    ref, ref, msend.at[kind, 0], mrecv.at[kind, source], "exp", source
                ).wait_recv()
            return carry

        lax.fori_loop(1, size, arrive_more, 0)

        def attend_more(step, carry):
            c, here, one = visit(step)
            one(each, size * each + more, span + LANES)
            staged[here, span + 2 * LANES :] = stats[...].astype(BF16)
            for s in range(2):
                target = 2 * c + s

                @pl.when(target != me)
                def _():
                    answer_more_remote(target).start()

                @pl.when(target == me)
                def _():
                    pltpu.make_async_copy(
                        answer_more(me), landed_more.at[more], nown.at[0]
                    ).start()

            return carry

        lax.fori_loop(0, pairs, attend_more, 0)
        pltpu.make_async_copy(answer_more(me), landed_more.at[more], nown.at[0]).wait()

    pltpu.make_async_copy(answer(me), landed.at[me], oown.at[0]).wait()

    small[3].wait()

    def answered(o, carry):
        source = lax.rem(me + o, size)
        remote(
            landed.at[source], landed.at[source], osend.at[0], orecv.at[source], "exp", source
        ).wait_recv()
        return carry

    lax.fori_loop(1, size, answered, 0)
    for i, device in enumerate(extras):
        @pl.when(me != device)
        def _():
            remote(
                landed_more.at[i], landed_more.at[i], nsend.at[0], nrecv.at[i], "exp", device
            ).wait_recv()

    tops = landed[0, :, span:].astype(F32)
    for i in range(1, size):
        tops += landed[i, :, span:].astype(F32)
    for i in range(len(extras)):
        tops += landed_more[i, :, LANES:].astype(F32)
    theirs = pltpu.roll(tops, LANES - HEADS, 1) + pltpu.roll(tops, LANES - 2 * HEADS, 1)
    used = lane < HEADS
    ours = jnp.where(used, sum_all[...], 1.0)
    theirs = jnp.where(used, theirs, 1.0)
    tops = jnp.where(used, tops, 0.0)
    top = jnp.maximum(top_all[...], tops)
    own_scale = jnp.exp(top_all[...] - top)
    far_scale = jnp.exp(tops - top)
    total = own_scale * ours + far_scale * theirs
    own_scale, far_scale = own_scale / total, far_scale / total
    squares = jnp.zeros((rows, 1), F32)
    left = lane < HDIM
    for block in range(width // LANES):
        at = slice(block * LANES, (block + 1) * LANES)
        i, j = divmod(block, each)
        a = PAIR * block
        if i < size:
            far = landed[i, :, j * LANES : (j + 1) * LANES]
        else:
            far = landed_more[block - size * each, :, :LANES]
        out = acc[:, at] * jnp.where(left, own_scale[:, a : a + 1], own_scale[:, a + 1 : a + 2])
        out += far.astype(F32) * jnp.where(
            left, far_scale[:, a : a + 1], far_scale[:, a + 1 : a + 2]
        )
        attended = out.astype(BF16)
        att_ref[:, at] = attended
        stream = (res[:, at].astype(F32) + attended.astype(F32)).astype(BF16)
        stream_ref[:, at] = stream
        stream = stream.astype(F32)
        squares += jnp.sum(stream * stream, axis=1, keepdims=True)
    factor = lax.rsqrt(squares / width + EPSILON)
    normed_ref[...] = (stream_ref[...].astype(F32) * factor * gain_ref[...].reshape(1, width)).astype(BF16)

    def sent(o, carry):
        i = lax.rem(me + o, size)
        for kind, (src, dst) in enumerate(base_copies(i)):
            base_remote(kind, src, dst, i).wait_send()
        answer_remote(i).wait_send()

        @pl.when(holds_more)
        def _():
            answer_more_remote(i).wait_send()

        return carry

    lax.fori_loop(1, size, sent, 0)
    for i, device in enumerate(extras):
        @pl.when(me != device)
        def _():
            for kind, (src, dst) in enumerate(more_copies(i)):
                more_remote(kind, src, dst, i).wait_send()


def attention(
    parents, chosen, picks, lengths, group_ids, gain, queries, draft_keys, draft_values, residual, cache_keys, cache_values,
    prompt_keys, prompt_values, size,
):
    requests, tree, width = queries.shape
    rows, cache = requests * tree, cache_keys.shape[1]
    groups, positions = prompt_keys.shape[:2]
    each, extras = share_of(size, width // LANES)
    count, span, chunks = len(extras), each * LANES, width // WIDE
    path = picks.shape[1]
    flat = lambda a: a.reshape(rows, width)
    vmem = pl.BlockSpec(memory_space=pltpu.VMEM)
    hbm = pl.BlockSpec(memory_space=pltpu.HBM)
    dma = pltpu.SemaphoreType.DMA
    row_block = jax.ShapeDtypeStruct((rows, width), BF16)
    return pl.pallas_call(
        functools.partial(attention_kernel, size, each, extras),
        out_shape=[
            row_block, row_block, row_block,
            jax.ShapeDtypeStruct((requests * 2 * path, width), BF16),
            jax.ShapeDtypeStruct((8, LANES), F32),
        ],
        in_specs=[pl.BlockSpec(memory_space=pltpu.SMEM)] * 2 + [vmem] * 4 + [hbm] * 8,
        out_specs=[vmem] * 5,
        scratch_shapes=[
            pltpu.VMEM((requests, chunks, cache, WIDE), BF16),
            pltpu.VMEM((requests, chunks, cache, WIDE), BF16),
            pltpu.VMEM((rows, width), BF16),
            pltpu.VMEM((rows, width), BF16),
            pltpu.VMEM((rows, width), BF16),
            pltpu.VMEM((rows, width), BF16),
            pltpu.VMEM((8, LANES), F32),
            pltpu.VMEM((rows, width), F32),
            pltpu.VMEM((rows, LANES), F32),
            pltpu.VMEM((rows, LANES), F32),
            pltpu.VMEM((groups, size * positions, span + LANES), BF16),
            pltpu.VMEM((groups, size * positions, span + LANES), BF16),
            pltpu.VMEM((size * rows, span + LANES), BF16),
            pltpu.VMEM((size, 8, LANES), F32),
            pltpu.VMEM((size * rows, span + 3 * LANES), BF16),
            pltpu.VMEM((size, rows, span + LANES), BF16),
            pltpu.VMEM((count, rows, 2 * LANES), BF16),
            pltpu.VMEM((2 * rows, LANES), F32),
            dma((2, requests, chunks)), dma((4,)), dma((4, size)), dma((4, size)), dma((7,)),
            dma((3, count)), dma((3, size)), dma((size,)), dma((size,)), dma((1,)),
            dma((size,)), dma((count,)), dma((1,)),
        ],
        compiler_params=pltpu.CompilerParams(
            collective_id=0, has_side_effects=True, vmem_limit_bytes=60 * 1024 * 1024
        ),
        name="attention",
    )(
        lengths, group_ids, parents, chosen, picks, gain, flat(queries), flat(draft_keys), flat(draft_values), flat(residual),
        cache_keys, cache_values, prompt_keys, prompt_values,
    )


def cuts_of(width):
    pieces = width // PIECE
    back = 2 if pieces % 2 == 0 else pieces
    return pieces, back


def few_of(size):
    return -(-size * SPILL // MAIN) * MAIN


def turns_of(depth):
    if depth == 4:
        return [[1, 3, 2], [3, 0, 2], [0, 3, 1], [2, 0, 1]]
    turns = []
    for z in range(depth):
        ends = [(i, depth - 1 - i) for i in range(depth // 2)]
        pairs = [pair[::-1] if z < depth // 2 else pair for pair in ends]
        turns.append([h for pair in pairs for h in pair if h != z])
    return turns


def expert_kernel(
    depth, size,
    normed_hbm, stream_hbm, code_hbm, router_ref, wg_hbm, wu_hbm, wd_hbm,
    out_ref,
    wg, wu, wd, stream, held, codes, staged, spilled, x, x_spill, hidden, y, y_spill, land, land_spill,
    mix, mix_spill, sums, part, passed,
    wsem, zsend, zrecv, dsend, drecv, ysend, yrecv, rsend, rrecv,
):
    z, e = lax.axis_index("req"), lax.axis_index("exp")
    rows, width = normed_hbm.shape
    units = wg.shape[0]
    holders = size // EXPERTS
    split = width // PIECE
    cuts, back = cuts_of(width)
    piece = width // cuts
    main = size * MAIN
    few = few_of(size)
    unit = main + few
    low = z < depth // 2

    weights = [
        pltpu.make_async_copy(src, dst, wsem.at[i])
        for i, (src, dst) in enumerate(((wg_hbm, wg), (wu_hbm, wu), (wd_hbm, wd)))
    ]
    inputs = [
        pltpu.make_async_copy(src, dst, wsem.at[3 + i])
        for i, (src, dst) in enumerate(
            ((normed_hbm, held.at[z]), (code_hbm, codes.at[z]), (stream_hbm, stream))
        )
    ]
    for copy in inputs:
        copy.start()

    barrier = pltpu.get_barrier_semaphore()
    greet_plane(size)

    @pl.when(z < depth - 1)
    def _():
        pl.semaphore_signal(barrier, inc=1, device_id={"req": z + 1}, device_id_type=MESH)

    @pl.when(z > 0)
    def _():
        pl.semaphore_signal(barrier, inc=1, device_id={"req": z - 1}, device_id_type=MESH)

    def order(p):
        near = jnp.where(low, z, depth - 1 - z)
        step = (p + 1) // 2
        at = jnp.where(p > 2 * near, p, jnp.where(p % 2 == 1, near - step, near + step))
        return jnp.where(low, at, depth - 1 - at)

    def place(k):
        near = jnp.where(low, z, depth - 1 - z)
        at = jnp.where(low, k, depth - 1 - k)
        gap = at - near
        return jnp.where(
            gap == 0, 0, jnp.where(gap < 0, -2 * gap - 1, jnp.where(gap <= near, 2 * gap, at))
        )

    def along(k, way):
        target = z + 1 if way == 0 else z - 1
        return [
            remote(ref.at[k], ref.at[k], zsend.at[kind, way, k], zrecv.at[kind, k], "req", target)
            for kind, ref in enumerate((codes, held))
        ]

    def passes(k, way):
        if way == 0:
            return jnp.logical_and(k <= z, z < depth - 1)
        return jnp.logical_and(k >= z, z > 0)

    def pass_on(k):
        for way in range(2):
            @pl.when(passes(k, way))
            def _():
                for copy in along(k, way):
                    copy.start()

    def block(p, target, height=main):
        return pl.ds(pl.multiple_of(p * height + target * MAIN, MAIN), MAIN)

    def spot(target):
        return pl.ds(pl.multiple_of(target * MAIN, MAIN), MAIN)

    def outward(p, target, kinds=(0, 1)):
        return [
            remote(
                src, dst, dsend.at[kind, p, target], drecv.at[kind, p, e], "exp", target
            )
            for kind, (src, dst) in enumerate(
                (
                    (staged.at[block(p, target)], x.at[block(p, e, unit)]),
                    (spilled.at[p, spot(target)], x_spill.at[p, spot(e)]),
                )
            )
            if kind in kinds
        ]

    def homeward(p, target, only=None):
        groups = [
            (
                y.at[block(p, target, unit), pl.ds(g * (width // back), width // back)],
                land.at[block(p, e), pl.ds(g * (width // back), width // back)],
            )
            for g in range(back)
        ]
        return [
            remote(
                src, dst, ysend.at[kind, p, target], yrecv.at[kind, p, e], "exp", target
            )
            for kind, (src, dst) in enumerate(
                [(y_spill.at[p, spot(target)], land_spill.at[p, spot(e)])] + groups
            )
            if only is None or kind == only
        ]

    def start_all(copies, p, **kinds):
        def send(o, carry):
            for copy in copies(p, lax.rem(e + o, size), **kinds):
                copy.start()
            return carry

        lax.fori_loop(1, size, send, 0)

    slot = iota((main, rows), 0)
    slot_side, slot_item = slot % MAIN // SPILL, slot % SPILL
    spill_code = ((slot // MAIN) // holders * CODE + MAIN + slot_item).astype(F32)
    wanted = iota((main, rows), 0)
    wanted_code = ((wanted // MAIN) // holders * CODE + wanted % MAIN).astype(F32)

    def pick_main(p, k):
        code = codes[k]
        pick = flag(
            jnp.logical_or(code[0:1, :rows] == wanted_code, code[1:2, :rows] == wanted_code)
        )
        here = pl.ds(pl.multiple_of(p * main, main), main)
        step = 3 * WIDE if width % (3 * WIDE) == 0 else WIDE
        for c in range(0, width, step):
            staged[here, c : c + step] = matmul(pick, held[k, :, c : c + step]).astype(BF16)

    def pick_spill(p, k):
        code = codes[k]
        match = jnp.logical_or(code[0:1, :rows] == spill_code, code[1:2, :rows] == spill_code)
        total = None
        for side in range(split):
            picked = matmul(
                flag(jnp.logical_and(match, slot_side == side)),
                held[k, :, side * PIECE : (side + 1) * PIECE],
            )
            total = picked if total is None else total + picked
        spilled[p] = total.astype(BF16)

    def keep(p):
        x[block(p, e, unit), :] = staged[block(p, e), :]
        x_spill[p, spot(e)] = spilled[p, spot(e)]

    def stage(p, carry):
        k = order(p)
        for copy in along(k, 0):
            copy.wait_recv()
        pass_on(k)
        pick_main(p, k)
        start_all(outward, p, kinds=(0,))
        pick_spill(p, k)
        start_all(outward, p, kinds=(1,))
        keep(p)
        return carry

    def all_landed(p, refs, sem, first=0):
        def wait(o, carry):
            source = lax.rem(e + o, size)
            for kind, ref in enumerate(refs(source), first):
                remote(
                    ref, ref, dsend.at[0, 0, 0], sem.at[kind, p, source], "exp", source
                ).wait_recv()
            return carry

        lax.fori_loop(1, size, wait, 0)

    few_row, few_col = iota((few, main), 0), iota((few, main), 1)
    row_few, col_few = iota((main, few), 1), iota((main, few), 0)

    def arrive(p):
        all_landed(p, lambda s: (x.at[block(p, s, unit)], x_spill.at[p, spot(s)]), drecv)
        for side in range(split):
            unpack = flag(
                few_col == few_row // SPILL * MAIN + side * SPILL + few_row % SPILL
            )
            x[p * unit + main : (p + 1) * unit, side * PIECE : (side + 1) * PIECE] = matmul(
                unpack, x_spill[p]
            ).astype(BF16)

    def pack(p):
        total = None
        for side in range(split):
            move = flag(col_few == row_few // SPILL * MAIN + side * SPILL + row_few % SPILL)
            moved = matmul(
                move, y[p * unit + main : (p + 1) * unit, side * PIECE : (side + 1) * PIECE]
            )
            total = moved if total is None else total + moved
        y_spill[p] = total.astype(BF16)

    def returned(p, g):
        at = pl.ds(g * (width // back), width // back)
        if g == 0:
            all_landed(p, lambda s: (land_spill.at[p, spot(s)],), yrecv)
        all_landed(p, lambda s: (land.at[block(p, s), at],), yrecv, 1 + g)

    def parts_of(start, count):
        return [
            (at, min(2 * WIDE, start + count - at))
            for at in range(start, start + count, 2 * WIDE)
        ]

    def up(start, count):
        here = slice(start, start + count)
        for at in range(0, units, 2 * WIDE):
            tile = slice(at, min(at + 2 * WIDE, units))
            gate = matmul_nt(x[here, :], wg[tile, :])
            value = matmul_nt(x[here, :], wu[tile, :])
            hidden[0:count, tile] = (gate / (1.0 + jnp.exp(-gate)) * value).astype(BF16)

    def down(start, count):
        for at in range(0, width, WIDE):
            tile = slice(at, at + WIDE)
            y[start : start + count, tile] = matmul(hidden[0:count, :], wd[:, tile]).astype(BF16)

    def both(start, count):
        for at in parts_of(start * unit, count * unit):
            up(*at)
            down(*at)

    def give_back(p):
        def send(kind):
            def one(o, carry):
                homeward(p, lax.rem(e + o, size), kind)[0].start()
                return carry

            lax.fori_loop(1, size, one, 0)

        for kind in range(1 + back):
            send(kind)
        land[block(p, e), :] = y[block(p, e, unit), :]
        land_spill[p, spot(e)] = y_spill[p, spot(e)]

    for copy in inputs[:2]:
        copy.wait()
    pick_main(0, z)
    pick_spill(0, z)
    pl.semaphore_wait(
        barrier, size - 1 + jnp.where(z > 0, 1, 0) + jnp.where(z < depth - 1, 1, 0)
    )
    pass_on(z)
    start_all(outward, 0)
    keep(0)
    for copy in weights:
        copy.start()
    lax.fori_loop(1, depth - 1, stage, 0)
    for copy in weights:
        copy.wait()
    inputs[2].wait()
    near = depth // 2
    inside = jnp.logical_and(z > 0, z < depth - 1)

    @pl.when(inside)
    def _():
        stage(depth - 1, 0)

    for p in range(near):
        arrive(p)
    first = parts_of(0, near * unit)
    for at in first[:-1]:
        up(*at)
        down(*at)
    up(*first[-1])

    @pl.when(jnp.logical_not(inside))
    def _():
        stage(depth - 1, 0)

    down(*first[-1])
    for p in range(near):
        pack(p)
    for p in range(1, near):
        give_back(p)

    eye = flag(iota((rows, rows), 0) == iota((rows, rows), 1))
    mixed_slot = iota((rows, main), 1)
    mixed_code = ((mixed_slot // MAIN) // holders * CODE + mixed_slot % MAIN).astype(F32)
    mixed_side = mixed_slot % MAIN // SPILL
    mixed_spill = (
        (mixed_slot // MAIN) // holders * CODE + MAIN + mixed_slot % SPILL
    ).astype(F32)

    def weigh(k, carry):
        columns = matmul_nt(eye, codes[k][:, :rows].astype(BF16))
        first, second = columns[:, 0:1], columns[:, 1:2]
        logits = matmul_nt(held[k], router_ref[...])
        choice = (iota(logits.shape, 1) * CODE).astype(F32)

        def chosen(code):
            hit = jnp.logical_and(code >= choice, code < choice + CODE)
            return jnp.sum(jnp.where(hit, logits, 0.0), axis=1, keepdims=True)

        gate = 1.0 / (1.0 + jnp.exp(chosen(second) - chosen(first)))
        mix[k] = (
            jnp.where(first == mixed_code, gate, 0.0)
            + jnp.where(second == mixed_code, 1.0 - gate, 0.0)
        ).astype(BF16)
        mix_spill[k] = (
            jnp.where(first == mixed_spill, gate, 0.0)
            + jnp.where(second == mixed_spill, 1.0 - gate, 0.0)
        ).astype(BF16)
        return carry

    lax.fori_loop(0, depth, weigh, 0)

    for p in range(near, depth - 1):
        arrive(p)
    both(near, depth - 1 - near)
    for p in range(near, depth - 1):
        pack(p)
    arrive(depth - 1)
    both(depth - 1, 1)
    pack(depth - 1)
    for p in range(depth - 1, near - 1, -1):
        give_back(p)
    give_back(0)

    def relay(h, side, way):
        target = z + 1 if way == 0 else z - 1
        at = jnp.where(jnp.logical_and(way == 1, target == h), depth, h)
        return remote(
            part.at[h, side], passed.at[at, side], rsend.at[h, side], rrecv.at[at, side], "req",
            target,
        )

    def arrived(at, side):
        remote(
            passed.at[at, side], passed.at[at, side], rsend.at[0, 0], rrecv.at[at, side], "req",
            jnp.where(z > 0, z - 1, z + 1),
        ).wait_recv()

    def combine(h, side):
        p = place(h)
        here = pl.ds(pl.multiple_of(p * main, main), main)
        for c in range(piece // PIECE):
            number = side * (piece // PIECE) + c
            at = slice(number * PIECE, (number + 1) * PIECE)
            spill = mix_spill[h]
            sums[:, c * PIECE : (c + 1) * PIECE] = matmul(mix[h], land[here, at]) + matmul(
                jnp.where(mixed_side == number, spill, jnp.zeros_like(spill)), land_spill[p]
            )

    turns = turns_of(depth)

    def reduce(j, carry):
        h = jnp.int32(0)
        for at, turn in enumerate(turns):
            for i, home in enumerate(turn):
                h = jnp.where(jnp.logical_and(z == at, j == i), home, h)
        p = place(h)
        rising = h > z
        joined = jnp.logical_or(
            jnp.logical_and(rising, z > 0),
            jnp.logical_and(jnp.logical_not(rising), z < depth - 1),
        )
        for side in range(cuts):
            if side % (cuts // back) == 0:
                returned(p, side // (cuts // back))
            combine(h, side)

            @pl.when(joined)
            def _():
                arrived(h, side)
                sums[...] += passed[h, side].astype(F32)

            part[h, side] = sums[...].astype(BF16)

            @pl.when(rising)
            def _():
                relay(h, side, 0).start()

            @pl.when(jnp.logical_not(rising))
            def _():
                relay(h, side, 1).start()

        return carry

    lax.fori_loop(0, depth - 1, reduce, 0)
    for side in range(cuts):
        at = slice(side * piece, (side + 1) * piece)
        if side % (cuts // back) == 0:
            returned(0, side // (cuts // back))
        combine(z, side)
        sums[...] += stream[:, at].astype(F32)

        @pl.when(z > 0)
        def _():
            arrived(z, side)
            sums[...] += passed[z, side].astype(F32)

        @pl.when(z < depth - 1)
        def _():
            arrived(depth, side)
            sums[...] += passed[depth, side].astype(F32)

        out_ref[:, at] = sums[...].astype(BF16)

    def finish(k, carry):
        for way in range(2):
            @pl.when(passes(k, way))
            def _():
                for copy in along(k, way):
                    copy.wait_send()

        for side in range(cuts):
            @pl.when(k > z)
            def _():
                relay(k, side, 0).wait_send()

            @pl.when(k < z)
            def _():
                relay(k, side, 1).wait_send()

        def plane_done(o, carry):
            target = lax.rem(e + o, size)
            for copy in outward(k, target) + homeward(k, target):
                copy.wait_send()
            return carry

        lax.fori_loop(1, size, plane_done, 0)
        return carry

    lax.fori_loop(0, depth, finish, 0)


def expert_layer(normed, stream, code, router, w_gate, w_up, w_down, depth, size):
    rows, width = normed.shape
    units = w_gate.shape[0]
    cuts, back = cuts_of(width)
    piece = width // cuts
    main = size * MAIN
    unit = main + few_of(size)
    most = min(2 * WIDE, max(depth // 2, 1) * unit)
    dma = pltpu.SemaphoreType.DMA
    vmem = pl.BlockSpec(memory_space=pltpu.VMEM)
    hbm = pl.BlockSpec(memory_space=pltpu.HBM)
    return pl.pallas_call(
        functools.partial(expert_kernel, depth, size),
        out_shape=jax.ShapeDtypeStruct((rows, width), BF16),
        in_specs=[hbm] * 3 + [vmem] + [hbm] * 3,
        out_specs=vmem,
        scratch_shapes=[
            pltpu.VMEM((units, width), BF16),
            pltpu.VMEM((units, width), BF16),
            pltpu.VMEM((units, width), BF16),
            pltpu.VMEM((rows, width), BF16),
            pltpu.VMEM((depth, rows, width), BF16),
            pltpu.VMEM((depth, 8, LANES), F32),
            pltpu.VMEM((depth * main, width), BF16),
            pltpu.VMEM((depth, main, PIECE), BF16),
            pltpu.VMEM((depth * unit, width), BF16),
            pltpu.VMEM((depth, main, PIECE), BF16),
            pltpu.VMEM((most, units), BF16),
            pltpu.VMEM((depth * unit, width), BF16),
            pltpu.VMEM((depth, main, PIECE), BF16),
            pltpu.VMEM((depth * main, width), BF16),
            pltpu.VMEM((depth, main, PIECE), BF16),
            pltpu.VMEM((depth, rows, main), BF16),
            pltpu.VMEM((depth, rows, main), BF16),
            pltpu.VMEM((rows, piece), F32),
            pltpu.VMEM((depth, cuts, rows, piece), BF16),
            pltpu.VMEM((depth + 1, cuts, rows, piece), BF16),
            dma((6,)), dma((2, 2, depth)), dma((2, depth)),
            dma((2, depth, size)), dma((2, depth, size)),
            dma((1 + back, depth, size)), dma((1 + back, depth, size)),
            dma((depth, cuts)), dma((depth + 1, cuts)),
        ],
        compiler_params=pltpu.CompilerParams(
            collective_id=1, has_side_effects=True, vmem_limit_bytes=60 * 1024 * 1024
        ),
        name="experts",
    )(normed, stream, code, router, w_gate, w_up, w_down)


def on_device(
    queries,
    draft_keys,
    draft_values,
    tree_parents,
    cache_keys,
    cache_values,
    cache_lengths,
    prompt_keys,
    prompt_values,
    group_ids,
    residual,
    norm_gain,
    router,
    w_gate,
    w_up,
    w_down,
    expert_ids,
    accepted_rows,
):
    requests, tree, width = queries.shape
    rows = requests * tree
    depth, size = lax.axis_size("req"), lax.axis_size("exp")

    attended, stream, normed, kept, code = attention(
        tree_parents, jnp.swapaxes(expert_ids, 1, 2), accepted_rows, cache_lengths, group_ids,
        norm_gain, queries, draft_keys, draft_values,
        residual, cache_keys, cache_values, prompt_keys, prompt_values, size,
    )
    layer_out = expert_layer(
        normed, stream, code, router.T, w_gate[0].T, w_up[0].T, w_down[0], depth, size
    )
    return (
        attended.reshape(requests, tree, width),
        layer_out.reshape(requests, tree, width),
        kept.reshape(requests, 2, accepted_rows.shape[1], width),
    )


def solution(mesh):
    both = ("req", "exp")
    return jax.shard_map(
        on_device,
        mesh=mesh,
        in_specs=(
            P(both, None, None),
            P(both, None, None),
            P(both, None, None),
            P(both, None),
            P(both, None, None),
            P(both, None, None),
            P(both),
            P("req", "exp", None),
            P("req", "exp", None),
            P(both),
            P(both, None, None),
            P(),
            P(),
            P("exp", None, "req"),
            P("exp", None, "req"),
            P("exp", "req", None),
            P(both, None, None),
            P(both, None),
        ),
        out_specs=(
            P(both, None, None),
            P(both, None, None),
            P(both, None, None, None),
        ),
        check_vma=False,
    )
```
